32 devices in a mesh: band: 4 (over x, core), row: 8 (over z, y).
Axes of the slice: x: 2, y: 2, z: 4, core: 2. Of those that a mesh axis runs over, the one named last changes fastest.
Arguments:
- shape_coupling_matrices: bfloat16 [512, 4, 128, 128], P('row'), may hold values from 0 to 0.00390625
- target_strip_index: int32 [512, 4], P('row'), may hold values from 0 to 511, as said below
- occupied_entries_per_strip: int32 [512], P('row'), may hold values from 1 to 4
- prior_leaving_energy: bfloat16 [4, 65536], P('band', 'row'), may hold values from 0.19921875 to 3
- facet_kelvins: float32 [65536], P('row'), may hold values from 0.6 to 1.6
- emitting_ability: float32 [4, 65536], P('band', 'row'), may hold values from 0.2 to 0.9
- centre_frequency: float32 [4], P('band'), may hold values from 0.28 to 6.3
- frequency_span: float32 [4], P('band'), may hold values from 0.5 to 1.5
- prescribed_power_density: float32 [65536], P('row'), may hold values from -6 to 6
Outputs:
- corrected_kelvins: float32 [65536], P('row')
- refreshed_leaving_energy: float32 [4, 65536], P('band', 'row')
The draws below stay inside these ranges and needn't reach their ends.
Inputs may be any that keep to these rules, and one draw needn't show every extreme that they name: `target_strip_index`: of the 256 entries of one device's rows, exactly 32 name a column tile held by each index of row.
All inputs are finite; a program needn't handle non-finite values.
Results may differ from the reference program's by a relative error of at most 0.0003.
Values may be sent and summed in bfloat16 or wider, within the bound.
No kernel may reach another device: no remote copies, remote signals or barrier semaphores. Data moves between devices by JAX's collectives and lax.ppermute only.
A program may use at most 64 MiB of HBM per device.

```python
import jax
import jax.numpy as jnp
from jax import lax

TILE = 128
SLOTS = 4
TILES_DEV = 64
FACET_TOTAL = 65536
ROW_TILES = 512
BANDS = 4
N_ROW = 8


def draw_target_strip_index(key, part):
    entries = TILES_DEV * SLOTS
    first_key, second_key = jax.random.split(jax.random.fold_in(key, 11))
    slab_keys = jax.random.split(first_key, N_ROW)
    shuffled = jax.vmap(lambda single: jax.random.permutation(single, entries))(slab_keys)
    owners = shuffled % N_ROW
    local_tiles = jax.random.randint(second_key, (N_ROW, entries), 0, TILES_DEV)
    columns = owners * TILES_DEV + local_tiles
    return columns.reshape(ROW_TILES, SLOTS).astype(jnp.int32)


def draw_centre_frequency(key, part):
    position = jnp.arange(BANDS).astype(jnp.float32) / max(BANDS - 1, 1)
    base = 0.4 * 12.0 ** position
    jitter = jax.random.uniform(jax.random.fold_in(key, 5), (BANDS,), jnp.float32, 0.85, 1.15)
    return (base * jitter).astype(jnp.float32)


def set_ends(values, key, least, top_value):
    dims = values.shape
    place = [jax.random.randint(jax.random.fold_in(key, axis), (), 0, dims[axis]) for axis in range(len(dims))]
    values = values.at[tuple(place)].set(least)
    longest = dims.index(max(dims))
    place[longest] = (place[longest] + 1) % dims[longest]
    return values.at[tuple(place)].set(top_value)


def level_of(stream_key, dims, cuts, smallest, high):
    loudness, own = 1.0, jax.random.fold_in(stream_key, 6)
    for dim, shards_of in cuts:
        steps = jnp.exp(jax.random.uniform(jax.random.fold_in(own, dim), (shards_of,), jnp.float32, smallest / len(cuts), high / len(cuts)))
        loudness = loudness * jnp.repeat(steps, dims[dim] // shards_of).reshape([-1 if axis == dim else 1 for axis in range(len(dims))])
    return loudness


def noise(rng, extent, scale, reach, pieces=(), held_as=jnp.bfloat16):
    values = scale * jax.random.normal(rng, extent, jnp.float32)
    if pieces:
        values = values * level_of(rng, extent, pieces, -0.22, 0.18)
    return jnp.clip(values, -reach, reach).astype(held_as)


def setup_inputs(seed: int = 0) -> dict:
    seeds = jax.random.split(jax.random.key(seed), 10)
    shape_coupling_matrices = jnp.clip(0.00390625 * jax.random.uniform(seeds[0], (ROW_TILES, SLOTS, TILE, TILE), jnp.float32) ** level_of(seeds[0], (ROW_TILES, SLOTS, TILE, TILE), ((0, 8),), -0.2, 0.2), 0.0, 0.00390625).astype(jnp.bfloat16)
    target_strip_index = draw_target_strip_index(jax.random.fold_in(seeds[9], 71), 0)
    occupied_entries_per_strip = set_ends(jax.random.randint(seeds[2], (ROW_TILES,), 1, SLOTS + 1), jax.random.fold_in(seeds[2], 1), 1, SLOTS).astype(jnp.int32)
    prior_leaving_energy = jnp.clip(0.19921875 + 2.8007812 * jax.random.uniform(seeds[3], (BANDS, FACET_TOTAL), jnp.float32) ** level_of(seeds[3], (BANDS, FACET_TOTAL), ((0, 4), (1, 8)), -0.2, 0.2), 0.19921875, 3.0).astype(jnp.bfloat16)
    facet_kelvins = jnp.clip(0.6 + 1.0 * jax.random.uniform(seeds[4], (FACET_TOTAL,), jnp.float32) ** level_of(seeds[4], (FACET_TOTAL,), ((0, 8),), -0.2, 0.2), 0.6, 1.6)
    emitting_ability = jnp.clip(0.2 + 0.7 * jax.random.uniform(seeds[5], (BANDS, FACET_TOTAL), jnp.float32) ** level_of(seeds[5], (BANDS, FACET_TOTAL), ((0, 4), (1, 8)), -0.2, 0.2), 0.2, 0.9)
    centre_frequency = draw_centre_frequency(jax.random.fold_in(seeds[9], 71), 0)
    frequency_span = jnp.clip(0.5 + 1.0 * jax.random.uniform(seeds[7], (BANDS,), jnp.float32) ** level_of(seeds[7], (BANDS,), ((0, 4),), -0.2, 0.2), 0.5, 1.5)
    prescribed_power_density = noise(seeds[8], (FACET_TOTAL,), 1.0, 6.0, ((0, 8),), jnp.float32)
    return dict(shape_coupling_matrices=shape_coupling_matrices, target_strip_index=target_strip_index, occupied_entries_per_strip=occupied_entries_per_strip, prior_leaving_energy=prior_leaving_energy, facet_kelvins=facet_kelvins, emitting_ability=emitting_ability, centre_frequency=centre_frequency, frequency_span=frequency_span, prescribed_power_density=prescribed_power_density)


def emitter_terms(centre_sample, frequency_spacing, facet_kelvins):
    return frequency_spacing[:, None] * centre_sample[:, None] ** 3 / jnp.expm1(centre_sample[:, None] / facet_kelvins[None, :])


def reference(shape_coupling_matrices, target_strip_index, occupied_entries_per_strip, prior_leaving_energy, facet_kelvins, emitting_ability, centre_frequency, frequency_span, prescribed_power_density):
    tiled = prior_leaving_energy.reshape(BANDS, ROW_TILES, TILE)[:, target_strip_index]
    slot_mask = (lax.broadcasted_iota(jnp.int32, (ROW_TILES, SLOTS), 1) < occupied_entries_per_strip[:, None]).astype(jnp.float32)
    weighted = tiled.astype(jnp.float32) * slot_mask[None, :, :, None]
    incoming = jnp.einsum("rkij,brkj->bri", shape_coupling_matrices.astype(jnp.float32), weighted,
                          precision=lax.Precision.HIGHEST).reshape(BANDS, FACET_TOTAL)
    thermal_distribution = emitter_terms(centre_frequency, frequency_span, facet_kelvins)
    planck_sum = jnp.sum(thermal_distribution, 0)
    energy_portion = thermal_distribution / planck_sum
    kelvins_third_power = facet_kelvins ** 3
    ideal_emitter_power = energy_portion * kelvins_third_power * facet_kelvins
    refreshed_leaving_energy = emitting_ability * ideal_emitter_power + (1.0 - emitting_ability) * incoming
    quotient = emitting_ability / (1.0 - emitting_ability)
    balance_power_density = jnp.sum(quotient * (ideal_emitter_power - refreshed_leaving_energy), 0)
    power_gradient = jnp.sum(quotient * 4.0 * energy_portion * kelvins_third_power, 0)
    corrected_kelvins = facet_kelvins - (balance_power_density - prescribed_power_density) / power_gradient
    return corrected_kelvins, refreshed_leaving_energy
```

```python
import jax
import jax.numpy as jnp
from jax import lax
from jax.sharding import PartitionSpec as P


def emitter_terms(centre_sample, frequency_spacing, facet_kelvins):
    return (
        frequency_spacing[:, None]
        * centre_sample[:, None] ** 3
        / jnp.expm1(centre_sample[:, None] / facet_kelvins[None, :])
    )


def shifted(x, axis, size):
    outs = [x]
    for s in range(1, size):
        outs.append(lax.ppermute(x, axis, [(i, (i + s) % size) for i in range(size)]))
    return jnp.stack(outs)


def canonical(by_shift, me, size):
    order = (me - jnp.arange(size)) % size
    return jnp.take(by_shift, order, axis=0)


def make_on_device(n_band, n_row):
    def on_device(
        shape_coupling_matrices,
        target_strip_index,
        occupied_entries_per_strip,
        prior_leaving_energy,
        facet_kelvins,
        emitting_ability,
        centre_frequency,
        frequency_span,
        prescribed_power_density,
    ):
        band_me = lax.axis_index("band")
        row_me = lax.axis_index("row")
        bands_here, facets_here = prior_leaving_energy.shape
        tile_rows, slot_count = target_strip_index.shape
        tile_size = shape_coupling_matrices.shape[2]
        tiles_dev = facets_here // tile_size
        entries = tile_rows * slot_count

        scalars = jnp.concatenate([centre_frequency, frequency_span])
        all_scalars = canonical(shifted(scalars, "band", n_band), band_me, n_band)
        by_row = shifted(prior_leaving_energy, "row", n_row)
        gathered = by_row.reshape(n_row * tiles_dev, tile_size)

        flat_cols = target_strip_index.reshape(entries)
        owner = flat_cols // tiles_dev
        local = flat_cols % tiles_dev
        picked = gathered[((row_me - owner) % n_row) * tiles_dev + local]
        picked = picked.reshape(bands_here, tile_rows, slot_count, tile_size)
        slot_used = (
            lax.broadcasted_iota(jnp.int32, (tile_rows, slot_count), 1)
            < occupied_entries_per_strip[:, None]
        )
        masked = jnp.where(slot_used[None, :, :, None], picked, jnp.zeros_like(picked))
        incoming = jnp.einsum(
            "rkij,brkj->bri", shape_coupling_matrices, masked, preferred_element_type=jnp.float32
        ).reshape(bands_here, facets_here)

        partial_terms = emitter_terms(centre_frequency, frequency_span, facet_kelvins)
        all_terms = emitter_terms(all_scalars[:, 0], all_scalars[:, 1], facet_kelvins)
        planck_sum = jnp.sum(all_terms, 0)
        energy_portion = partial_terms / planck_sum
        kelvins_third_power = facet_kelvins**3
        ideal_emitter_power = energy_portion * kelvins_third_power * facet_kelvins
        refreshed_leaving_energy = (
            emitting_ability * ideal_emitter_power + (1.0 - emitting_ability) * incoming
        )
        quotient = emitting_ability / (1.0 - emitting_ability)
        flux_part = jnp.sum(quotient * (ideal_emitter_power - refreshed_leaving_energy), 0)
        gradient_piece = jnp.sum(quotient * 4.0 * energy_portion * kelvins_third_power, 0)
        pieces = jnp.stack([flux_part, gradient_piece])
        summed = jnp.sum(canonical(shifted(pieces, "band", n_band), band_me, n_band), 0)
        balance_power_density, power_gradient = summed[0], summed[1]
        corrected_kelvins = (
            facet_kelvins - (balance_power_density - prescribed_power_density) / power_gradient
        )
        return (corrected_kelvins, refreshed_leaving_energy)

    return on_device


def solution(mesh):
    in_specs = (
        P("row", None, None, None),
        P("row", None),
        P("row"),
        P("band", "row"),
        P("row"),
        P("band", "row"),
        P("band"),
        P("band"),
        P("row"),
    )
    out_specs = (P("row"), P("band", "row"))
    on_device = make_on_device(mesh.shape["band"], mesh.shape["row"])
    return jax.shard_map(
        on_device, mesh=mesh, in_specs=in_specs, out_specs=out_specs, check_vma=False
    )
```

```python
import jax
import jax.numpy as jnp
from jax import lax
from jax.sharding import PartitionSpec as P


def emitter_terms(centre_sample, frequency_spacing, facet_kelvins):
    return (
        frequency_spacing[:, None]
        * centre_sample[:, None] ** 3
        / jnp.expm1(centre_sample[:, None] / facet_kelvins[None, :])
    )


def shifted(x, axis, size):
    outs = [x]
    for s in range(1, size):
        outs.append(lax.ppermute(x, axis, [(i, (i + s) % size) for i in range(size)]))
    return jnp.stack(outs)


def canonical(by_shift, me, size):
    order = (me - jnp.arange(size)) % size
    return jnp.take(by_shift, order, axis=0)


def make_on_device(n_band, n_row):
    def on_device(
        shape_coupling_matrices,
        target_strip_index,
        occupied_entries_per_strip,
        prior_leaving_energy,
        facet_kelvins,
        emitting_ability,
        centre_frequency,
        frequency_span,
        prescribed_power_density,
    ):
        band_me = lax.axis_index("band")
        row_me = lax.axis_index("row")
        bands_here, facets_here = prior_leaving_energy.shape
        tile_rows, slot_count = target_strip_index.shape
        tile_size = shape_coupling_matrices.shape[2]
        tiles_dev = facets_here // tile_size
        entries = tile_rows * slot_count

        by_row = shifted(prior_leaving_energy, "row", n_row)
        gathered = by_row.reshape(n_row * tiles_dev, tile_size)

        flat_cols = target_strip_index.reshape(entries)
        owner = flat_cols // tiles_dev
        local = flat_cols % tiles_dev
        picked = gathered[((row_me - owner) % n_row) * tiles_dev + local]
        picked = picked.reshape(bands_here, tile_rows, slot_count, tile_size)
        slot_used = (
            lax.broadcasted_iota(jnp.int32, (tile_rows, slot_count), 1)
            < occupied_entries_per_strip[:, None]
        )
        masked = jnp.where(slot_used[None, :, :, None], picked, jnp.zeros_like(picked))
        incoming = jnp.einsum(
            "rkij,brkj->bri", shape_coupling_matrices, masked, preferred_element_type=jnp.float32
        ).reshape(bands_here, facets_here)

        partial_terms = emitter_terms(centre_frequency, frequency_span, facet_kelvins)
        quotient = emitting_ability / (1.0 - emitting_ability)
        pieces = jnp.concatenate(
            [
                partial_terms,
                emitting_ability * partial_terms,
                quotient * partial_terms,
                emitting_ability * incoming,
            ]
        )
        summed = jnp.sum(canonical(shifted(pieces, "band", n_band), band_me, n_band), 0)
        planck_sum, emitted_sum, gradient_sum, absorbed_sum = summed[0], summed[1], summed[2], summed[3]
        energy_portion = partial_terms / planck_sum
        kelvins_third_power = facet_kelvins**3
        ideal_emitter_power = energy_portion * kelvins_third_power * facet_kelvins
        refreshed_leaving_energy = (
            emitting_ability * ideal_emitter_power + (1.0 - emitting_ability) * incoming
        )
        balance_power_density = (
            emitted_sum / planck_sum * kelvins_third_power * facet_kelvins - absorbed_sum
        )
        power_gradient = gradient_sum / planck_sum * 4.0 * kelvins_third_power
        corrected_kelvins = (
            facet_kelvins - (balance_power_density - prescribed_power_density) / power_gradient
        )
        return (corrected_kelvins, refreshed_leaving_energy)

    return on_device


def solution(mesh):
    in_specs = (
        P("row", None, None, None),
        P("row", None),
        P("row"),
        P("band", "row"),
        P("row"),
        P("band", "row"),
        P("band"),
        P("band"),
        P("row"),
    )
    out_specs = (P("row"), P("band", "row"))
    on_device = make_on_device(mesh.shape["band"], mesh.shape["row"])
    return jax.shard_map(
        on_device, mesh=mesh, in_specs=in_specs, out_specs=out_specs, check_vma=False
    )
```

```python
import jax
import jax.numpy as jnp
from jax import lax
from jax.experimental import pallas as pl
from jax.experimental.pallas import tpu as pltpu
from jax.sharding import PartitionSpec as P


def emitter_terms(centre_sample, frequency_spacing, facet_kelvins):
    return (
        frequency_spacing[:, None]
        * centre_sample[:, None] ** 3
        / jnp.expm1(centre_sample[:, None] / facet_kelvins[None, :])
    )


def shifted(x, axis, size):
    outs = [x]
    for s in range(1, size):
        outs.append(lax.ppermute(x, axis, [(i, (i + s) % size) for i in range(size)]))
    return jnp.stack(outs)


def canonical(by_shift, me, size):
    order = (me - jnp.arange(size)) % size
    return jnp.take(by_shift, order, axis=0)


def incoming_kernel(n_src, rows_per_step, slot_count):
    def kernel(index_ref, used_ref, *refs):
        sources = refs[:n_src]
        coupling_ref, out_ref, table_ref = refs[n_src:]
        step = pl.program_id(0)
        tiles_per_src = sources[0].shape[0]

        @pl.when(step == 0)
        def _():
            for s in range(n_src):
                table_ref[pl.ds(s * tiles_per_src, tiles_per_src), :] = sources[s][...].astype(
                    jnp.float32
                )

        for rr in range(rows_per_step):
            r = step * rows_per_step + rr
            acc = jnp.zeros((8, coupling_ref.shape[-1]), jnp.float32)
            for k in range(slot_count):
                row = table_ref[pl.ds(index_ref[r * slot_count + k], 1), :]
                row = jnp.where(k < used_ref[r], row, jnp.zeros_like(row))
                lhs = jnp.broadcast_to(row, (8, row.shape[1])).astype(jnp.bfloat16)
                acc = acc + lax.dot_general(
                    lhs,
                    coupling_ref[rr, k],
                    (((1,), (1,)), ((), ())),
                    preferred_element_type=jnp.float32,
                )
            out_ref[pl.ds(rr, 1), :] = acc[0:1]

    return kernel


def incoming_of(index, used, sources, coupling):
    tile_rows, slot_count, tile_size, _ = coupling.shape
    rows_per_step = 32 if tile_rows % 32 == 0 else tile_rows
    n_src = len(sources)
    tiles_per_src = sources[0].shape[0]
    full = lambda shape: pl.BlockSpec(shape, lambda g, i, o: (0,) * len(shape))
    return pl.pallas_call(
        incoming_kernel(n_src, rows_per_step, slot_count),
        grid_spec=pltpu.PrefetchScalarGridSpec(
            num_scalar_prefetch=2,
            grid=(tile_rows // rows_per_step,),
            in_specs=[full(src.shape) for src in sources]
            + [
                pl.BlockSpec(
                    (rows_per_step, slot_count, tile_size, tile_size),
                    lambda g, i, o: (g, 0, 0, 0),
                )
            ],
            out_specs=pl.BlockSpec((rows_per_step, tile_size), lambda g, i, o: (g, 0)),
            scratch_shapes=[pltpu.VMEM((n_src * tiles_per_src, tile_size), jnp.float32)],
        ),
        out_shape=jax.ShapeDtypeStruct((tile_rows, tile_size), jnp.float32),
        compiler_params=pltpu.CompilerParams(dimension_semantics=("arbitrary",)),
    )(index, used, *sources, coupling)


def make_on_device(n_band, n_row):
    def on_device(
        shape_coupling_matrices,
        target_strip_index,
        occupied_entries_per_strip,
        prior_leaving_energy,
        facet_kelvins,
        emitting_ability,
        centre_frequency,
        frequency_span,
        prescribed_power_density,
    ):
        band_me = lax.axis_index("band")
        row_me = lax.axis_index("row")
        bands_here, facets_here = prior_leaving_energy.shape
        tile_rows, slot_count = target_strip_index.shape
        tile_size = shape_coupling_matrices.shape[2]
        tiles_dev = facets_here // tile_size
        entries = tile_rows * slot_count

        own = prior_leaving_energy.reshape(tiles_dev, tile_size)
        sources = [own] + [
            lax.ppermute(own, "row", [(i, (i + s) % n_row) for i in range(n_row)])
            for s in range(1, n_row)
        ]
        flat_cols = target_strip_index.reshape(entries)
        owner = flat_cols // tiles_dev
        local = flat_cols % tiles_dev
        index = ((row_me - owner) % n_row) * tiles_dev + local
        incoming = incoming_of(
            index, occupied_entries_per_strip, sources, shape_coupling_matrices
        ).reshape(bands_here, facets_here)

        partial_terms = emitter_terms(centre_frequency, frequency_span, facet_kelvins)
        quotient = emitting_ability / (1.0 - emitting_ability)
        pieces = jnp.concatenate(
            [
                partial_terms,
                emitting_ability * partial_terms,
                quotient * partial_terms,
                emitting_ability * incoming,
            ]
        )
        summed = jnp.sum(canonical(shifted(pieces, "band", n_band), band_me, n_band), 0)
        planck_sum, emitted_sum, gradient_sum, absorbed_sum = summed[0], summed[1], summed[2], summed[3]
        energy_portion = partial_terms / planck_sum
        kelvins_third_power = facet_kelvins**3
        ideal_emitter_power = energy_portion * kelvins_third_power * facet_kelvins
        refreshed_leaving_energy = (
            emitting_ability * ideal_emitter_power + (1.0 - emitting_ability) * incoming
        )
        balance_power_density = (
            emitted_sum / planck_sum * kelvins_third_power * facet_kelvins - absorbed_sum
        )
        power_gradient = gradient_sum / planck_sum * 4.0 * kelvins_third_power
        corrected_kelvins = (
            facet_kelvins - (balance_power_density - prescribed_power_density) / power_gradient
        )
        return (corrected_kelvins, refreshed_leaving_energy)

    return on_device


def solution(mesh):
    in_specs = (
        P("row", None, None, None),
        P("row", None),
        P("row"),
        P("band", "row"),
        P("row"),
        P("band", "row"),
        P("band"),
        P("band"),
        P("row"),
    )
    out_specs = (P("row"), P("band", "row"))
    on_device = make_on_device(mesh.shape["band"], mesh.shape["row"])
    return jax.shard_map(
        on_device, mesh=mesh, in_specs=in_specs, out_specs=out_specs, check_vma=False
    )
```

```python
import jax
import jax.numpy as jnp
from jax import lax
from jax.experimental import pallas as pl
from jax.experimental.pallas import tpu as pltpu
from jax.sharding import PartitionSpec as P


def emitter_terms(centre_sample, frequency_spacing, facet_kelvins):
    return (
        frequency_spacing[:, None]
        * centre_sample[:, None] ** 3
        / jnp.expm1(centre_sample[:, None] / facet_kelvins[None, :])
    )


def shifted(x, axis, size):
    outs = [x]
    for s in range(1, size):
        outs.append(lax.ppermute(x, axis, [(i, (i + s) % size) for i in range(size)]))
    return jnp.stack(outs)


def canonical(by_shift, me, size):
    order = (me - jnp.arange(size)) % size
    return jnp.take(by_shift, order, axis=0)


def incoming_kernel(n_src, rows_per_step, slot_count):
    def kernel(index_ref, used_ref, *refs):
        sources = refs[:n_src]
        coupling_ref, out_ref, table_ref = refs[n_src:]
        step = pl.program_id(0)
        tiles_per_src = sources[0].shape[0]

        @pl.when(step == 0)
        def _():
            for s in range(n_src):
                table_ref[pl.ds(s * tiles_per_src, tiles_per_src), :] = sources[s][...].astype(
                    jnp.float32
                )

        for rr in range(rows_per_step):
            r = step * rows_per_step + rr
            acc = jnp.zeros(coupling_ref.shape[2:], jnp.float32)
            for k in range(slot_count):
                row = table_ref[pl.ds(index_ref[r * slot_count + k], 1), :]
                row = jnp.where(k < used_ref[r], row, jnp.zeros_like(row))
                acc = acc + coupling_ref[rr, k].astype(jnp.float32) * row
            out_ref[pl.ds(rr, 1), :] = jnp.sum(acc.T, axis=0, keepdims=True)

    return kernel


def incoming_of(index, used, sources, coupling):
    tile_rows, slot_count, tile_size, _ = coupling.shape
    rows_per_step = 32 if tile_rows % 32 == 0 else tile_rows
    n_src = len(sources)
    tiles_per_src = sources[0].shape[0]
    full = lambda shape: pl.BlockSpec(shape, lambda g, i, o: (0,) * len(shape))
    return pl.pallas_call(
        incoming_kernel(n_src, rows_per_step, slot_count),
        grid_spec=pltpu.PrefetchScalarGridSpec(
            num_scalar_prefetch=2,
            grid=(tile_rows // rows_per_step,),
            in_specs=[full(src.shape) for src in sources]
            + [
                pl.BlockSpec(
                    (rows_per_step, slot_count, tile_size, tile_size),
                    lambda g, i, o: (g, 0, 0, 0),
                )
            ],
            out_specs=pl.BlockSpec((rows_per_step, tile_size), lambda g, i, o: (g, 0)),
            scratch_shapes=[pltpu.VMEM((n_src * tiles_per_src, tile_size), jnp.float32)],
        ),
        out_shape=jax.ShapeDtypeStruct((tile_rows, tile_size), jnp.float32),
        compiler_params=pltpu.CompilerParams(dimension_semantics=("arbitrary",)),
    )(index, used, *sources, coupling)


def make_on_device(n_band, n_row):
    def on_device(
        shape_coupling_matrices,
        target_strip_index,
        occupied_entries_per_strip,
        prior_leaving_energy,
        facet_kelvins,
        emitting_ability,
        centre_frequency,
        frequency_span,
        prescribed_power_density,
    ):
        band_me = lax.axis_index("band")
        row_me = lax.axis_index("row")
        bands_here, facets_here = prior_leaving_energy.shape
        tile_rows, slot_count = target_strip_index.shape
        tile_size = shape_coupling_matrices.shape[2]
        tiles_dev = facets_here // tile_size
        entries = tile_rows * slot_count

        own = prior_leaving_energy.reshape(tiles_dev, tile_size)
        sources = [own] + [
            lax.ppermute(own, "row", [(i, (i + s) % n_row) for i in range(n_row)])
            for s in range(1, n_row)
        ]
        flat_cols = target_strip_index.reshape(entries)
        owner = flat_cols // tiles_dev
        local = flat_cols % tiles_dev
        index = ((row_me - owner) % n_row) * tiles_dev + local
        incoming = incoming_of(
            index, occupied_entries_per_strip, sources, shape_coupling_matrices
        ).reshape(bands_here, facets_here)

        partial_terms = emitter_terms(centre_frequency, frequency_span, facet_kelvins)
        quotient = emitting_ability / (1.0 - emitting_ability)
        pieces = jnp.concatenate(
            [
                partial_terms,
                emitting_ability * partial_terms,
                quotient * partial_terms,
                emitting_ability * incoming,
            ]
        )
        summed = jnp.sum(canonical(shifted(pieces, "band", n_band), band_me, n_band), 0)
        planck_sum, emitted_sum, gradient_sum, absorbed_sum = summed[0], summed[1], summed[2], summed[3]
        energy_portion = partial_terms / planck_sum
        kelvins_third_power = facet_kelvins**3
        ideal_emitter_power = energy_portion * kelvins_third_power * facet_kelvins
        refreshed_leaving_energy = (
            emitting_ability * ideal_emitter_power + (1.0 - emitting_ability) * incoming
        )
        balance_power_density = (
            emitted_sum / planck_sum * kelvins_third_power * facet_kelvins - absorbed_sum
        )
        power_gradient = gradient_sum / planck_sum * 4.0 * kelvins_third_power
        corrected_kelvins = (
            facet_kelvins - (balance_power_density - prescribed_power_density) / power_gradient
        )
        return (corrected_kelvins, refreshed_leaving_energy)

    return on_device


def solution(mesh):
    in_specs = (
        P("row", None, None, None),
        P("row", None),
        P("row"),
        P("band", "row"),
        P("row"),
        P("band", "row"),
        P("band"),
        P("band"),
        P("row"),
    )
    out_specs = (P("row"), P("band", "row"))
    on_device = make_on_device(mesh.shape["band"], mesh.shape["row"])
    return jax.shard_map(
        on_device, mesh=mesh, in_specs=in_specs, out_specs=out_specs, check_vma=False
    )
```

```python
import jax
import jax.numpy as jnp
from jax import lax
from jax.experimental import pallas as pl
from jax.experimental.pallas import tpu as pltpu
from jax.sharding import PartitionSpec as P


def emitter_terms(centre_sample, frequency_spacing, facet_kelvins):
    return (
        frequency_spacing[:, None]
        * centre_sample[:, None] ** 3
        / jnp.expm1(centre_sample[:, None] / facet_kelvins[None, :])
    )


def shifted(x, axis, size):
    outs = [x]
    for s in range(1, size):
        outs.append(lax.ppermute(x, axis, [(i, (i + s) % size) for i in range(size)]))
    return jnp.stack(outs)


def canonical(by_shift, me, size):
    order = (me - jnp.arange(size)) % size
    return jnp.take(by_shift, order, axis=0)


def incoming_kernel(n_src, rows_per_step, slot_count):
    def kernel(index_ref, used_ref, *refs):
        sources = refs[:n_src]
        coupling_ref, out_ref, table_ref = refs[n_src:]
        step = pl.program_id(0)
        tiles_per_src = sources[0].shape[0]

        @pl.when(step == 0)
        def _():
            for s in range(n_src):
                table_ref[pl.ds(s * tiles_per_src, tiles_per_src), :] = sources[s][...].astype(
                    jnp.float32
                )

        for rr in range(rows_per_step):
            r = step * rows_per_step + rr
            acc = jnp.zeros(coupling_ref.shape[2:], jnp.float32)
            for k in range(slot_count):
                row = table_ref[pl.ds(index_ref[r * slot_count + k], 1), :]
                row = jnp.where(k < used_ref[r], row, jnp.zeros_like(row))
                acc = acc + coupling_ref[rr, k].astype(jnp.float32) * row
            out_ref[pl.ds(rr, 1), :] = jnp.sum(acc.T, axis=0, keepdims=True)

    return kernel


def incoming_of(index, used, sources, coupling):
    tile_rows, slot_count, tile_size, _ = coupling.shape
    rows_per_step = 32 if tile_rows % 32 == 0 else tile_rows
    n_src = len(sources)
    tiles_per_src = sources[0].shape[0]
    full = lambda shape: pl.BlockSpec(shape, lambda g, i, o: (0,) * len(shape))
    return pl.pallas_call(
        incoming_kernel(n_src, rows_per_step, slot_count),
        grid_spec=pltpu.PrefetchScalarGridSpec(
            num_scalar_prefetch=2,
            grid=(tile_rows // rows_per_step,),
            in_specs=[full(src.shape) for src in sources]
            + [
                pl.BlockSpec(
                    (rows_per_step, slot_count, tile_size, tile_size),
                    lambda g, i, o: (g, 0, 0, 0),
                )
            ],
            out_specs=pl.BlockSpec((rows_per_step, tile_size), lambda g, i, o: (g, 0)),
            scratch_shapes=[pltpu.VMEM((n_src * tiles_per_src, tile_size), jnp.float32)],
        ),
        out_shape=jax.ShapeDtypeStruct((tile_rows, tile_size), jnp.float32),
        compiler_params=pltpu.CompilerParams(dimension_semantics=("arbitrary",)),
    )(index, used, *sources, coupling)


def make_on_device(n_band, n_row):
    def on_device(
        shape_coupling_matrices,
        target_strip_index,
        occupied_entries_per_strip,
        prior_leaving_energy,
        facet_kelvins,
        emitting_ability,
        centre_frequency,
        frequency_span,
        prescribed_power_density,
    ):
        band_me = lax.axis_index("band")
        row_me = lax.axis_index("row")
        bands_here, facets_here = prior_leaving_energy.shape
        tile_rows, slot_count = target_strip_index.shape
        tile_size = shape_coupling_matrices.shape[2]
        tiles_dev = facets_here // tile_size
        entries = tile_rows * slot_count

        own = prior_leaving_energy.reshape(tiles_dev, tile_size)
        flat_cols = target_strip_index.reshape(entries)
        owner = flat_cols // tiles_dev
        local = flat_cols % tiles_dev
        if n_row % 2 == 0:
            partner = lax.ppermute(own, "row", [(i, i ^ 1) for i in range(n_row)])
            pair = jnp.concatenate([own, partner])
            sources = [pair] + [
                lax.ppermute(pair, "row", [(i, (i + 2 * s) % n_row) for i in range(n_row)])
                for s in range(1, n_row // 2)
            ]
            half = (owner ^ row_me) & 1
            shift = ((row_me - (owner ^ half)) % n_row) // 2
            index = (shift * 2 + half) * tiles_dev + local
        else:
            sources = [own] + [
                lax.ppermute(own, "row", [(i, (i + s) % n_row) for i in range(n_row)])
                for s in range(1, n_row)
            ]
            index = ((row_me - owner) % n_row) * tiles_dev + local
        incoming = incoming_of(
            index, occupied_entries_per_strip, sources, shape_coupling_matrices
        ).reshape(bands_here, facets_here)

        partial_terms = emitter_terms(centre_frequency, frequency_span, facet_kelvins)
        quotient = emitting_ability / (1.0 - emitting_ability)
        pieces = jnp.concatenate(
            [
                partial_terms,
                emitting_ability * partial_terms,
                quotient * partial_terms,
                emitting_ability * incoming,
            ]
        )
        summed = jnp.sum(canonical(shifted(pieces, "band", n_band), band_me, n_band), 0)
        planck_sum, emitted_sum, gradient_sum, absorbed_sum = summed[0], summed[1], summed[2], summed[3]
        energy_portion = partial_terms / planck_sum
        kelvins_third_power = facet_kelvins**3
        ideal_emitter_power = energy_portion * kelvins_third_power * facet_kelvins
        refreshed_leaving_energy = (
            emitting_ability * ideal_emitter_power + (1.0 - emitting_ability) * incoming
        )
        balance_power_density = (
            emitted_sum / planck_sum * kelvins_third_power * facet_kelvins - absorbed_sum
        )
        power_gradient = gradient_sum / planck_sum * 4.0 * kelvins_third_power
        corrected_kelvins = (
            facet_kelvins - (balance_power_density - prescribed_power_density) / power_gradient
        )
        return (corrected_kelvins, refreshed_leaving_energy)

    return on_device


def solution(mesh):
    in_specs = (
        P("row", None, None, None),
        P("row", None),
        P("row"),
        P("band", "row"),
        P("row"),
        P("band", "row"),
        P("band"),
        P("band"),
        P("row"),
    )
    out_specs = (P("row"), P("band", "row"))
    on_device = make_on_device(mesh.shape["band"], mesh.shape["row"])
    return jax.shard_map(
        on_device, mesh=mesh, in_specs=in_specs, out_specs=out_specs, check_vma=False
    )
```

```python
import jax
import jax.numpy as jnp
from jax import lax
from jax.experimental import pallas as pl
from jax.experimental.pallas import tpu as pltpu
from jax.sharding import PartitionSpec as P


def emitter_terms(centre_sample, frequency_spacing, facet_kelvins):
    return (
        frequency_spacing[:, None]
        * centre_sample[:, None] ** 3
        / jnp.expm1(centre_sample[:, None] / facet_kelvins[None, :])
    )


def shifted(x, axis, size):
    outs = [x]
    for s in range(1, size):
        outs.append(lax.ppermute(x, axis, [(i, (i + s) % size) for i in range(size)]))
    return outs


def order_free_sum(parts):
    parts = list(parts)
    n = len(parts)
    for sweep in range(n):
        for i in range(sweep % 2, n - 1, 2):
            lo = jnp.minimum(parts[i], parts[i + 1])
            hi = jnp.maximum(parts[i], parts[i + 1])
            parts[i], parts[i + 1] = lo, hi
    total = parts[0]
    for p in parts[1:]:
        total = total + p
    return total


def incoming_kernel(n_src, rows_per_step, slot_count):
    def kernel(index_ref, used_ref, *refs):
        sources = refs[:n_src]
        coupling_ref, out_ref, table_ref = refs[n_src:]
        step = pl.program_id(0)
        tiles_per_src = sources[0].shape[0]

        @pl.when(step == 0)
        def _():
            for s in range(n_src):
                table_ref[pl.ds(s * tiles_per_src, tiles_per_src), :] = sources[s][...].astype(
                    jnp.float32
                )

        for rr in range(rows_per_step):
            r = step * rows_per_step + rr
            acc = jnp.zeros(coupling_ref.shape[2:], jnp.float32)
            for k in range(slot_count):
                row = table_ref[pl.ds(index_ref[r * slot_count + k], 1), :]
                row = jnp.where(k < used_ref[r], row, jnp.zeros_like(row))
                acc = acc + coupling_ref[rr, k].astype(jnp.float32) * row
            out_ref[pl.ds(rr, 1), :] = jnp.sum(acc.T, axis=0, keepdims=True)

    return kernel


def incoming_of(index, used, sources, coupling):
    tile_rows, slot_count, tile_size, _ = coupling.shape
    rows_per_step = 32 if tile_rows % 32 == 0 else tile_rows
    n_src = len(sources)
    tiles_per_src = sources[0].shape[0]
    full = lambda shape: pl.BlockSpec(shape, lambda g, i, o: (0,) * len(shape))
    return pl.pallas_call(
        incoming_kernel(n_src, rows_per_step, slot_count),
        grid_spec=pltpu.PrefetchScalarGridSpec(
            num_scalar_prefetch=2,
            grid=(tile_rows // rows_per_step,),
            in_specs=[full(src.shape) for src in sources]
            + [
                pl.BlockSpec(
                    (rows_per_step, slot_count, tile_size, tile_size),
                    lambda g, i, o: (g, 0, 0, 0),
                )
            ],
            out_specs=pl.BlockSpec((rows_per_step, tile_size), lambda g, i, o: (g, 0)),
            scratch_shapes=[pltpu.VMEM((n_src * tiles_per_src, tile_size), jnp.float32)],
        ),
        out_shape=jax.ShapeDtypeStruct((tile_rows, tile_size), jnp.float32),
        compiler_params=pltpu.CompilerParams(dimension_semantics=("arbitrary",)),
    )(index, used, *sources, coupling)


def make_on_device(n_band, n_row):
    def on_device(
        shape_coupling_matrices,
        target_strip_index,
        occupied_entries_per_strip,
        prior_leaving_energy,
        facet_kelvins,
        emitting_ability,
        centre_frequency,
        frequency_span,
        prescribed_power_density,
    ):
        row_me = lax.axis_index("row")
        bands_here, facets_here = prior_leaving_energy.shape
        tile_rows, slot_count = target_strip_index.shape
        tile_size = shape_coupling_matrices.shape[2]
        tiles_dev = facets_here // tile_size
        entries = tile_rows * slot_count

        own = prior_leaving_energy.reshape(tiles_dev, tile_size)
        flat_cols = target_strip_index.reshape(entries)
        owner = flat_cols // tiles_dev
        local = flat_cols % tiles_dev
        if n_row % 2 == 0:
            partner = lax.ppermute(own, "row", [(i, i ^ 1) for i in range(n_row)])
            pair = jnp.concatenate([own, partner])
            sources = [pair] + [
                lax.ppermute(pair, "row", [(i, (i + 2 * s) % n_row) for i in range(n_row)])
                for s in range(1, n_row // 2)
            ]
            half = (owner ^ row_me) & 1
            shift = ((row_me - (owner ^ half)) % n_row) // 2
            index = (shift * 2 + half) * tiles_dev + local
        else:
            sources = [own] + [
                lax.ppermute(own, "row", [(i, (i + s) % n_row) for i in range(n_row)])
                for s in range(1, n_row)
            ]
            index = ((row_me - owner) % n_row) * tiles_dev + local
        incoming = incoming_of(
            index, occupied_entries_per_strip, sources, shape_coupling_matrices
        ).reshape(bands_here, facets_here)

        partial_terms = emitter_terms(centre_frequency, frequency_span, facet_kelvins)
        quotient = emitting_ability / (1.0 - emitting_ability)
        pieces = jnp.concatenate(
            [
                partial_terms,
                emitting_ability * partial_terms,
                quotient * partial_terms,
                emitting_ability * incoming,
            ]
        )
        summed = order_free_sum(shifted(pieces, "band", n_band))
        planck_sum, emitted_sum, gradient_sum, absorbed_sum = summed[0], summed[1], summed[2], summed[3]
        energy_portion = partial_terms / planck_sum
        kelvins_third_power = facet_kelvins**3
        ideal_emitter_power = energy_portion * kelvins_third_power * facet_kelvins
        refreshed_leaving_energy = (
            emitting_ability * ideal_emitter_power + (1.0 - emitting_ability) * incoming
        )
        balance_power_density = (
            emitted_sum / planck_sum * kelvins_third_power * facet_kelvins - absorbed_sum
        )
        power_gradient = gradient_sum / planck_sum * 4.0 * kelvins_third_power
        corrected_kelvins = (
            facet_kelvins - (balance_power_density - prescribed_power_density) / power_gradient
        )
        return (corrected_kelvins, refreshed_leaving_energy)

    return on_device


def solution(mesh):
    in_specs = (
        P("row", None, None, None),
        P("row", None),
        P("row"),
        P("band", "row"),
        P("row"),
        P("band", "row"),
        P("band"),
        P("band"),
        P("row"),
    )
    out_specs = (P("row"), P("band", "row"))
    on_device = make_on_device(mesh.shape["band"], mesh.shape["row"])
    return jax.shard_map(
        on_device, mesh=mesh, in_specs=in_specs, out_specs=out_specs, check_vma=False
    )
```

```python
import jax
import jax.numpy as jnp
from jax import lax
from jax.experimental import pallas as pl
from jax.experimental.pallas import tpu as pltpu
from jax.sharding import PartitionSpec as P


def emitter_terms(centre_sample, frequency_spacing, facet_kelvins):
    return (
        frequency_spacing[:, None]
        * centre_sample[:, None] ** 3
        / jnp.expm1(centre_sample[:, None] / facet_kelvins[None, :])
    )


def shifted(x, axis, size):
    outs = [x]
    for s in range(1, size):
        outs.append(lax.ppermute(x, axis, [(i, (i + s) % size) for i in range(size)]))
    return outs


def order_free_sum(parts):
    parts = list(parts)
    n = len(parts)
    for sweep in range(n):
        for i in range(sweep % 2, n - 1, 2):
            lo = jnp.minimum(parts[i], parts[i + 1])
            hi = jnp.maximum(parts[i], parts[i + 1])
            parts[i], parts[i + 1] = lo, hi
    total = parts[0]
    for p in parts[1:]:
        total = total + p
    return total


def incoming_kernel(n_src, rows_per_step, slot_count):
    def kernel(index_ref, used_ref, *refs):
        sources = refs[:n_src]
        coupling_ref, out_ref, table_ref = refs[n_src:]
        step = pl.program_id(0)
        tiles_per_src = sources[0].shape[0]

        @pl.when(step == 0)
        def _():
            for s in range(n_src):
                table_ref[pl.ds(s * tiles_per_src, tiles_per_src), :] = sources[s][...].astype(
                    jnp.float32
                )

        for rr in range(rows_per_step):
            r = step * rows_per_step + rr
            acc = jnp.zeros(coupling_ref.shape[2:], jnp.float32)
            for k in range(slot_count):
                row = table_ref[pl.ds(index_ref[r * slot_count + k], 1), :]
                row = jnp.where(k < used_ref[r], row, jnp.zeros_like(row))
                acc = acc + coupling_ref[rr, k].astype(jnp.float32) * row
            out_ref[pl.ds(rr, 1), :] = jnp.sum(acc.T, axis=0, keepdims=True)

    return kernel


def incoming_of(index, used, sources, coupling):
    tile_rows, slot_count, tile_size, _ = coupling.shape
    rows_per_step = 32 if tile_rows % 32 == 0 else tile_rows
    n_src = len(sources)
    tiles_per_src = sources[0].shape[0]
    full = lambda shape: pl.BlockSpec(shape, lambda g, i, o: (0,) * len(shape))
    return pl.pallas_call(
        incoming_kernel(n_src, rows_per_step, slot_count),
        grid_spec=pltpu.PrefetchScalarGridSpec(
            num_scalar_prefetch=2,
            grid=(tile_rows // rows_per_step,),
            in_specs=[full(src.shape) for src in sources]
            + [
                pl.BlockSpec(
                    (rows_per_step, slot_count, tile_size, tile_size),
                    lambda g, i, o: (g, 0, 0, 0),
                )
            ],
            out_specs=pl.BlockSpec((rows_per_step, tile_size), lambda g, i, o: (g, 0)),
            scratch_shapes=[pltpu.VMEM((n_src * tiles_per_src, tile_size), jnp.float32)],
        ),
        out_shape=jax.ShapeDtypeStruct((tile_rows, tile_size), jnp.float32),
        compiler_params=pltpu.CompilerParams(dimension_semantics=("arbitrary",)),
    )(index, used, *sources, coupling)


def make_on_device(n_band, n_row):
    def on_device(
        shape_coupling_matrices,
        target_strip_index,
        occupied_entries_per_strip,
        prior_leaving_energy,
        facet_kelvins,
        emitting_ability,
        centre_frequency,
        frequency_span,
        prescribed_power_density,
    ):
        row_me = lax.axis_index("row")
        bands_here, facets_here = prior_leaving_energy.shape
        tile_rows, slot_count = target_strip_index.shape
        tile_size = shape_coupling_matrices.shape[2]
        tiles_dev = facets_here // tile_size
        entries = tile_rows * slot_count

        own = prior_leaving_energy.reshape(tiles_dev, tile_size)
        flat_cols = target_strip_index.reshape(entries)
        owner = flat_cols // tiles_dev
        local = flat_cols % tiles_dev
        if n_row % 2 == 0:
            partner = lax.ppermute(own, "row", [(i, i ^ 1) for i in range(n_row)])
            pair = jnp.concatenate([own, partner])
            sources = [pair] + [
                lax.ppermute(pair, "row", [(i, (i + 2 * s) % n_row) for i in range(n_row)])
                for s in range(1, n_row // 2)
            ]
            half = (owner ^ row_me) & 1
            shift = ((row_me - (owner ^ half)) % n_row) // 2
            index = (shift * 2 + half) * tiles_dev + local
        else:
            sources = [own] + [
                lax.ppermute(own, "row", [(i, (i + s) % n_row) for i in range(n_row)])
                for s in range(1, n_row)
            ]
            index = ((row_me - owner) % n_row) * tiles_dev + local
        incoming = incoming_of(
            index, occupied_entries_per_strip, sources, shape_coupling_matrices
        ).reshape(bands_here, facets_here)

        partial_terms = emitter_terms(centre_frequency, frequency_span, facet_kelvins)
        quotient = emitting_ability / (1.0 - emitting_ability)
        early = order_free_sum(
            shifted(
                jnp.concatenate(
                    [partial_terms, emitting_ability * partial_terms, quotient * partial_terms]
                ),
                "band",
                n_band,
            )
        )
        planck_sum, emitted_sum, gradient_sum = early[0], early[1], early[2]
        absorbed_sum = order_free_sum(shifted(emitting_ability * incoming, "band", n_band))[0]
        energy_portion = partial_terms / planck_sum
        kelvins_third_power = facet_kelvins**3
        ideal_emitter_power = energy_portion * kelvins_third_power * facet_kelvins
        refreshed_leaving_energy = (
            emitting_ability * ideal_emitter_power + (1.0 - emitting_ability) * incoming
        )
        balance_power_density = (
            emitted_sum / planck_sum * kelvins_third_power * facet_kelvins - absorbed_sum
        )
        power_gradient = gradient_sum / planck_sum * 4.0 * kelvins_third_power
        corrected_kelvins = (
            facet_kelvins - (balance_power_density - prescribed_power_density) / power_gradient
        )
        return (corrected_kelvins, refreshed_leaving_energy)

    return on_device


def solution(mesh):
    in_specs = (
        P("row", None, None, None),
        P("row", None),
        P("row"),
        P("band", "row"),
        P("row"),
        P("band", "row"),
        P("band"),
        P("band"),
        P("row"),
    )
    out_specs = (P("row"), P("band", "row"))
    on_device = make_on_device(mesh.shape["band"], mesh.shape["row"])
    return jax.shard_map(
        on_device, mesh=mesh, in_specs=in_specs, out_specs=out_specs, check_vma=False
    )
```

```python
import jax
import jax.numpy as jnp
from jax import lax
from jax.experimental import pallas as pl
from jax.experimental.pallas import tpu as pltpu
from jax.sharding import PartitionSpec as P


def emitter_terms(centre_sample, frequency_spacing, facet_kelvins):
    return (
        frequency_spacing[:, None]
        * centre_sample[:, None] ** 3
        / jnp.expm1(centre_sample[:, None] / facet_kelvins[None, :])
    )


def shifted(x, axis, size):
    outs = [x]
    for s in range(1, size):
        outs.append(lax.ppermute(x, axis, [(i, (i + s) % size) for i in range(size)]))
    return outs


def order_free_sum(parts):
    parts = list(parts)
    n = len(parts)
    for sweep in range(n):
        for i in range(sweep % 2, n - 1, 2):
            lo = jnp.minimum(parts[i], parts[i + 1])
            hi = jnp.maximum(parts[i], parts[i + 1])
            parts[i], parts[i + 1] = lo, hi
    total = parts[0]
    for p in parts[1:]:
        total = total + p
    return total


def incoming_kernel(n_src, rows_per_step, slot_count):
    def kernel(index_ref, used_ref, *refs):
        sources = refs[:n_src]
        coupling_ref, emitting_ref, out_ref, absorbed_ref, table_ref = refs[n_src:]
        step = pl.program_id(0)
        tiles_per_src = sources[0].shape[0]

        @pl.when(step == 0)
        def _():
            for s in range(n_src):
                table_ref[pl.ds(s * tiles_per_src, tiles_per_src), :] = sources[s][...].astype(
                    jnp.float32
                )

        for rr in range(rows_per_step):
            r = step * rows_per_step + rr
            acc = jnp.zeros(coupling_ref.shape[2:], jnp.float32)
            for k in range(slot_count):
                row = table_ref[pl.ds(index_ref[r * slot_count + k], 1), :]
                row = jnp.where(k < used_ref[r], row, jnp.zeros_like(row))
                acc = acc + coupling_ref[rr, k].astype(jnp.float32) * row
            incoming = jnp.sum(acc.T, axis=0, keepdims=True)
            out_ref[pl.ds(rr, 1), :] = incoming
            absorbed_ref[pl.ds(rr, 1), :] = incoming * emitting_ref[pl.ds(rr, 1), :]

    return kernel


def incoming_of(index, used, sources, coupling, emitting):
    tile_rows, slot_count, tile_size, _ = coupling.shape
    rows_per_step = 32 if tile_rows % 32 == 0 else tile_rows
    n_src = len(sources)
    tiles_per_src = sources[0].shape[0]
    full = lambda shape: pl.BlockSpec(shape, lambda g, i, o: (0,) * len(shape))
    return pl.pallas_call(
        incoming_kernel(n_src, rows_per_step, slot_count),
        grid_spec=pltpu.PrefetchScalarGridSpec(
            num_scalar_prefetch=2,
            grid=(tile_rows // rows_per_step,),
            in_specs=[full(src.shape) for src in sources]
            + [
                pl.BlockSpec(
                    (rows_per_step, slot_count, tile_size, tile_size),
                    lambda g, i, o: (g, 0, 0, 0),
                ),
                pl.BlockSpec((rows_per_step, tile_size), lambda g, i, o: (g, 0)),
            ],
            out_specs=[
                pl.BlockSpec((rows_per_step, tile_size), lambda g, i, o: (g, 0)),
                pl.BlockSpec((rows_per_step, tile_size), lambda g, i, o: (g, 0)),
            ],
            scratch_shapes=[pltpu.VMEM((n_src * tiles_per_src, tile_size), jnp.float32)],
        ),
        out_shape=[jax.ShapeDtypeStruct((tile_rows, tile_size), jnp.float32)] * 2,
        compiler_params=pltpu.CompilerParams(dimension_semantics=("arbitrary",)),
    )(index, used, *sources, coupling, emitting)


def make_on_device(n_band, n_row):
    def on_device(
        shape_coupling_matrices,
        target_strip_index,
        occupied_entries_per_strip,
        prior_leaving_energy,
        facet_kelvins,
        emitting_ability,
        centre_frequency,
        frequency_span,
        prescribed_power_density,
    ):
        row_me = lax.axis_index("row")
        bands_here, facets_here = prior_leaving_energy.shape
        tile_rows, slot_count = target_strip_index.shape
        tile_size = shape_coupling_matrices.shape[2]
        tiles_dev = facets_here // tile_size
        entries = tile_rows * slot_count

        own = prior_leaving_energy.reshape(tiles_dev, tile_size)
        flat_cols = target_strip_index.reshape(entries)
        owner = flat_cols // tiles_dev
        local = flat_cols % tiles_dev
        if n_row % 2 == 0:
            partner = lax.ppermute(own, "row", [(i, i ^ 1) for i in range(n_row)])
            pair = jnp.concatenate([own, partner])
            sources = [pair] + [
                lax.ppermute(pair, "row", [(i, (i + 2 * s) % n_row) for i in range(n_row)])
                for s in range(1, n_row // 2)
            ]
            half = (owner ^ row_me) & 1
            shift = ((row_me - (owner ^ half)) % n_row) // 2
            index = (shift * 2 + half) * tiles_dev + local
        else:
            sources = [own] + [
                lax.ppermute(own, "row", [(i, (i + s) % n_row) for i in range(n_row)])
                for s in range(1, n_row)
            ]
            index = ((row_me - owner) % n_row) * tiles_dev + local
        incoming, absorbed = incoming_of(
            index,
            occupied_entries_per_strip,
            sources,
            shape_coupling_matrices,
            emitting_ability.reshape(tile_rows, tile_size),
        )
        incoming = incoming.reshape(bands_here, facets_here)

        partial_terms = emitter_terms(centre_frequency, frequency_span, facet_kelvins)
        quotient = emitting_ability / (1.0 - emitting_ability)
        early = order_free_sum(
            shifted(
                jnp.concatenate(
                    [partial_terms, emitting_ability * partial_terms, quotient * partial_terms]
                ),
                "band",
                n_band,
            )
        )
        planck_sum, emitted_sum, gradient_sum = early[0], early[1], early[2]
        absorbed_sum = order_free_sum(shifted(absorbed, "band", n_band)).reshape(facets_here)
        energy_portion = partial_terms / planck_sum
        kelvins_third_power = facet_kelvins**3
        ideal_emitter_power = energy_portion * kelvins_third_power * facet_kelvins
        refreshed_leaving_energy = (
            emitting_ability * ideal_emitter_power + (1.0 - emitting_ability) * incoming
        )
        balance_power_density = (
            emitted_sum / planck_sum * kelvins_third_power * facet_kelvins - absorbed_sum
        )
        power_gradient = gradient_sum / planck_sum * 4.0 * kelvins_third_power
        corrected_kelvins = (
            facet_kelvins - (balance_power_density - prescribed_power_density) / power_gradient
        )
        return (corrected_kelvins, refreshed_leaving_energy)

    return on_device


def solution(mesh):
    in_specs = (
        P("row", None, None, None),
        P("row", None),
        P("row"),
        P("band", "row"),
        P("row"),
        P("band", "row"),
        P("band"),
        P("band"),
        P("row"),
    )
    out_specs = (P("row"), P("band", "row"))
    on_device = make_on_device(mesh.shape["band"], mesh.shape["row"])
    return jax.shard_map(
        on_device, mesh=mesh, in_specs=in_specs, out_specs=out_specs, check_vma=False
    )
```

```python
import jax
import jax.numpy as jnp
from jax import lax
from jax.experimental import pallas as pl
from jax.experimental.pallas import tpu as pltpu
from jax.sharding import PartitionSpec as P


def emitter_terms(centre_sample, frequency_spacing, facet_kelvins):
    return (
        frequency_spacing[:, None]
        * centre_sample[:, None] ** 3
        / jnp.expm1(centre_sample[:, None] / facet_kelvins[None, :])
    )


def shifted(x, axis, size):
    outs = [x]
    for s in range(1, size):
        outs.append(lax.ppermute(x, axis, [(i, (i + s) % size) for i in range(size)]))
    return outs


def order_free_sum(parts):
    parts = list(parts)
    n = len(parts)
    for sweep in range(n):
        for i in range(sweep % 2, n - 1, 2):
            lo = jnp.minimum(parts[i], parts[i + 1])
            hi = jnp.maximum(parts[i], parts[i + 1])
            parts[i], parts[i + 1] = lo, hi
    total = parts[0]
    for p in parts[1:]:
        total = total + p
    return total


def incoming_kernel(n_src, rows_per_step, slot_count):
    def kernel(index_ref, used_ref, *refs):
        sources = refs[:n_src]
        coupling_ref, emitting_ref, out_ref, absorbed_ref, table_ref = refs[n_src:]
        step = pl.program_id(0)
        tiles_per_src = sources[0].shape[0]

        @pl.when(step == 0)
        def _():
            for s in range(n_src):
                table_ref[pl.ds(s * tiles_per_src, tiles_per_src), :] = sources[s][...].astype(
                    jnp.float32
                )

        for rr in range(rows_per_step):
            r = step * rows_per_step + rr
            acc = jnp.zeros(coupling_ref.shape[2:], jnp.float32)
            for k in range(slot_count):
                row = table_ref[pl.ds(index_ref[r * slot_count + k], 1), :]
                row = jnp.where(k < used_ref[r], row, jnp.zeros_like(row))
                acc = acc + coupling_ref[rr, k].astype(jnp.float32) * row
            incoming = jnp.sum(acc.T, axis=0, keepdims=True)
            out_ref[pl.ds(rr, 1), :] = incoming
            absorbed_ref[pl.ds(rr, 1), :] = incoming * emitting_ref[pl.ds(rr, 1), :]

    return kernel


def incoming_of(index, used, sources, coupling, emitting):
    tile_rows, slot_count, tile_size, _ = coupling.shape
    rows_per_step = 32 if tile_rows % 32 == 0 else tile_rows
    n_src = len(sources)
    tiles_per_src = sources[0].shape[0]
    full = lambda shape: pl.BlockSpec(shape, lambda g, i, o: (0,) * len(shape))
    return pl.pallas_call(
        incoming_kernel(n_src, rows_per_step, slot_count),
        grid_spec=pltpu.PrefetchScalarGridSpec(
            num_scalar_prefetch=2,
            grid=(tile_rows // rows_per_step,),
            in_specs=[full(src.shape) for src in sources]
            + [
                pl.BlockSpec(
                    (rows_per_step, slot_count, tile_size, tile_size),
                    lambda g, i, o: (g, 0, 0, 0),
                ),
                pl.BlockSpec((rows_per_step, tile_size), lambda g, i, o: (g, 0)),
            ],
            out_specs=[
                pl.BlockSpec((rows_per_step, tile_size), lambda g, i, o: (g, 0)),
                pl.BlockSpec((rows_per_step, tile_size), lambda g, i, o: (g, 0)),
            ],
            scratch_shapes=[pltpu.VMEM((n_src * tiles_per_src, tile_size), jnp.float32)],
        ),
        out_shape=[jax.ShapeDtypeStruct((tile_rows, tile_size), jnp.float32)] * 2,
        compiler_params=pltpu.CompilerParams(dimension_semantics=("arbitrary",)),
    )(index, used, *sources, coupling, emitting)


def make_on_device(n_band, n_row):
    def on_device(
        shape_coupling_matrices,
        target_strip_index,
        occupied_entries_per_strip,
        prior_leaving_energy,
        facet_kelvins,
        emitting_ability,
        centre_frequency,
        frequency_span,
        prescribed_power_density,
    ):
        row_me = lax.axis_index("row")
        bands_here, facets_here = prior_leaving_energy.shape
        tile_rows, slot_count = target_strip_index.shape
        tile_size = shape_coupling_matrices.shape[2]
        tiles_dev = facets_here // tile_size
        entries = tile_rows * slot_count

        own = prior_leaving_energy.reshape(tiles_dev, tile_size)
        flat_cols = target_strip_index.reshape(entries)
        owner = flat_cols // tiles_dev
        local = flat_cols % tiles_dev
        if n_row % 2 == 0:
            partner = lax.ppermute(own, "row", [(i, i ^ 1) for i in range(n_row)])
            pair = jnp.concatenate([own, partner])
            sources = [pair] + [
                lax.ppermute(pair, "row", [(i, (i + 2 * s) % n_row) for i in range(n_row)])
                for s in range(1, n_row // 2)
            ]
            half = (owner ^ row_me) & 1
            shift = ((row_me - (owner ^ half)) % n_row) // 2
            index = (shift * 2 + half) * tiles_dev + local
        else:
            sources = [own] + [
                lax.ppermute(own, "row", [(i, (i + s) % n_row) for i in range(n_row)])
                for s in range(1, n_row)
            ]
            index = ((row_me - owner) % n_row) * tiles_dev + local
        incoming, absorbed = incoming_of(
            index,
            occupied_entries_per_strip,
            sources,
            shape_coupling_matrices,
            emitting_ability.reshape(tile_rows, tile_size),
        )
        incoming = incoming.reshape(bands_here, facets_here)

        partial_terms = emitter_terms(centre_frequency, frequency_span, facet_kelvins)
        quotient = emitting_ability / (1.0 - emitting_ability)
        packed = jnp.concatenate(
            [emitting_ability.reshape(facets_here), centre_frequency, frequency_span]
        )
        planck_parts, emitted_parts, gradient_parts = [], [], []
        for got in shifted(packed, "band", n_band):
            e_b = got[:facets_here]
            planck_b = emitter_terms(got[facets_here:facets_here + 1], got[facets_here + 1:], facet_kelvins)[0]
            planck_parts.append(planck_b)
            emitted_parts.append(e_b * planck_b)
            gradient_parts.append(e_b / (1.0 - e_b) * planck_b)
        planck_sum = order_free_sum(planck_parts)
        emitted_sum = order_free_sum(emitted_parts)
        gradient_sum = order_free_sum(gradient_parts)
        absorbed_sum = order_free_sum(shifted(absorbed, "band", n_band)).reshape(facets_here)
        energy_portion = partial_terms / planck_sum
        kelvins_third_power = facet_kelvins**3
        ideal_emitter_power = energy_portion * kelvins_third_power * facet_kelvins
        refreshed_leaving_energy = (
            emitting_ability * ideal_emitter_power + (1.0 - emitting_ability) * incoming
        )
        balance_power_density = (
            emitted_sum / planck_sum * kelvins_third_power * facet_kelvins - absorbed_sum
        )
        power_gradient = gradient_sum / planck_sum * 4.0 * kelvins_third_power
        corrected_kelvins = (
            facet_kelvins - (balance_power_density - prescribed_power_density) / power_gradient
        )
        return (corrected_kelvins, refreshed_leaving_energy)

    return on_device


def solution(mesh):
    in_specs = (
        P("row", None, None, None),
        P("row", None),
        P("row"),
        P("band", "row"),
        P("row"),
        P("band", "row"),
        P("band"),
        P("band"),
        P("row"),
    )
    out_specs = (P("row"), P("band", "row"))
    on_device = make_on_device(mesh.shape["band"], mesh.shape["row"])
    return jax.shard_map(
        on_device, mesh=mesh, in_specs=in_specs, out_specs=out_specs, check_vma=False
    )
```

```python
import jax
import jax.numpy as jnp
from jax import lax
from jax.experimental import pallas as pl
from jax.experimental.pallas import tpu as pltpu
from jax.sharding import PartitionSpec as P


def emitter_terms(centre_sample, frequency_spacing, facet_kelvins):
    return (
        frequency_spacing[:, None]
        * centre_sample[:, None] ** 3
        / jnp.expm1(centre_sample[:, None] / facet_kelvins[None, :])
    )


def shifted(x, axis, size):
    outs = [x]
    for s in range(1, size):
        outs.append(lax.ppermute(x, axis, [(i, (i + s) % size) for i in range(size)]))
    return outs


def order_free_sum(parts):
    parts = list(parts)
    n = len(parts)
    for sweep in range(n):
        for i in range(sweep % 2, n - 1, 2):
            lo = jnp.minimum(parts[i], parts[i + 1])
            hi = jnp.maximum(parts[i], parts[i + 1])
            parts[i], parts[i + 1] = lo, hi
    total = parts[0]
    for p in parts[1:]:
        total = total + p
    return total


def incoming_kernel(n_src, rows_per_step, slot_count):
    def kernel(index_ref, used_ref, *refs):
        sources = refs[:n_src]
        coupling_ref, emitting_ref, out_ref, absorbed_ref, table_ref = refs[n_src:]
        step = pl.program_id(0)
        tiles_per_src = sources[0].shape[0]

        @pl.when(step == 0)
        def _():
            for s in range(n_src):
                table_ref[pl.ds(s * tiles_per_src, tiles_per_src), :] = sources[s][...].astype(
                    jnp.float32
                )

        for rr in range(rows_per_step):
            r = step * rows_per_step + rr
            acc = jnp.zeros(coupling_ref.shape[2:], jnp.float32)
            for k in range(slot_count):
                row = table_ref[pl.ds(index_ref[r * slot_count + k], 1), :]
                row = jnp.where(k < used_ref[r], row, jnp.zeros_like(row))
                acc = acc + coupling_ref[rr, k].astype(jnp.float32) * row
            incoming = jnp.sum(acc.T, axis=0, keepdims=True)
            out_ref[pl.ds(rr, 1), :] = incoming
            absorbed_ref[pl.ds(rr, 1), :] = incoming * emitting_ref[pl.ds(rr, 1), :]

    return kernel


def incoming_of(index, used, sources, coupling, emitting):
    tile_rows, slot_count, tile_size, _ = coupling.shape
    rows_per_step = 32 if tile_rows % 32 == 0 else tile_rows
    n_src = len(sources)
    tiles_per_src = sources[0].shape[0]
    full = lambda shape: pl.BlockSpec(shape, lambda g, i, o: (0,) * len(shape))
    return pl.pallas_call(
        incoming_kernel(n_src, rows_per_step, slot_count),
        grid_spec=pltpu.PrefetchScalarGridSpec(
            num_scalar_prefetch=2,
            grid=(tile_rows // rows_per_step,),
            in_specs=[full(src.shape) for src in sources]
            + [
                pl.BlockSpec(
                    (rows_per_step, slot_count, tile_size, tile_size),
                    lambda g, i, o: (g, 0, 0, 0),
                ),
                pl.BlockSpec((rows_per_step, tile_size), lambda g, i, o: (g, 0)),
            ],
            out_specs=[
                pl.BlockSpec((rows_per_step, tile_size), lambda g, i, o: (g, 0)),
                pl.BlockSpec((rows_per_step, tile_size), lambda g, i, o: (g, 0)),
            ],
            scratch_shapes=[pltpu.VMEM((n_src * tiles_per_src, tile_size), jnp.float32)],
        ),
        out_shape=[jax.ShapeDtypeStruct((tile_rows, tile_size), jnp.float32)] * 2,
        compiler_params=pltpu.CompilerParams(dimension_semantics=("arbitrary",)),
    )(index, used, *sources, coupling, emitting)


def make_on_device(n_band, n_row):
    def on_device(
        shape_coupling_matrices,
        target_strip_index,
        occupied_entries_per_strip,
        prior_leaving_energy,
        facet_kelvins,
        emitting_ability,
        centre_frequency,
        frequency_span,
        prescribed_power_density,
    ):
        row_me = lax.axis_index("row")
        bands_here, facets_here = prior_leaving_energy.shape
        tile_rows, slot_count = target_strip_index.shape
        tile_size = shape_coupling_matrices.shape[2]
        tiles_dev = facets_here // tile_size
        entries = tile_rows * slot_count

        own = prior_leaving_energy.reshape(tiles_dev, tile_size)
        flat_cols = target_strip_index.reshape(entries)
        owner = flat_cols // tiles_dev
        local = flat_cols % tiles_dev
        if n_row % 2 == 0:
            partner = lax.ppermute(own, "row", [(i, i ^ 1) for i in range(n_row)])
            pair = jnp.concatenate([own, partner])
            sources = [pair] + [
                lax.ppermute(pair, "row", [(i, (i + 2 * s) % n_row) for i in range(n_row)])
                for s in range(1, n_row // 2)
            ]
            half = (owner ^ row_me) & 1
            shift = ((row_me - (owner ^ half)) % n_row) // 2
            index = (shift * 2 + half) * tiles_dev + local
        else:
            sources = [own] + [
                lax.ppermute(own, "row", [(i, (i + s) % n_row) for i in range(n_row)])
                for s in range(1, n_row)
            ]
            index = ((row_me - owner) % n_row) * tiles_dev + local
        incoming, absorbed = incoming_of(
            index,
            occupied_entries_per_strip,
            sources,
            shape_coupling_matrices,
            emitting_ability.reshape(tile_rows, tile_size),
        )
        incoming = incoming.reshape(bands_here, facets_here)

        partial_terms = emitter_terms(centre_frequency, frequency_span, facet_kelvins)
        quotient = emitting_ability / (1.0 - emitting_ability)
        early = order_free_sum(
            shifted(
                jnp.concatenate(
                    [partial_terms, emitting_ability * partial_terms, quotient * partial_terms]
                ),
                "band",
                n_band,
            )
        )
        planck_sum, emitted_sum, gradient_sum = early[0], early[1], early[2]
        absorbed_sum = order_free_sum(shifted(absorbed, "band", n_band)).reshape(facets_here)
        energy_portion = partial_terms / planck_sum
        kelvins_third_power = facet_kelvins**3
        ideal_emitter_power = energy_portion * kelvins_third_power * facet_kelvins
        refreshed_leaving_energy = (
            emitting_ability * ideal_emitter_power + (1.0 - emitting_ability) * incoming
        )
        emitted_less_imposed = (
            emitted_sum / planck_sum * kelvins_third_power * facet_kelvins
            - prescribed_power_density
        )
        power_gradient = gradient_sum / planck_sum * 4.0 * kelvins_third_power
        corrected_kelvins = (
            facet_kelvins - (emitted_less_imposed - absorbed_sum) / power_gradient
        )
        return (corrected_kelvins, refreshed_leaving_energy)

    return on_device


def solution(mesh):
    in_specs = (
        P("row", None, None, None),
        P("row", None),
        P("row"),
        P("band", "row"),
        P("row"),
        P("band", "row"),
        P("band"),
        P("band"),
        P("row"),
    )
    out_specs = (P("row"), P("band", "row"))
    on_device = make_on_device(mesh.shape["band"], mesh.shape["row"])
    return jax.shard_map(
        on_device, mesh=mesh, in_specs=in_specs, out_specs=out_specs, check_vma=False
    )
```

```python
import jax
import jax.numpy as jnp
from jax import lax
from jax.experimental import pallas as pl
from jax.experimental.pallas import tpu as pltpu
from jax.sharding import PartitionSpec as P


def emitter_terms(centre_sample, frequency_spacing, facet_kelvins):
    return (
        frequency_spacing[:, None]
        * centre_sample[:, None] ** 3
        / jnp.expm1(centre_sample[:, None] / facet_kelvins[None, :])
    )


def shifted(x, axis, size):
    outs = [x]
    for s in range(1, size):
        outs.append(lax.ppermute(x, axis, [(i, (i + s) % size) for i in range(size)]))
    return outs


def order_free_sum(parts):
    parts = list(parts)
    n = len(parts)
    for sweep in range(n):
        for i in range(sweep % 2, n - 1, 2):
            lo = jnp.minimum(parts[i], parts[i + 1])
            hi = jnp.maximum(parts[i], parts[i + 1])
            parts[i], parts[i + 1] = lo, hi
    total = parts[0]
    for p in parts[1:]:
        total = total + p
    return total


def incoming_kernel(n_src, slot_count):
    def kernel(index_ref, used_ref, *refs):
        sources = refs[:n_src]
        coupling_hbm, emitting_ref, out_ref, absorbed_ref, table_ref, coupling_buf, sems = refs[
            n_src:
        ]
        tile_rows = coupling_buf.shape[0]
        tiles_per_src = sources[0].shape[0]

        def copy(r, n):
            return pltpu.make_async_copy(
                coupling_hbm.at[r, pl.ds(0, n)], coupling_buf.at[r, pl.ds(0, n)], sems.at[r]
            )

        def each_used(r, act):
            for n in range(1, slot_count + 1):
                pl.when(used_ref[r] == n)(lambda n=n: act(copy(r, n)))

        def start(r, carry):
            each_used(r, lambda c: c.start())
            return carry

        lax.fori_loop(0, tile_rows, start, 0)
        for s in range(n_src):
            table_ref[pl.ds(s * tiles_per_src, tiles_per_src), :] = sources[s][...].astype(
                jnp.float32
            )

        def row_tile(r, carry):
            each_used(r, lambda c: c.wait())
            used = used_ref[r]
            acc = None
            for k in range(slot_count):
                row = table_ref[pl.ds(index_ref[r * slot_count + k], 1), :]
                term = coupling_buf[r, k].astype(jnp.float32) * row
                if k > 0:
                    term = jnp.where(k < used, term, jnp.zeros_like(term))
                acc = term if acc is None else acc + term
            incoming = jnp.sum(acc.T, axis=0, keepdims=True)
            out_ref[pl.ds(r, 1), :] = incoming
            absorbed_ref[pl.ds(r, 1), :] = incoming * emitting_ref[pl.ds(r, 1), :]
            return carry

        lax.fori_loop(0, tile_rows, row_tile, 0, unroll=4)

    return kernel


def incoming_of(index, used, sources, coupling, emitting):
    tile_rows, slot_count, tile_size, _ = coupling.shape
    n_src = len(sources)
    tiles_per_src = sources[0].shape[0]
    full = lambda shape: pl.BlockSpec(shape, lambda g, i, o: (0,) * len(shape))
    return pl.pallas_call(
        incoming_kernel(n_src, slot_count),
        grid_spec=pltpu.PrefetchScalarGridSpec(
            num_scalar_prefetch=2,
            grid=(1,),
            in_specs=[full(src.shape) for src in sources]
            + [pl.BlockSpec(memory_space=pl.ANY), full(emitting.shape)],
            out_specs=[full((tile_rows, tile_size)), full((tile_rows, tile_size))],
            scratch_shapes=[
                pltpu.VMEM((n_src * tiles_per_src, tile_size), jnp.float32),
                pltpu.VMEM(coupling.shape, coupling.dtype),
                pltpu.SemaphoreType.DMA((tile_rows,)),
            ],
        ),
        out_shape=[jax.ShapeDtypeStruct((tile_rows, tile_size), jnp.float32)] * 2,
        compiler_params=pltpu.CompilerParams(dimension_semantics=("arbitrary",)),
    )(index, used, *sources, coupling, emitting)


def make_on_device(n_band, n_row):
    def on_device(
        shape_coupling_matrices,
        target_strip_index,
        occupied_entries_per_strip,
        prior_leaving_energy,
        facet_kelvins,
        emitting_ability,
        centre_frequency,
        frequency_span,
        prescribed_power_density,
    ):
        row_me = lax.axis_index("row")
        bands_here, facets_here = prior_leaving_energy.shape
        tile_rows, slot_count = target_strip_index.shape
        tile_size = shape_coupling_matrices.shape[2]
        tiles_dev = facets_here // tile_size
        entries = tile_rows * slot_count

        own = prior_leaving_energy.reshape(tiles_dev, tile_size)
        flat_cols = target_strip_index.reshape(entries)
        owner = flat_cols // tiles_dev
        local = flat_cols % tiles_dev
        if n_row % 2 == 0:
            partner = lax.ppermute(own, "row", [(i, i ^ 1) for i in range(n_row)])
            pair = jnp.concatenate([own, partner])
            sources = [pair] + [
                lax.ppermute(pair, "row", [(i, (i + 2 * s) % n_row) for i in range(n_row)])
                for s in range(1, n_row // 2)
            ]
            half = (owner ^ row_me) & 1
            shift = ((row_me - (owner ^ half)) % n_row) // 2
            index = (shift * 2 + half) * tiles_dev + local
        else:
            sources = [own] + [
                lax.ppermute(own, "row", [(i, (i + s) % n_row) for i in range(n_row)])
                for s in range(1, n_row)
            ]
            index = ((row_me - owner) % n_row) * tiles_dev + local
        incoming, absorbed = incoming_of(
            index,
            occupied_entries_per_strip,
            sources,
            shape_coupling_matrices,
            emitting_ability.reshape(tile_rows, tile_size),
        )
        incoming = incoming.reshape(bands_here, facets_here)

        partial_terms = emitter_terms(centre_frequency, frequency_span, facet_kelvins)
        quotient = emitting_ability / (1.0 - emitting_ability)
        early = order_free_sum(
            shifted(
                jnp.concatenate(
                    [partial_terms, emitting_ability * partial_terms, quotient * partial_terms]
                ),
                "band",
                n_band,
            )
        )
        planck_sum, emitted_sum, gradient_sum = early[0], early[1], early[2]
        absorbed_sum = order_free_sum(shifted(absorbed, "band", n_band)).reshape(facets_here)
        energy_portion = partial_terms / planck_sum
        kelvins_third_power = facet_kelvins**3
        ideal_emitter_power = energy_portion * kelvins_third_power * facet_kelvins
        refreshed_leaving_energy = (
            emitting_ability * ideal_emitter_power + (1.0 - emitting_ability) * incoming
        )
        emitted_less_imposed = (
            emitted_sum / planck_sum * kelvins_third_power * facet_kelvins
            - prescribed_power_density
        )
        power_gradient = gradient_sum / planck_sum * 4.0 * kelvins_third_power
        corrected_kelvins = (
            facet_kelvins - (emitted_less_imposed - absorbed_sum) / power_gradient
        )
        return (corrected_kelvins, refreshed_leaving_energy)

    return on_device


def solution(mesh):
    in_specs = (
        P("row", None, None, None),
        P("row", None),
        P("row"),
        P("band", "row"),
        P("row"),
        P("band", "row"),
        P("band"),
        P("band"),
        P("row"),
    )
    out_specs = (P("row"), P("band", "row"))
    on_device = make_on_device(mesh.shape["band"], mesh.shape["row"])
    return jax.shard_map(
        on_device, mesh=mesh, in_specs=in_specs, out_specs=out_specs, check_vma=False
    )
```

```python
import jax
import jax.numpy as jnp
from jax import lax
from jax.experimental import pallas as pl
from jax.experimental.pallas import tpu as pltpu
from jax.sharding import PartitionSpec as P


def emitter_terms(centre_sample, frequency_spacing, facet_kelvins):
    return (
        frequency_spacing[:, None]
        * centre_sample[:, None] ** 3
        / jnp.expm1(centre_sample[:, None] / facet_kelvins[None, :])
    )


def shifted(x, axis, size):
    outs = [x]
    for s in range(1, size):
        outs.append(lax.ppermute(x, axis, [(i, (i + s) % size) for i in range(size)]))
    return outs


def order_free_sum(parts):
    parts = list(parts)
    n = len(parts)
    for sweep in range(n):
        for i in range(sweep % 2, n - 1, 2):
            lo = jnp.minimum(parts[i], parts[i + 1])
            hi = jnp.maximum(parts[i], parts[i + 1])
            parts[i], parts[i + 1] = lo, hi
    total = parts[0]
    for p in parts[1:]:
        total = total + p
    return total


def incoming_kernel(n_src, slot_count):
    def kernel(index_ref, used_ref, *refs):
        sources = refs[:n_src]
        coupling_hbm, emitting_ref, out_ref, absorbed_ref, table_ref, coupling_buf, sems = refs[
            n_src:
        ]
        tile_rows = coupling_buf.shape[0]
        tiles_per_src = sources[0].shape[0]

        def copy(r, n):
            return pltpu.make_async_copy(
                coupling_hbm.at[r, pl.ds(0, n)], coupling_buf.at[r, pl.ds(0, n)], sems.at[r]
            )

        def each_used(r, act):
            for n in range(1, slot_count + 1):
                pl.when(used_ref[r] == n)(lambda n=n: act(copy(r, n)))

        for r in range(tile_rows):
            each_used(r, lambda c: c.start())
        for s in range(n_src):
            table_ref[pl.ds(s * tiles_per_src, tiles_per_src), :] = sources[s][...].astype(
                jnp.float32
            )

        for r in range(tile_rows):
            each_used(r, lambda c: c.wait())
            used = used_ref[r]
            acc = None
            for k in range(slot_count):
                row = table_ref[pl.ds(index_ref[r * slot_count + k], 1), :]
                term = coupling_buf[r, k].astype(jnp.float32) * row
                if k > 0:
                    term = jnp.where(k < used, term, jnp.zeros_like(term))
                acc = term if acc is None else acc + term
            incoming = jnp.sum(acc.T, axis=0, keepdims=True)
            out_ref[pl.ds(r, 1), :] = incoming
            absorbed_ref[pl.ds(r, 1), :] = incoming * emitting_ref[pl.ds(r, 1), :]

    return kernel


def incoming_of(index, used, sources, coupling, emitting):
    tile_rows, slot_count, tile_size, _ = coupling.shape
    n_src = len(sources)
    tiles_per_src = sources[0].shape[0]
    full = lambda shape: pl.BlockSpec(shape, lambda g, i, o: (0,) * len(shape))
    return pl.pallas_call(
        incoming_kernel(n_src, slot_count),
        grid_spec=pltpu.PrefetchScalarGridSpec(
            num_scalar_prefetch=2,
            grid=(1,),
            in_specs=[full(src.shape) for src in sources]
            + [pl.BlockSpec(memory_space=pl.ANY), full(emitting.shape)],
            out_specs=[full((tile_rows, tile_size)), full((tile_rows, tile_size))],
            scratch_shapes=[
                pltpu.VMEM((n_src * tiles_per_src, tile_size), jnp.float32),
                pltpu.VMEM(coupling.shape, coupling.dtype),
                pltpu.SemaphoreType.DMA((tile_rows,)),
            ],
        ),
        out_shape=[jax.ShapeDtypeStruct((tile_rows, tile_size), jnp.float32)] * 2,
        compiler_params=pltpu.CompilerParams(dimension_semantics=("arbitrary",)),
    )(index, used, *sources, coupling, emitting)


def make_on_device(n_band, n_row):
    def on_device(
        shape_coupling_matrices,
        target_strip_index,
        occupied_entries_per_strip,
        prior_leaving_energy,
        facet_kelvins,
        emitting_ability,
        centre_frequency,
        frequency_span,
        prescribed_power_density,
    ):
        row_me = lax.axis_index("row")
        bands_here, facets_here = prior_leaving_energy.shape
        tile_rows, slot_count = target_strip_index.shape
        tile_size = shape_coupling_matrices.shape[2]
        tiles_dev = facets_here // tile_size
        entries = tile_rows * slot_count

        own = prior_leaving_energy.reshape(tiles_dev, tile_size)
        flat_cols = target_strip_index.reshape(entries)
        owner = flat_cols // tiles_dev
        local = flat_cols % tiles_dev
        if n_row % 2 == 0:
            partner = lax.ppermute(own, "row", [(i, i ^ 1) for i in range(n_row)])
            pair = jnp.concatenate([own, partner])
            sources = [pair] + [
                lax.ppermute(pair, "row", [(i, (i + 2 * s) % n_row) for i in range(n_row)])
                for s in range(1, n_row // 2)
            ]
            half = (owner ^ row_me) & 1
            shift = ((row_me - (owner ^ half)) % n_row) // 2
            index = (shift * 2 + half) * tiles_dev + local
        else:
            sources = [own] + [
                lax.ppermute(own, "row", [(i, (i + s) % n_row) for i in range(n_row)])
                for s in range(1, n_row)
            ]
            index = ((row_me - owner) % n_row) * tiles_dev + local
        incoming, absorbed = incoming_of(
            index,
            occupied_entries_per_strip,
            sources,
            shape_coupling_matrices,
            emitting_ability.reshape(tile_rows, tile_size),
        )
        incoming = incoming.reshape(bands_here, facets_here)

        partial_terms = emitter_terms(centre_frequency, frequency_span, facet_kelvins)
        quotient = emitting_ability / (1.0 - emitting_ability)
        early = order_free_sum(
            shifted(
                jnp.concatenate(
                    [partial_terms, emitting_ability * partial_terms, quotient * partial_terms]
                ),
                "band",
                n_band,
            )
        )
        planck_sum, emitted_sum, gradient_sum = early[0], early[1], early[2]
        absorbed_sum = order_free_sum(shifted(absorbed, "band", n_band)).reshape(facets_here)
        energy_portion = partial_terms / planck_sum
        kelvins_third_power = facet_kelvins**3
        ideal_emitter_power = energy_portion * kelvins_third_power * facet_kelvins
        refreshed_leaving_energy = (
            emitting_ability * ideal_emitter_power + (1.0 - emitting_ability) * incoming
        )
        emitted_less_imposed = (
            emitted_sum / planck_sum * kelvins_third_power * facet_kelvins
            - prescribed_power_density
        )
        power_gradient = gradient_sum / planck_sum * 4.0 * kelvins_third_power
        corrected_kelvins = (
            facet_kelvins - (emitted_less_imposed - absorbed_sum) / power_gradient
        )
        return (corrected_kelvins, refreshed_leaving_energy)

    return on_device


def solution(mesh):
    in_specs = (
        P("row", None, None, None),
        P("row", None),
        P("row"),
        P("band", "row"),
        P("row"),
        P("band", "row"),
        P("band"),
        P("band"),
        P("row"),
    )
    out_specs = (P("row"), P("band", "row"))
    on_device = make_on_device(mesh.shape["band"], mesh.shape["row"])
    return jax.shard_map(
        on_device, mesh=mesh, in_specs=in_specs, out_specs=out_specs, check_vma=False
    )
```

```python
import jax
import jax.numpy as jnp
from jax import lax
from jax.experimental import pallas as pl
from jax.experimental.pallas import tpu as pltpu
from jax.sharding import PartitionSpec as P


def emitter_terms(centre_sample, frequency_spacing, facet_kelvins):
    return (
        frequency_spacing[:, None]
        * centre_sample[:, None] ** 3
        / jnp.expm1(centre_sample[:, None] / facet_kelvins[None, :])
    )


def shifted(x, axis, size):
    outs = [x]
    for s in range(1, size):
        outs.append(lax.ppermute(x, axis, [(i, (i + s) % size) for i in range(size)]))
    return outs


def order_free_sum(parts):
    parts = list(parts)
    n = len(parts)
    for sweep in range(n):
        for i in range(sweep % 2, n - 1, 2):
            lo = jnp.minimum(parts[i], parts[i + 1])
            hi = jnp.maximum(parts[i], parts[i + 1])
            parts[i], parts[i + 1] = lo, hi
    total = parts[0]
    for p in parts[1:]:
        total = total + p
    return total


def incoming_kernel(n_src, rows_per_step, slot_count):
    def kernel(index_ref, used_ref, *refs):
        sources = refs[:n_src]
        coupling_ref, emitting_ref, out_ref, absorbed_ref, table_ref = refs[n_src:]
        step = pl.program_id(0)
        tiles_per_src = sources[0].shape[0]

        @pl.when(step == 0)
        def _():
            for s in range(n_src):
                table_ref[pl.ds(s * tiles_per_src, tiles_per_src), :] = sources[s][...].astype(
                    jnp.float32
                )

        for rr in range(rows_per_step):
            r = step * rows_per_step + rr
            acc = jnp.zeros(coupling_ref.shape[2:], jnp.float32)
            for k in range(slot_count):
                row = table_ref[pl.ds(index_ref[r * slot_count + k], 1), :]
                row = jnp.where(k < used_ref[r], row, jnp.zeros_like(row))
                acc = acc + coupling_ref[rr, k].astype(jnp.float32) * row
            incoming = jnp.sum(acc.T, axis=0, keepdims=True)
            out_ref[pl.ds(rr, 1), :] = incoming
            absorbed_ref[pl.ds(rr, 1), :] = incoming * emitting_ref[pl.ds(rr, 1), :]

    return kernel


def incoming_of(index, used, sources, coupling, emitting):
    tile_rows, slot_count, tile_size, _ = coupling.shape
    rows_per_step = 32 if tile_rows % 32 == 0 else tile_rows
    n_src = len(sources)
    tiles_per_src = sources[0].shape[0]
    full = lambda shape: pl.BlockSpec(shape, lambda g, i, o: (0,) * len(shape))
    return pl.pallas_call(
        incoming_kernel(n_src, rows_per_step, slot_count),
        grid_spec=pltpu.PrefetchScalarGridSpec(
            num_scalar_prefetch=2,
            grid=(tile_rows // rows_per_step,),
            in_specs=[full(src.shape) for src in sources]
            + [
                pl.BlockSpec(
                    (rows_per_step, slot_count, tile_size, tile_size),
                    lambda g, i, o: (g, 0, 0, 0),
                ),
                pl.BlockSpec((rows_per_step, tile_size), lambda g, i, o: (g, 0)),
            ],
            out_specs=[
                pl.BlockSpec((rows_per_step, tile_size), lambda g, i, o: (g, 0)),
                pl.BlockSpec((rows_per_step, tile_size), lambda g, i, o: (g, 0)),
            ],
            scratch_shapes=[pltpu.VMEM((n_src * tiles_per_src, tile_size), jnp.float32)],
        ),
        out_shape=[jax.ShapeDtypeStruct((tile_rows, tile_size), jnp.float32)] * 2,
        compiler_params=pltpu.CompilerParams(dimension_semantics=("arbitrary",)),
    )(index, used, *sources, coupling, emitting)


def butterfly_sum(x, axis, size):
    step = 1
    while step < size:
        x = x + lax.ppermute(x, axis, [(i, i ^ step) for i in range(size)])
        step *= 2
    return x


def make_on_device(n_band, n_row):
    def on_device(
        shape_coupling_matrices,
        target_strip_index,
        occupied_entries_per_strip,
        prior_leaving_energy,
        facet_kelvins,
        emitting_ability,
        centre_frequency,
        frequency_span,
        prescribed_power_density,
    ):
        row_me = lax.axis_index("row")
        bands_here, facets_here = prior_leaving_energy.shape
        tile_rows, slot_count = target_strip_index.shape
        tile_size = shape_coupling_matrices.shape[2]
        tiles_dev = facets_here // tile_size
        entries = tile_rows * slot_count

        own = prior_leaving_energy.reshape(tiles_dev, tile_size)
        flat_cols = target_strip_index.reshape(entries)
        owner = flat_cols // tiles_dev
        local = flat_cols % tiles_dev
        if n_row % 2 == 0:
            partner = lax.ppermute(own, "row", [(i, i ^ 1) for i in range(n_row)])
            pair = jnp.concatenate([own, partner])
            sources = [pair] + [
                lax.ppermute(pair, "row", [(i, (i + 2 * s) % n_row) for i in range(n_row)])
                for s in range(1, n_row // 2)
            ]
            half = (owner ^ row_me) & 1
            shift = ((row_me - (owner ^ half)) % n_row) // 2
            index = (shift * 2 + half) * tiles_dev + local
        else:
            sources = [own] + [
                lax.ppermute(own, "row", [(i, (i + s) % n_row) for i in range(n_row)])
                for s in range(1, n_row)
            ]
            index = ((row_me - owner) % n_row) * tiles_dev + local
        incoming, absorbed = incoming_of(
            index,
            occupied_entries_per_strip,
            sources,
            shape_coupling_matrices,
            emitting_ability.reshape(tile_rows, tile_size),
        )
        incoming = incoming.reshape(bands_here, facets_here)

        partial_terms = emitter_terms(centre_frequency, frequency_span, facet_kelvins)
        quotient = emitting_ability / (1.0 - emitting_ability)
        early_pieces = jnp.concatenate(
            [partial_terms, emitting_ability * partial_terms, quotient * partial_terms]
        )
        if n_band & (n_band - 1) == 0:
            early = butterfly_sum(early_pieces, "band", n_band)
        else:
            early = order_free_sum(shifted(early_pieces, "band", n_band))
        planck_sum, emitted_sum, gradient_sum = early[0], early[1], early[2]
        absorbed_sum = order_free_sum(shifted(absorbed, "band", n_band)).reshape(facets_here)
        energy_portion = partial_terms / planck_sum
        kelvins_third_power = facet_kelvins**3
        ideal_emitter_power = energy_portion * kelvins_third_power * facet_kelvins
        refreshed_leaving_energy = (
            emitting_ability * ideal_emitter_power + (1.0 - emitting_ability) * incoming
        )
        emitted_less_imposed = (
            emitted_sum / planck_sum * kelvins_third_power * facet_kelvins
            - prescribed_power_density
        )
        power_gradient = gradient_sum / planck_sum * 4.0 * kelvins_third_power
        corrected_kelvins = (
            facet_kelvins - (emitted_less_imposed - absorbed_sum) / power_gradient
        )
        return (corrected_kelvins, refreshed_leaving_energy)

    return on_device


def solution(mesh):
    in_specs = (
        P("row", None, None, None),
        P("row", None),
        P("row"),
        P("band", "row"),
        P("row"),
        P("band", "row"),
        P("band"),
        P("band"),
        P("row"),
    )
    out_specs = (P("row"), P("band", "row"))
    on_device = make_on_device(mesh.shape["band"], mesh.shape["row"])
    return jax.shard_map(
        on_device, mesh=mesh, in_specs=in_specs, out_specs=out_specs, check_vma=False
    )
```

```python
import jax
import jax.numpy as jnp
from jax import lax
from jax.experimental import pallas as pl
from jax.experimental.pallas import tpu as pltpu
from jax.sharding import PartitionSpec as P


def emitter_terms(centre_sample, frequency_spacing, facet_kelvins):
    return (
        frequency_spacing[:, None]
        * centre_sample[:, None] ** 3
        / jnp.expm1(centre_sample[:, None] / facet_kelvins[None, :])
    )


def shifted(x, axis, size):
    outs = [x]
    for s in range(1, size):
        outs.append(lax.ppermute(x, axis, [(i, (i + s) % size) for i in range(size)]))
    return outs


def order_free_sum(parts):
    parts = list(parts)
    n = len(parts)
    for sweep in range(n):
        for i in range(sweep % 2, n - 1, 2):
            lo = jnp.minimum(parts[i], parts[i + 1])
            hi = jnp.maximum(parts[i], parts[i + 1])
            parts[i], parts[i + 1] = lo, hi
    total = parts[0]
    for p in parts[1:]:
        total = total + p
    return total


def incoming_kernel(n_src, rows_per_step, slot_count):
    def kernel(index_ref, used_ref, *refs):
        sources = refs[:n_src]
        coupling_ref, emitting_ref, out_ref, absorbed_ref, table_ref = refs[n_src:]
        step = pl.program_id(0)
        tiles_per_src = sources[0].shape[0]

        @pl.when(step == 0)
        def _():
            for s in range(n_src):
                table_ref[pl.ds(s * tiles_per_src, tiles_per_src), :] = sources[s][...].astype(
                    jnp.float32
                )

        for rr in range(rows_per_step):
            r = step * rows_per_step + rr
            acc = jnp.zeros(coupling_ref.shape[2:], jnp.float32)
            for k in range(slot_count):
                row = table_ref[pl.ds(index_ref[r * slot_count + k], 1), :]
                row = jnp.where(k < used_ref[r], row, jnp.zeros_like(row))
                acc = acc + coupling_ref[rr, k].astype(jnp.float32) * row
            incoming = jnp.sum(acc.T, axis=0, keepdims=True)
            out_ref[pl.ds(rr, 1), :] = incoming
            absorbed_ref[pl.ds(rr, 1), :] = incoming * emitting_ref[pl.ds(rr, 1), :]

    return kernel


def incoming_of(index, used, sources, coupling, emitting):
    tile_rows, slot_count, tile_size, _ = coupling.shape
    rows_per_step = 32 if tile_rows % 32 == 0 else tile_rows
    n_src = len(sources)
    tiles_per_src = sources[0].shape[0]
    full = lambda shape: pl.BlockSpec(shape, lambda g, i, o: (0,) * len(shape))
    return pl.pallas_call(
        incoming_kernel(n_src, rows_per_step, slot_count),
        grid_spec=pltpu.PrefetchScalarGridSpec(
            num_scalar_prefetch=2,
            grid=(tile_rows // rows_per_step,),
            in_specs=[full(src.shape) for src in sources]
            + [
                pl.BlockSpec(
                    (rows_per_step, slot_count, tile_size, tile_size),
                    lambda g, i, o: (g, 0, 0, 0),
                ),
                pl.BlockSpec((rows_per_step, tile_size), lambda g, i, o: (g, 0)),
            ],
            out_specs=[
                pl.BlockSpec((rows_per_step, tile_size), lambda g, i, o: (g, 0)),
                pl.BlockSpec((rows_per_step, tile_size), lambda g, i, o: (g, 0)),
            ],
            scratch_shapes=[pltpu.VMEM((n_src * tiles_per_src, tile_size), jnp.float32)],
        ),
        out_shape=[jax.ShapeDtypeStruct((tile_rows, tile_size), jnp.float32)] * 2,
        compiler_params=pltpu.CompilerParams(dimension_semantics=("arbitrary",)),
    )(index, used, *sources, coupling, emitting)


def butterfly_sum(x, axis, size):
    step = 1
    while step < size:
        x = x + lax.ppermute(x, axis, [(i, i ^ step) for i in range(size)])
        step *= 2
    return x


def make_on_device(n_band, n_row):
    def on_device(
        shape_coupling_matrices,
        target_strip_index,
        occupied_entries_per_strip,
        prior_leaving_energy,
        facet_kelvins,
        emitting_ability,
        centre_frequency,
        frequency_span,
        prescribed_power_density,
    ):
        row_me = lax.axis_index("row")
        bands_here, facets_here = prior_leaving_energy.shape
        tile_rows, slot_count = target_strip_index.shape
        tile_size = shape_coupling_matrices.shape[2]
        tiles_dev = facets_here // tile_size
        entries = tile_rows * slot_count

        own = prior_leaving_energy.reshape(tiles_dev, tile_size)
        flat_cols = target_strip_index.reshape(entries)
        owner = flat_cols // tiles_dev
        local = flat_cols % tiles_dev
        if n_row % 2 == 0:
            partner = lax.ppermute(own, "row", [(i, i ^ 1) for i in range(n_row)])
            pair = jnp.concatenate([own, partner])
            sources = [pair] + [
                lax.ppermute(pair, "row", [(i, (i + 2 * s) % n_row) for i in range(n_row)])
                for s in range(1, n_row // 2)
            ]
            half = (owner ^ row_me) & 1
            shift = ((row_me - (owner ^ half)) % n_row) // 2
            index = (shift * 2 + half) * tiles_dev + local
        else:
            sources = [own] + [
                lax.ppermute(own, "row", [(i, (i + s) % n_row) for i in range(n_row)])
                for s in range(1, n_row)
            ]
            index = ((row_me - owner) % n_row) * tiles_dev + local
        incoming, absorbed = incoming_of(
            index,
            occupied_entries_per_strip,
            sources,
            shape_coupling_matrices,
            emitting_ability.reshape(tile_rows, tile_size),
        )
        incoming = incoming.reshape(bands_here, facets_here)

        partial_terms = emitter_terms(centre_frequency, frequency_span, facet_kelvins)
        quotient = emitting_ability / (1.0 - emitting_ability)
        early_pieces = jnp.concatenate(
            [partial_terms, emitting_ability * partial_terms, quotient * partial_terms]
        )
        if n_band & (n_band - 1) == 0:
            early = butterfly_sum(early_pieces, "band", n_band)
        else:
            early = order_free_sum(shifted(early_pieces, "band", n_band))
        planck_sum, emitted_sum, gradient_sum = early[0], early[1], early[2]
        if n_band & (n_band - 1) == 0:
            absorbed_sum = butterfly_sum(absorbed, "band", n_band).reshape(facets_here)
        else:
            absorbed_sum = order_free_sum(shifted(absorbed, "band", n_band)).reshape(facets_here)
        energy_portion = partial_terms / planck_sum
        kelvins_third_power = facet_kelvins**3
        ideal_emitter_power = energy_portion * kelvins_third_power * facet_kelvins
        refreshed_leaving_energy = (
            emitting_ability * ideal_emitter_power + (1.0 - emitting_ability) * incoming
        )
        emitted_less_imposed = (
            emitted_sum / planck_sum * kelvins_third_power * facet_kelvins
            - prescribed_power_density
        )
        power_gradient = gradient_sum / planck_sum * 4.0 * kelvins_third_power
        corrected_kelvins = (
            facet_kelvins - (emitted_less_imposed - absorbed_sum) / power_gradient
        )
        return (corrected_kelvins, refreshed_leaving_energy)

    return on_device


def solution(mesh):
    in_specs = (
        P("row", None, None, None),
        P("row", None),
        P("row"),
        P("band", "row"),
        P("row"),
        P("band", "row"),
        P("band"),
        P("band"),
        P("row"),
    )
    out_specs = (P("row"), P("band", "row"))
    on_device = make_on_device(mesh.shape["band"], mesh.shape["row"])
    return jax.shard_map(
        on_device, mesh=mesh, in_specs=in_specs, out_specs=out_specs, check_vma=False
    )
```

```python
import jax
import jax.numpy as jnp
from jax import lax
from jax.experimental import pallas as pl
from jax.experimental.pallas import tpu as pltpu
from jax.sharding import PartitionSpec as P


def emitter_terms(centre_sample, frequency_spacing, facet_kelvins):
    return (
        frequency_spacing[:, None]
        * centre_sample[:, None] ** 3
        / jnp.expm1(centre_sample[:, None] / facet_kelvins[None, :])
    )


def shifted(x, axis, size):
    outs = [x]
    for s in range(1, size):
        outs.append(lax.ppermute(x, axis, [(i, (i + s) % size) for i in range(size)]))
    return outs


def order_free_sum(parts):
    parts = list(parts)
    n = len(parts)
    for sweep in range(n):
        for i in range(sweep % 2, n - 1, 2):
            lo = jnp.minimum(parts[i], parts[i + 1])
            hi = jnp.maximum(parts[i], parts[i + 1])
            parts[i], parts[i + 1] = lo, hi
    total = parts[0]
    for p in parts[1:]:
        total = total + p
    return total


def incoming_kernel(n_src, rows_per_step, slot_count):
    def kernel(index_ref, used_ref, *refs):
        sources = refs[:n_src]
        coupling_ref, emitting_ref, out_ref, absorbed_ref, table_ref = refs[n_src:]
        step = pl.program_id(0)
        tiles_per_src = sources[0].shape[0]

        @pl.when(step == 0)
        def _():
            for s in range(n_src):
                table_ref[pl.ds(s * tiles_per_src, tiles_per_src), :] = sources[s][...].astype(
                    jnp.float32
                )

        for rr in range(rows_per_step):
            r = step * rows_per_step + rr
            acc = jnp.zeros(coupling_ref.shape[2:], jnp.float32)
            for k in range(slot_count):
                row = table_ref[pl.ds(index_ref[k, r], 1), :]
                row = jnp.where(k < used_ref[r], row, jnp.zeros_like(row))
                acc = acc + coupling_ref[rr, k].astype(jnp.float32) * row
            incoming = jnp.sum(acc.T, axis=0, keepdims=True)
            out_ref[pl.ds(rr, 1), :] = incoming
            absorbed_ref[pl.ds(rr, 1), :] = incoming * emitting_ref[pl.ds(rr, 1), :]

    return kernel


def incoming_of(index, used, sources, coupling, emitting):
    tile_rows, slot_count, tile_size, _ = coupling.shape
    rows_per_step = 32 if tile_rows % 32 == 0 else tile_rows
    n_src = len(sources)
    tiles_per_src = sources[0].shape[0]
    full = lambda shape: pl.BlockSpec(shape, lambda g, i, o: (0,) * len(shape))
    return pl.pallas_call(
        incoming_kernel(n_src, rows_per_step, slot_count),
        grid_spec=pltpu.PrefetchScalarGridSpec(
            num_scalar_prefetch=2,
            grid=(tile_rows // rows_per_step,),
            in_specs=[full(src.shape) for src in sources]
            + [
                pl.BlockSpec(
                    (rows_per_step, slot_count, tile_size, tile_size),
                    lambda g, i, o: (g, 0, 0, 0),
                ),
                pl.BlockSpec((rows_per_step, tile_size), lambda g, i, o: (g, 0)),
            ],
            out_specs=[
                pl.BlockSpec((rows_per_step, tile_size), lambda g, i, o: (g, 0)),
                pl.BlockSpec((rows_per_step, tile_size), lambda g, i, o: (g, 0)),
            ],
            scratch_shapes=[pltpu.VMEM((n_src * tiles_per_src, tile_size), jnp.float32)],
        ),
        out_shape=[jax.ShapeDtypeStruct((tile_rows, tile_size), jnp.float32)] * 2,
        compiler_params=pltpu.CompilerParams(dimension_semantics=("arbitrary",)),
    )(index, used, *sources, coupling, emitting)


def butterfly_sum(x, axis, size):
    step = 1
    while step < size:
        x = x + lax.ppermute(x, axis, [(i, i ^ step) for i in range(size)])
        step *= 2
    return x


def make_on_device(n_band, n_row):
    def on_device(
        shape_coupling_matrices,
        target_strip_index,
        occupied_entries_per_strip,
        prior_leaving_energy,
        facet_kelvins,
        emitting_ability,
        centre_frequency,
        frequency_span,
        prescribed_power_density,
    ):
        row_me = lax.axis_index("row")
        bands_here, facets_here = prior_leaving_energy.shape
        tile_rows, slot_count = target_strip_index.shape
        tile_size = shape_coupling_matrices.shape[2]
        tiles_dev = facets_here // tile_size

        own = prior_leaving_energy.reshape(tiles_dev, tile_size)
        flat_cols = target_strip_index.T
        owner = flat_cols // tiles_dev
        local = flat_cols % tiles_dev
        if n_row % 2 == 0:
            partner = lax.ppermute(own, "row", [(i, i ^ 1) for i in range(n_row)])
            pair = jnp.concatenate([own, partner])
            sources = [pair] + [
                lax.ppermute(pair, "row", [(i, (i + 2 * s) % n_row) for i in range(n_row)])
                for s in range(1, n_row // 2)
            ]
            half = (owner ^ row_me) & 1
            shift = ((row_me - (owner ^ half)) % n_row) // 2
            index = (shift * 2 + half) * tiles_dev + local
        else:
            sources = [own] + [
                lax.ppermute(own, "row", [(i, (i + s) % n_row) for i in range(n_row)])
                for s in range(1, n_row)
            ]
            index = ((row_me - owner) % n_row) * tiles_dev + local
        incoming, absorbed = incoming_of(
            index,
            occupied_entries_per_strip,
            sources,
            shape_coupling_matrices,
            emitting_ability.reshape(tile_rows, tile_size),
        )
        incoming = incoming.reshape(bands_here, facets_here)

        partial_terms = emitter_terms(centre_frequency, frequency_span, facet_kelvins)
        quotient = emitting_ability / (1.0 - emitting_ability)
        early_pieces = jnp.concatenate(
            [partial_terms, emitting_ability * partial_terms, quotient * partial_terms]
        )
        if n_band & (n_band - 1) == 0:
            early = butterfly_sum(early_pieces, "band", n_band)
        else:
            early = order_free_sum(shifted(early_pieces, "band", n_band))
        planck_sum, emitted_sum, gradient_sum = early[0], early[1], early[2]
        absorbed_sum = order_free_sum(shifted(absorbed, "band", n_band)).reshape(facets_here)
        energy_portion = partial_terms / planck_sum
        kelvins_third_power = facet_kelvins**3
        ideal_emitter_power = energy_portion * kelvins_third_power * facet_kelvins
        refreshed_leaving_energy = (
            emitting_ability * ideal_emitter_power + (1.0 - emitting_ability) * incoming
        )
        emitted_less_imposed = (
            emitted_sum / planck_sum * kelvins_third_power * facet_kelvins
            - prescribed_power_density
        )
        power_gradient = gradient_sum / planck_sum * 4.0 * kelvins_third_power
        corrected_kelvins = (
            facet_kelvins - (emitted_less_imposed - absorbed_sum) / power_gradient
        )
        return (corrected_kelvins, refreshed_leaving_energy)

    return on_device


def solution(mesh):
    in_specs = (
        P("row", None, None, None),
        P("row", None),
        P("row"),
        P("band", "row"),
        P("row"),
        P("band", "row"),
        P("band"),
        P("band"),
        P("row"),
    )
    out_specs = (P("row"), P("band", "row"))
    on_device = make_on_device(mesh.shape["band"], mesh.shape["row"])
    return jax.shard_map(
        on_device, mesh=mesh, in_specs=in_specs, out_specs=out_specs, check_vma=False
    )
```

```python
import jax
import jax.numpy as jnp
from jax import lax
from jax.experimental import pallas as pl
from jax.experimental.pallas import tpu as pltpu
from jax.sharding import PartitionSpec as P


def emitter_terms(centre_sample, frequency_spacing, facet_kelvins):
    return (
        frequency_spacing[:, None]
        * centre_sample[:, None] ** 3
        / jnp.expm1(centre_sample[:, None] / facet_kelvins[None, :])
    )


def shifted(x, axis, size):
    outs = [x]
    for s in range(1, size):
        outs.append(lax.ppermute(x, axis, [(i, (i + s) % size) for i in range(size)]))
    return outs


def order_free_sum(parts):
    parts = list(parts)
    n = len(parts)
    for sweep in range(n):
        for i in range(sweep % 2, n - 1, 2):
            lo = jnp.minimum(parts[i], parts[i + 1])
            hi = jnp.maximum(parts[i], parts[i + 1])
            parts[i], parts[i + 1] = lo, hi
    total = parts[0]
    for p in parts[1:]:
        total = total + p
    return total


def incoming_kernel(n_src, rows_per_step, slot_count, n_row, paired):
    def kernel(cols_ref, me_ref, used_ref, *refs):
        sources = refs[:n_src]
        coupling_ref, emitting_ref, out_ref, absorbed_ref, table_ref = refs[n_src:]
        step = pl.program_id(0)
        tiles_per_src = sources[0].shape[0]
        tiles_dev = tiles_per_src // 2 if paired else tiles_per_src

        def slot_row(col, me):
            owner = lax.div(col, tiles_dev)
            local = col - owner * tiles_dev
            if paired:
                half = (owner ^ me) & 1
                shift = lax.div(lax.rem(me - (owner ^ half) + n_row, n_row), 2)
                return (shift * 2 + half) * tiles_dev + local
            return lax.rem(me - owner + n_row, n_row) * tiles_dev + local

        @pl.when(step == 0)
        def _():
            for s in range(n_src):
                table_ref[pl.ds(s * tiles_per_src, tiles_per_src), :] = sources[s][...].astype(
                    jnp.float32
                )

        for rr in range(rows_per_step):
            r = step * rows_per_step + rr
            acc = jnp.zeros(coupling_ref.shape[2:], jnp.float32)
            for k in range(slot_count):
                row = table_ref[pl.ds(slot_row(cols_ref[k, r], me_ref[0]), 1), :]
                row = jnp.where(k < used_ref[r], row, jnp.zeros_like(row))
                acc = acc + coupling_ref[rr, k].astype(jnp.float32) * row
            incoming = jnp.sum(acc.T, axis=0, keepdims=True)
            out_ref[pl.ds(rr, 1), :] = incoming
            absorbed_ref[pl.ds(rr, 1), :] = incoming * emitting_ref[pl.ds(rr, 1), :]

    return kernel


def incoming_of(cols, me, used, sources, coupling, emitting, n_row, paired):
    tile_rows, slot_count, tile_size, _ = coupling.shape
    rows_per_step = 32 if tile_rows % 32 == 0 else tile_rows
    n_src = len(sources)
    tiles_per_src = sources[0].shape[0]
    full = lambda shape: pl.BlockSpec(shape, lambda g, c, m, u: (0,) * len(shape))
    return pl.pallas_call(
        incoming_kernel(n_src, rows_per_step, slot_count, n_row, paired),
        grid_spec=pltpu.PrefetchScalarGridSpec(
            num_scalar_prefetch=3,
            grid=(tile_rows // rows_per_step,),
            in_specs=[full(src.shape) for src in sources]
            + [
                pl.BlockSpec(
                    (rows_per_step, slot_count, tile_size, tile_size),
                    lambda g, c, m, u: (g, 0, 0, 0),
                ),
                pl.BlockSpec((rows_per_step, tile_size), lambda g, c, m, u: (g, 0)),
            ],
            out_specs=[
                pl.BlockSpec((rows_per_step, tile_size), lambda g, c, m, u: (g, 0)),
                pl.BlockSpec((rows_per_step, tile_size), lambda g, c, m, u: (g, 0)),
            ],
            scratch_shapes=[pltpu.VMEM((n_src * tiles_per_src, tile_size), jnp.float32)],
        ),
        out_shape=[jax.ShapeDtypeStruct((tile_rows, tile_size), jnp.float32)] * 2,
        compiler_params=pltpu.CompilerParams(dimension_semantics=("arbitrary",)),
    )(cols, me, used, *sources, coupling, emitting)


def butterfly_sum(x, axis, size):
    step = 1
    while step < size:
        x = x + lax.ppermute(x, axis, [(i, i ^ step) for i in range(size)])
        step *= 2
    return x


def make_on_device(n_band, n_row):
    def on_device(
        shape_coupling_matrices,
        target_strip_index,
        occupied_entries_per_strip,
        prior_leaving_energy,
        facet_kelvins,
        emitting_ability,
        centre_frequency,
        frequency_span,
        prescribed_power_density,
    ):
        row_me = lax.axis_index("row")
        bands_here, facets_here = prior_leaving_energy.shape
        tile_rows, slot_count = target_strip_index.shape
        tile_size = shape_coupling_matrices.shape[2]
        tiles_dev = facets_here // tile_size

        own = prior_leaving_energy.reshape(tiles_dev, tile_size)
        paired = n_row % 2 == 0
        if paired:
            partner = lax.ppermute(own, "row", [(i, i ^ 1) for i in range(n_row)])
            pair = jnp.concatenate([own, partner])
            sources = [pair] + [
                lax.ppermute(pair, "row", [(i, (i + 2 * s) % n_row) for i in range(n_row)])
                for s in range(1, n_row // 2)
            ]
        else:
            sources = [own] + [
                lax.ppermute(own, "row", [(i, (i + s) % n_row) for i in range(n_row)])
                for s in range(1, n_row)
            ]
        incoming, absorbed = incoming_of(
            target_strip_index.T,
            jnp.reshape(row_me, (1,)).astype(jnp.int32),
            occupied_entries_per_strip,
            sources,
            shape_coupling_matrices,
            emitting_ability.reshape(tile_rows, tile_size),
            n_row,
            paired,
        )
        incoming = incoming.reshape(bands_here, facets_here)

        partial_terms = emitter_terms(centre_frequency, frequency_span, facet_kelvins)
        quotient = emitting_ability / (1.0 - emitting_ability)
        early_pieces = jnp.concatenate(
            [partial_terms, emitting_ability * partial_terms, quotient * partial_terms]
        )
        if n_band & (n_band - 1) == 0:
            early = butterfly_sum(early_pieces, "band", n_band)
        else:
            early = order_free_sum(shifted(early_pieces, "band", n_band))
        planck_sum, emitted_sum, gradient_sum = early[0], early[1], early[2]
        absorbed_sum = order_free_sum(shifted(absorbed, "band", n_band)).reshape(facets_here)
        energy_portion = partial_terms / planck_sum
        kelvins_third_power = facet_kelvins**3
        ideal_emitter_power = energy_portion * kelvins_third_power * facet_kelvins
        refreshed_leaving_energy = (
            emitting_ability * ideal_emitter_power + (1.0 - emitting_ability) * incoming
        )
        emitted_less_imposed = (
            emitted_sum / planck_sum * kelvins_third_power * facet_kelvins
            - prescribed_power_density
        )
        power_gradient = gradient_sum / planck_sum * 4.0 * kelvins_third_power
        corrected_kelvins = (
            facet_kelvins - (emitted_less_imposed - absorbed_sum) / power_gradient
        )
        return (corrected_kelvins, refreshed_leaving_energy)

    return on_device


def solution(mesh):
    in_specs = (
        P("row", None, None, None),
        P("row", None),
        P("row"),
        P("band", "row"),
        P("row"),
        P("band", "row"),
        P("band"),
        P("band"),
        P("row"),
    )
    out_specs = (P("row"), P("band", "row"))
    on_device = make_on_device(mesh.shape["band"], mesh.shape["row"])
    return jax.shard_map(
        on_device, mesh=mesh, in_specs=in_specs, out_specs=out_specs, check_vma=False
    )
```

```python
import jax
import jax.numpy as jnp
from jax import lax
from jax.experimental import pallas as pl
from jax.experimental.pallas import tpu as pltpu
from jax.sharding import PartitionSpec as P


def emitter_terms(centre_sample, frequency_spacing, facet_kelvins):
    return (
        frequency_spacing[:, None]
        * centre_sample[:, None] ** 3
        / jnp.expm1(centre_sample[:, None] / facet_kelvins[None, :])
    )


def shifted(x, axis, size):
    outs = [x]
    for s in range(1, size):
        outs.append(lax.ppermute(x, axis, [(i, (i + s) % size) for i in range(size)]))
    return outs


def order_free_sum(parts):
    parts = list(parts)
    n = len(parts)
    for sweep in range(n):
        for i in range(sweep % 2, n - 1, 2):
            lo = jnp.minimum(parts[i], parts[i + 1])
            hi = jnp.maximum(parts[i], parts[i + 1])
            parts[i], parts[i + 1] = lo, hi
    total = parts[0]
    for p in parts[1:]:
        total = total + p
    return total


def incoming_kernel(n_src, rows_per_step, slot_count):
    def kernel(index_ref, used_ref, *refs):
        sources = refs[:n_src]
        coupling_ref, emitting_ref, out_ref, absorbed_ref, table_ref = refs[n_src:]
        step = pl.program_id(0)
        tiles_per_src = sources[0].shape[0]

        @pl.when(step == 0)
        def _():
            for s in range(n_src):
                table_ref[pl.ds(s * tiles_per_src, tiles_per_src), :] = sources[s][...].astype(
                    jnp.float32
                )

        for rr in range(rows_per_step):
            r = step * rows_per_step + rr
            acc = jnp.zeros(coupling_ref.shape[2:], jnp.float32)
            for k in range(slot_count):
                row = table_ref[pl.ds(index_ref[k, r], 1), :]
                row = jnp.where(k < used_ref[r], row, jnp.zeros_like(row))
                acc = acc + coupling_ref[rr, k].astype(jnp.float32) * row
            incoming = jnp.sum(acc.T, axis=0, keepdims=True)
            out_ref[pl.ds(rr, 1), :] = incoming
            absorbed_ref[pl.ds(rr, 1), :] = incoming * emitting_ref[pl.ds(rr, 1), :]

    return kernel


def incoming_of(index, used, sources, coupling, emitting):
    tile_rows, slot_count, tile_size, _ = coupling.shape
    rows_per_step = 32 if tile_rows % 32 == 0 else tile_rows
    n_src = len(sources)
    tiles_per_src = sources[0].shape[0]
    full = lambda shape: pl.BlockSpec(shape, lambda g, i, o: (0,) * len(shape))
    return pl.pallas_call(
        incoming_kernel(n_src, rows_per_step, slot_count),
        grid_spec=pltpu.PrefetchScalarGridSpec(
            num_scalar_prefetch=2,
            grid=(tile_rows // rows_per_step,),
            in_specs=[full(src.shape) for src in sources]
            + [
                pl.BlockSpec(
                    (rows_per_step, slot_count, tile_size, tile_size),
                    lambda g, i, o: (g, 0, 0, 0),
                ),
                pl.BlockSpec((rows_per_step, tile_size), lambda g, i, o: (g, 0)),
            ],
            out_specs=[
                pl.BlockSpec((rows_per_step, tile_size), lambda g, i, o: (g, 0)),
                pl.BlockSpec((rows_per_step, tile_size), lambda g, i, o: (g, 0)),
            ],
            scratch_shapes=[pltpu.VMEM((n_src * tiles_per_src, tile_size), jnp.float32)],
        ),
        out_shape=[jax.ShapeDtypeStruct((tile_rows, tile_size), jnp.float32)] * 2,
        compiler_params=pltpu.CompilerParams(dimension_semantics=("arbitrary",)),
    )(index, used, *sources, coupling, emitting)


def butterfly_sum(x, axis, size):
    step = 1
    while step < size:
        x = x + lax.ppermute(x, axis, [(i, i ^ step) for i in range(size)])
        step *= 2
    return x


def make_on_device(n_band, n_row):
    def on_device(
        shape_coupling_matrices,
        target_strip_index,
        occupied_entries_per_strip,
        prior_leaving_energy,
        facet_kelvins,
        emitting_ability,
        centre_frequency,
        frequency_span,
        prescribed_power_density,
    ):
        row_me = lax.axis_index("row")
        bands_here, facets_here = prior_leaving_energy.shape
        tile_rows, slot_count = target_strip_index.shape
        tile_size = shape_coupling_matrices.shape[2]
        tiles_dev = facets_here // tile_size

        own = prior_leaving_energy.reshape(tiles_dev, tile_size)
        flat_cols = target_strip_index.T
        if tiles_dev & (tiles_dev - 1) == 0:
            owner = flat_cols >> (tiles_dev.bit_length() - 1)
            local = flat_cols & (tiles_dev - 1)
        else:
            owner = flat_cols // tiles_dev
            local = flat_cols - owner * tiles_dev
        if n_row % 2 == 0:
            partner = lax.ppermute(own, "row", [(i, i ^ 1) for i in range(n_row)])
            pair = jnp.concatenate([own, partner])
            sources = [pair] + [
                lax.ppermute(pair, "row", [(i, (i + 2 * s) % n_row) for i in range(n_row)])
                for s in range(1, n_row // 2)
            ]
            half = (owner ^ row_me) & 1
            back = row_me - (owner ^ half)
            shift = jnp.where(back < 0, back + n_row, back) >> 1
            index = (shift * 2 + half) * tiles_dev + local
        else:
            sources = [own] + [
                lax.ppermute(own, "row", [(i, (i + s) % n_row) for i in range(n_row)])
                for s in range(1, n_row)
            ]
            back = row_me - owner
            index = jnp.where(back < 0, back + n_row, back) * tiles_dev + local
        incoming, absorbed = incoming_of(
            index,
            occupied_entries_per_strip,
            sources,
            shape_coupling_matrices,
            emitting_ability.reshape(tile_rows, tile_size),
        )
        incoming = incoming.reshape(bands_here, facets_here)

        partial_terms = emitter_terms(centre_frequency, frequency_span, facet_kelvins)
        quotient = emitting_ability / (1.0 - emitting_ability)
        early_pieces = jnp.concatenate(
            [partial_terms, emitting_ability * partial_terms, quotient * partial_terms]
        )
        if n_band & (n_band - 1) == 0:
            early = butterfly_sum(early_pieces, "band", n_band)
        else:
            early = order_free_sum(shifted(early_pieces, "band", n_band))
        planck_sum, emitted_sum, gradient_sum = early[0], early[1], early[2]
        absorbed_sum = order_free_sum(shifted(absorbed, "band", n_band)).reshape(facets_here)
        energy_portion = partial_terms / planck_sum
        kelvins_third_power = facet_kelvins**3
        ideal_emitter_power = energy_portion * kelvins_third_power * facet_kelvins
        refreshed_leaving_energy = (
            emitting_ability * ideal_emitter_power + (1.0 - emitting_ability) * incoming
        )
        emitted_less_imposed = (
            emitted_sum / planck_sum * kelvins_third_power * facet_kelvins
            - prescribed_power_density
        )
        power_gradient = gradient_sum / planck_sum * 4.0 * kelvins_third_power
        corrected_kelvins = (
            facet_kelvins - (emitted_less_imposed - absorbed_sum) / power_gradient
        )
        return (corrected_kelvins, refreshed_leaving_energy)

    return on_device


def solution(mesh):
    in_specs = (
        P("row", None, None, None),
        P("row", None),
        P("row"),
        P("band", "row"),
        P("row"),
        P("band", "row"),
        P("band"),
        P("band"),
        P("row"),
    )
    out_specs = (P("row"), P("band", "row"))
    on_device = make_on_device(mesh.shape["band"], mesh.shape["row"])
    return jax.shard_map(
        on_device, mesh=mesh, in_specs=in_specs, out_specs=out_specs, check_vma=False
    )
```

```python
import jax
import jax.numpy as jnp
from jax import lax
from jax.experimental import pallas as pl
from jax.experimental.pallas import tpu as pltpu
from jax.sharding import PartitionSpec as P


def emitter_terms(centre_sample, frequency_spacing, facet_kelvins):
    return (
        frequency_spacing[:, None]
        * centre_sample[:, None] ** 3
        / jnp.expm1(centre_sample[:, None] / facet_kelvins[None, :])
    )


def shifted(x, axis, size):
    outs = [x]
    for s in range(1, size):
        outs.append(lax.ppermute(x, axis, [(i, (i + s) % size) for i in range(size)]))
    return outs


def order_free_sum(parts):
    parts = list(parts)
    n = len(parts)
    for sweep in range(n):
        for i in range(sweep % 2, n - 1, 2):
            lo = jnp.minimum(parts[i], parts[i + 1])
            hi = jnp.maximum(parts[i], parts[i + 1])
            parts[i], parts[i + 1] = lo, hi
    total = parts[0]
    for p in parts[1:]:
        total = total + p
    return total


def incoming_kernel(n_src, rows_per_step, slot_count):
    def kernel(index_ref, used_ref, *refs):
        sources = refs[:n_src]
        coupling_ref, emitting_ref, out_ref, absorbed_ref, table_ref = refs[n_src:]
        step = pl.program_id(0)
        tiles_per_src = sources[0].shape[0]

        @pl.when(step == 0)
        def _():
            for s in range(n_src):
                table_ref[pl.ds(s * tiles_per_src, tiles_per_src), :] = sources[s][...].astype(
                    jnp.float32
                )

        for rr in range(rows_per_step):
            r = step * rows_per_step + rr
            acc = jnp.zeros(coupling_ref.shape[2:], jnp.float32)
            for k in range(slot_count):
                row = table_ref[pl.ds(index_ref[k, r], 1), :]
                row = jnp.where(k < used_ref[r], row, jnp.zeros_like(row))
                acc = acc + coupling_ref[rr, k].astype(jnp.float32) * row
            incoming = jnp.sum(acc.T, axis=0, keepdims=True)
            out_ref[pl.ds(rr, 1), :] = incoming
            absorbed_ref[pl.ds(rr, 1), :] = incoming * emitting_ref[pl.ds(rr, 1), :]

    return kernel


def incoming_of(index, used, sources, coupling, emitting):
    tile_rows, slot_count, tile_size, _ = coupling.shape
    rows_per_step = 32 if tile_rows % 32 == 0 else tile_rows
    n_src = len(sources)
    tiles_per_src = sources[0].shape[0]
    full = lambda shape: pl.BlockSpec(shape, lambda g, i, o: (0,) * len(shape))
    return pl.pallas_call(
        incoming_kernel(n_src, rows_per_step, slot_count),
        grid_spec=pltpu.PrefetchScalarGridSpec(
            num_scalar_prefetch=2,
            grid=(tile_rows // rows_per_step,),
            in_specs=[full(src.shape) for src in sources]
            + [
                pl.BlockSpec(
                    (rows_per_step, slot_count, tile_size, tile_size),
                    lambda g, i, o: (g, 0, 0, 0),
                ),
                pl.BlockSpec((rows_per_step, tile_size), lambda g, i, o: (g, 0)),
            ],
            out_specs=[
                pl.BlockSpec((rows_per_step, tile_size), lambda g, i, o: (g, 0)),
                pl.BlockSpec((rows_per_step, tile_size), lambda g, i, o: (g, 0)),
            ],
            scratch_shapes=[pltpu.VMEM((n_src * tiles_per_src, tile_size), jnp.float32)],
        ),
        out_shape=[jax.ShapeDtypeStruct((tile_rows, tile_size), jnp.float32)] * 2,
        compiler_params=pltpu.CompilerParams(dimension_semantics=("arbitrary",)),
    )(index, used, *sources, coupling, emitting)


def butterfly_sum(x, axis, size):
    step = 1
    while step < size:
        x = x + lax.ppermute(x, axis, [(i, i ^ step) for i in range(size)])
        step *= 2
    return x


def make_on_device(n_band, n_row):
    def on_device(
        shape_coupling_matrices,
        target_strip_index,
        occupied_entries_per_strip,
        prior_leaving_energy,
        facet_kelvins,
        emitting_ability,
        centre_frequency,
        frequency_span,
        prescribed_power_density,
    ):
        row_me = lax.axis_index("row")
        bands_here, facets_here = prior_leaving_energy.shape
        tile_rows, slot_count = target_strip_index.shape
        tile_size = shape_coupling_matrices.shape[2]
        tiles_dev = facets_here // tile_size

        partial_terms = emitter_terms(centre_frequency, frequency_span, facet_kelvins)
        quotient = emitting_ability / (1.0 - emitting_ability)
        early_pieces = jnp.concatenate(
            [partial_terms, emitting_ability * partial_terms, quotient * partial_terms]
        )
        own = prior_leaving_energy.reshape(tiles_dev, tile_size)
        flat_cols = target_strip_index.T
        owner = flat_cols // tiles_dev
        local = flat_cols % tiles_dev
        paired = n_row % 2 == 0
        if paired:
            half = (owner ^ row_me) & 1
            shift = ((row_me - (owner ^ half)) % n_row) // 2
            index = (shift * 2 + half) * tiles_dev + local
        else:
            index = ((row_me - owner) % n_row) * tiles_dev + local
        own, index, early_pieces = lax.optimization_barrier((own, index, early_pieces))
        if paired:
            partner = lax.ppermute(own, "row", [(i, i ^ 1) for i in range(n_row)])
            pair = jnp.concatenate([own, partner])
            sources = [pair] + [
                lax.ppermute(pair, "row", [(i, (i + 2 * s) % n_row) for i in range(n_row)])
                for s in range(1, n_row // 2)
            ]
        else:
            sources = [own] + [
                lax.ppermute(own, "row", [(i, (i + s) % n_row) for i in range(n_row)])
                for s in range(1, n_row)
            ]
        incoming, absorbed = incoming_of(
            index,
            occupied_entries_per_strip,
            sources,
            shape_coupling_matrices,
            emitting_ability.reshape(tile_rows, tile_size),
        )
        incoming = incoming.reshape(bands_here, facets_here)

        if n_band & (n_band - 1) == 0:
            early = butterfly_sum(early_pieces, "band", n_band)
        else:
            early = order_free_sum(shifted(early_pieces, "band", n_band))
        planck_sum, emitted_sum, gradient_sum = early[0], early[1], early[2]
        absorbed_sum = order_free_sum(shifted(absorbed, "band", n_band)).reshape(facets_here)
        energy_portion = partial_terms / planck_sum
        kelvins_third_power = facet_kelvins**3
        ideal_emitter_power = energy_portion * kelvins_third_power * facet_kelvins
        refreshed_leaving_energy = (
            emitting_ability * ideal_emitter_power + (1.0 - emitting_ability) * incoming
        )
        emitted_less_imposed = (
            emitted_sum / planck_sum * kelvins_third_power * facet_kelvins
            - prescribed_power_density
        )
        power_gradient = gradient_sum / planck_sum * 4.0 * kelvins_third_power
        corrected_kelvins = (
            facet_kelvins - (emitted_less_imposed - absorbed_sum) / power_gradient
        )
        return (corrected_kelvins, refreshed_leaving_energy)

    return on_device


def solution(mesh):
    in_specs = (
        P("row", None, None, None),
        P("row", None),
        P("row"),
        P("band", "row"),
        P("row"),
        P("band", "row"),
        P("band"),
        P("band"),
        P("row"),
    )
    out_specs = (P("row"), P("band", "row"))
    on_device = make_on_device(mesh.shape["band"], mesh.shape["row"])
    return jax.shard_map(
        on_device, mesh=mesh, in_specs=in_specs, out_specs=out_specs, check_vma=False
    )
```

```python
import jax
import jax.numpy as jnp
from jax import lax
from jax.experimental import pallas as pl
from jax.experimental.pallas import tpu as pltpu
from jax.sharding import PartitionSpec as P


def emitter_terms(centre_sample, frequency_spacing, facet_kelvins):
    return (
        frequency_spacing[:, None]
        * centre_sample[:, None] ** 3
        / jnp.expm1(centre_sample[:, None] / facet_kelvins[None, :])
    )


def shifted(x, axis, size):
    outs = [x]
    for s in range(1, size):
        outs.append(lax.ppermute(x, axis, [(i, (i + s) % size) for i in range(size)]))
    return outs


def order_free_sum(parts):
    parts = list(parts)
    n = len(parts)
    for sweep in range(n):
        for i in range(sweep % 2, n - 1, 2):
            lo = jnp.minimum(parts[i], parts[i + 1])
            hi = jnp.maximum(parts[i], parts[i + 1])
            parts[i], parts[i + 1] = lo, hi
    total = parts[0]
    for p in parts[1:]:
        total = total + p
    return total


def chunk_bounds(tile_rows):
    first = min(8, tile_rows)
    rest = tile_rows - first
    bounds = [0, first]
    for c in range(1, 4):
        bounds.append(first + rest * c // 3)
    return sorted(set(bounds))


def incoming_kernel(n_src, slot_count, bounds):
    def kernel(index_ref, used_ref, *refs):
        sources = refs[:n_src]
        coupling_hbm, emitting_ref, out_ref, absorbed_ref, table_ref, coupling_buf, sems = refs[
            n_src:
        ]
        tiles_per_src = sources[0].shape[0]
        copies = [
            pltpu.make_async_copy(
                coupling_hbm.at[pl.ds(lo, hi - lo)], coupling_buf.at[pl.ds(lo, hi - lo)], sems.at[c]
            )
            for c, (lo, hi) in enumerate(zip(bounds[:-1], bounds[1:]))
        ]
        for cp in copies:
            cp.start()
        for s in range(n_src):
            table_ref[pl.ds(s * tiles_per_src, tiles_per_src), :] = sources[s][...].astype(
                jnp.float32
            )
        for c, (lo, hi) in enumerate(zip(bounds[:-1], bounds[1:])):
            copies[c].wait()
            for r in range(lo, hi):
                acc = jnp.zeros(coupling_buf.shape[2:], jnp.float32)
                for k in range(slot_count):
                    row = table_ref[pl.ds(index_ref[k, r], 1), :]
                    row = jnp.where(k < used_ref[r], row, jnp.zeros_like(row))
                    acc = acc + coupling_buf[r, k].astype(jnp.float32) * row
                incoming = jnp.sum(acc.T, axis=0, keepdims=True)
                out_ref[pl.ds(r, 1), :] = incoming
                absorbed_ref[pl.ds(r, 1), :] = incoming * emitting_ref[pl.ds(r, 1), :]

    return kernel


def incoming_of(index, used, sources, coupling, emitting):
    tile_rows, slot_count, tile_size, _ = coupling.shape
    n_src = len(sources)
    tiles_per_src = sources[0].shape[0]
    bounds = chunk_bounds(tile_rows)
    full = lambda shape: pl.BlockSpec(shape, lambda g, i, o: (0,) * len(shape))
    return pl.pallas_call(
        incoming_kernel(n_src, slot_count, bounds),
        grid_spec=pltpu.PrefetchScalarGridSpec(
            num_scalar_prefetch=2,
            grid=(1,),
            in_specs=[full(src.shape) for src in sources]
            + [pl.BlockSpec(memory_space=pl.ANY), full(emitting.shape)],
            out_specs=[full((tile_rows, tile_size)), full((tile_rows, tile_size))],
            scratch_shapes=[
                pltpu.VMEM((n_src * tiles_per_src, tile_size), jnp.float32),
                pltpu.VMEM(coupling.shape, coupling.dtype),
                pltpu.SemaphoreType.DMA((len(bounds) - 1,)),
            ],
        ),
        out_shape=[jax.ShapeDtypeStruct((tile_rows, tile_size), jnp.float32)] * 2,
        compiler_params=pltpu.CompilerParams(dimension_semantics=("arbitrary",)),
    )(index, used, *sources, coupling, emitting)


def butterfly_sum(x, axis, size):
    step = 1
    while step < size:
        x = x + lax.ppermute(x, axis, [(i, i ^ step) for i in range(size)])
        step *= 2
    return x


def make_on_device(n_band, n_row):
    def on_device(
        shape_coupling_matrices,
        target_strip_index,
        occupied_entries_per_strip,
        prior_leaving_energy,
        facet_kelvins,
        emitting_ability,
        centre_frequency,
        frequency_span,
        prescribed_power_density,
    ):
        row_me = lax.axis_index("row")
        bands_here, facets_here = prior_leaving_energy.shape
        tile_rows, slot_count = target_strip_index.shape
        tile_size = shape_coupling_matrices.shape[2]
        tiles_dev = facets_here // tile_size

        own = prior_leaving_energy.reshape(tiles_dev, tile_size)
        flat_cols = target_strip_index.T
        owner = flat_cols // tiles_dev
        local = flat_cols % tiles_dev
        if n_row % 2 == 0:
            partner = lax.ppermute(own, "row", [(i, i ^ 1) for i in range(n_row)])
            pair = jnp.concatenate([own, partner])
            sources = [pair] + [
                lax.ppermute(pair, "row", [(i, (i + 2 * s) % n_row) for i in range(n_row)])
                for s in range(1, n_row // 2)
            ]
            half = (owner ^ row_me) & 1
            shift = ((row_me - (owner ^ half)) % n_row) // 2
            index = (shift * 2 + half) * tiles_dev + local
        else:
            sources = [own] + [
                lax.ppermute(own, "row", [(i, (i + s) % n_row) for i in range(n_row)])
                for s in range(1, n_row)
            ]
            index = ((row_me - owner) % n_row) * tiles_dev + local
        incoming, absorbed = incoming_of(
            index,
            occupied_entries_per_strip,
            sources,
            shape_coupling_matrices,
            emitting_ability.reshape(tile_rows, tile_size),
        )
        incoming = incoming.reshape(bands_here, facets_here)

        partial_terms = emitter_terms(centre_frequency, frequency_span, facet_kelvins)
        quotient = emitting_ability / (1.0 - emitting_ability)
        early_pieces = jnp.concatenate(
            [partial_terms, emitting_ability * partial_terms, quotient * partial_terms]
        )
        if n_band & (n_band - 1) == 0:
            early = butterfly_sum(early_pieces, "band", n_band)
        else:
            early = order_free_sum(shifted(early_pieces, "band", n_band))
        planck_sum, emitted_sum, gradient_sum = early[0], early[1], early[2]
        absorbed_sum = order_free_sum(shifted(absorbed, "band", n_band)).reshape(facets_here)
        energy_portion = partial_terms / planck_sum
        kelvins_third_power = facet_kelvins**3
        ideal_emitter_power = energy_portion * kelvins_third_power * facet_kelvins
        refreshed_leaving_energy = (
            emitting_ability * ideal_emitter_power + (1.0 - emitting_ability) * incoming
        )
        emitted_less_imposed = (
            emitted_sum / planck_sum * kelvins_third_power * facet_kelvins
            - prescribed_power_density
        )
        power_gradient = gradient_sum / planck_sum * 4.0 * kelvins_third_power
        corrected_kelvins = (
            facet_kelvins - (emitted_less_imposed - absorbed_sum) / power_gradient
        )
        return (corrected_kelvins, refreshed_leaving_energy)

    return on_device


def solution(mesh):
    in_specs = (
        P("row", None, None, None),
        P("row", None),
        P("row"),
        P("band", "row"),
        P("row"),
        P("band", "row"),
        P("band"),
        P("band"),
        P("row"),
    )
    out_specs = (P("row"), P("band", "row"))
    on_device = make_on_device(mesh.shape["band"], mesh.shape["row"])
    return jax.shard_map(
        on_device, mesh=mesh, in_specs=in_specs, out_specs=out_specs, check_vma=False
    )
```

```python
import jax
import jax.numpy as jnp
from jax import lax
from jax.experimental import pallas as pl
from jax.experimental.pallas import tpu as pltpu
from jax.sharding import PartitionSpec as P


def emitter_terms(centre_sample, frequency_spacing, facet_kelvins):
    return (
        frequency_spacing[:, None]
        * centre_sample[:, None] ** 3
        / jnp.expm1(centre_sample[:, None] / facet_kelvins[None, :])
    )


def shifted(x, axis, size):
    outs = [x]
    for s in range(1, size):
        outs.append(lax.ppermute(x, axis, [(i, (i + s) % size) for i in range(size)]))
    return outs


def order_free_sum(parts):
    parts = list(parts)
    n = len(parts)
    for sweep in range(n):
        for i in range(sweep % 2, n - 1, 2):
            lo = jnp.minimum(parts[i], parts[i + 1])
            hi = jnp.maximum(parts[i], parts[i + 1])
            parts[i], parts[i + 1] = lo, hi
    total = parts[0]
    for p in parts[1:]:
        total = total + p
    return total


def incoming_kernel(n_src, rows_per_step, slot_count):
    def kernel(index_ref, used_ref, *refs):
        sources = refs[:n_src]
        coupling_ref, emitting_ref, out_ref, absorbed_ref, table_ref = refs[n_src:]
        step = pl.program_id(0)
        tiles_per_src = sources[0].shape[0]

        @pl.when(step == 0)
        def _():
            for s in range(n_src):
                table_ref[pl.ds(s * tiles_per_src, tiles_per_src), :] = sources[s][...].astype(
                    jnp.float32
                )

        for rr in range(rows_per_step):
            r = step * rows_per_step + rr
            acc = jnp.zeros(coupling_ref.shape[2:], jnp.float32)
            for k in range(slot_count):
                row = table_ref[pl.ds(index_ref[k, r], 1), :]
                row = jnp.where(k < used_ref[r], row, jnp.zeros_like(row))
                acc = acc + coupling_ref[rr, k].astype(jnp.float32) * row
            incoming = jnp.sum(acc.T, axis=0, keepdims=True)
            out_ref[pl.ds(rr, 1), :] = incoming
            absorbed_ref[pl.ds(rr, 1), :] = incoming * emitting_ref[pl.ds(rr, 1), :]

    return kernel


def incoming_of(index, used, sources, coupling, emitting):
    tile_rows, slot_count, tile_size, _ = coupling.shape
    rows_per_step = 32 if tile_rows % 32 == 0 else tile_rows
    n_src = len(sources)
    tiles_per_src = sources[0].shape[0]
    full = lambda shape: pl.BlockSpec(shape, lambda g, i, o: (0,) * len(shape))
    return pl.pallas_call(
        incoming_kernel(n_src, rows_per_step, slot_count),
        grid_spec=pltpu.PrefetchScalarGridSpec(
            num_scalar_prefetch=2,
            grid=(tile_rows // rows_per_step,),
            in_specs=[full(src.shape) for src in sources]
            + [
                pl.BlockSpec(
                    (rows_per_step, slot_count, tile_size, tile_size),
                    lambda g, i, o: (g, 0, 0, 0),
                ),
                pl.BlockSpec((rows_per_step, tile_size), lambda g, i, o: (g, 0)),
            ],
            out_specs=[
                pl.BlockSpec((rows_per_step, tile_size), lambda g, i, o: (g, 0)),
                pl.BlockSpec((rows_per_step, tile_size), lambda g, i, o: (g, 0)),
            ],
            scratch_shapes=[pltpu.VMEM((n_src * tiles_per_src, tile_size), jnp.float32)],
        ),
        out_shape=[jax.ShapeDtypeStruct((tile_rows, tile_size), jnp.float32)] * 2,
        compiler_params=pltpu.CompilerParams(dimension_semantics=("arbitrary",)),
    )(index, used, *sources, coupling, emitting)


def butterfly_sum(x, axis, size):
    step = 1
    while step < size:
        x = x + lax.ppermute(x, axis, [(i, i ^ step) for i in range(size)])
        step *= 2
    return x


def make_on_device(n_band, n_row):
    def on_device(
        shape_coupling_matrices,
        target_strip_index,
        occupied_entries_per_strip,
        prior_leaving_energy,
        facet_kelvins,
        emitting_ability,
        centre_frequency,
        frequency_span,
        prescribed_power_density,
    ):
        row_me = lax.axis_index("row")
        bands_here, facets_here = prior_leaving_energy.shape
        tile_rows, slot_count = target_strip_index.shape
        tile_size = shape_coupling_matrices.shape[2]
        tiles_dev = facets_here // tile_size

        own = prior_leaving_energy.reshape(tiles_dev, tile_size)
        flat_cols = target_strip_index.T
        owner = flat_cols // tiles_dev
        local = flat_cols % tiles_dev
        if n_row % 2 == 0:
            partner = lax.ppermute(prior_leaving_energy, "row", [(i, i ^ 1) for i in range(n_row)])
            pair = jnp.concatenate([own, partner.reshape(tiles_dev, tile_size)])
            sources = [pair] + [
                lax.ppermute(pair, "row", [(i, (i + 2 * s) % n_row) for i in range(n_row)])
                for s in range(1, n_row // 2)
            ]
            half = (owner ^ row_me) & 1
            shift = ((row_me - (owner ^ half)) % n_row) // 2
            index = (shift * 2 + half) * tiles_dev + local
        else:
            sources = [own] + [
                lax.ppermute(own, "row", [(i, (i + s) % n_row) for i in range(n_row)])
                for s in range(1, n_row)
            ]
            index = ((row_me - owner) % n_row) * tiles_dev + local
        incoming, absorbed = incoming_of(
            index,
            occupied_entries_per_strip,
            sources,
            shape_coupling_matrices,
            emitting_ability.reshape(tile_rows, tile_size),
        )
        incoming = incoming.reshape(bands_here, facets_here)

        partial_terms = emitter_terms(centre_frequency, frequency_span, facet_kelvins)
        quotient = emitting_ability / (1.0 - emitting_ability)
        early_pieces = jnp.concatenate(
            [partial_terms, emitting_ability * partial_terms, quotient * partial_terms]
        )
        if n_band & (n_band - 1) == 0:
            early = butterfly_sum(early_pieces, "band", n_band)
        else:
            early = order_free_sum(shifted(early_pieces, "band", n_band))
        planck_sum, emitted_sum, gradient_sum = early[0], early[1], early[2]
        absorbed_sum = order_free_sum(shifted(absorbed, "band", n_band)).reshape(facets_here)
        energy_portion = partial_terms / planck_sum
        kelvins_third_power = facet_kelvins**3
        ideal_emitter_power = energy_portion * kelvins_third_power * facet_kelvins
        refreshed_leaving_energy = (
            emitting_ability * ideal_emitter_power + (1.0 - emitting_ability) * incoming
        )
        emitted_less_imposed = (
            emitted_sum / planck_sum * kelvins_third_power * facet_kelvins
            - prescribed_power_density
        )
        power_gradient = gradient_sum / planck_sum * 4.0 * kelvins_third_power
        corrected_kelvins = (
            facet_kelvins - (emitted_less_imposed - absorbed_sum) / power_gradient
        )
        return (corrected_kelvins, refreshed_leaving_energy)

    return on_device


def solution(mesh):
    in_specs = (
        P("row", None, None, None),
        P("row", None),
        P("row"),
        P("band", "row"),
        P("row"),
        P("band", "row"),
        P("band"),
        P("band"),
        P("row"),
    )
    out_specs = (P("row"), P("band", "row"))
    on_device = make_on_device(mesh.shape["band"], mesh.shape["row"])
    return jax.shard_map(
        on_device, mesh=mesh, in_specs=in_specs, out_specs=out_specs, check_vma=False
    )
```

```python
import jax
import jax.numpy as jnp
from jax import lax
from jax.experimental import pallas as pl
from jax.experimental.pallas import tpu as pltpu
from jax.sharding import PartitionSpec as P


def emitter_terms(centre_sample, frequency_spacing, facet_kelvins):
    return (
        frequency_spacing[:, None]
        * centre_sample[:, None] ** 3
        / jnp.expm1(centre_sample[:, None] / facet_kelvins[None, :])
    )


def shifted(x, axis, size):
    outs = [x]
    for s in range(1, size):
        outs.append(lax.ppermute(x, axis, [(i, (i + s) % size) for i in range(size)]))
    return outs


def order_free_sum(parts):
    parts = list(parts)
    n = len(parts)
    for sweep in range(n):
        for i in range(sweep % 2, n - 1, 2):
            lo = jnp.minimum(parts[i], parts[i + 1])
            hi = jnp.maximum(parts[i], parts[i + 1])
            parts[i], parts[i + 1] = lo, hi
    total = parts[0]
    for p in parts[1:]:
        total = total + p
    return total


def incoming_kernel(n_src, rows_per_step, slot_count, n_row, paired):
    def kernel(me_ref, index_ref, used_ref, *refs):
        sources = refs[:n_src]
        coupling_ref, emitting_ref, out_ref, absorbed_ref, table_ref = refs[n_src:]
        step = pl.program_id(0)
        tiles_per_src = sources[0].shape[0]

        @pl.when(step == 0)
        def _():
            me = me_ref[0]
            halves = 2 if paired else 1
            tiles_dev = tiles_per_src // halves
            for s in range(n_src):
                sender = lax.rem(me - s * halves + n_row, n_row)
                for h in range(halves):
                    start = pl.multiple_of((sender ^ h) * tiles_dev, 8)
                    table_ref[pl.ds(start, tiles_dev), :] = sources[s][
                        pl.ds(h * tiles_dev, tiles_dev), :
                    ].astype(jnp.float32)

        for rr in range(rows_per_step):
            r = step * rows_per_step + rr
            acc = jnp.zeros(coupling_ref.shape[2:], jnp.float32)
            for k in range(slot_count):
                row = table_ref[pl.ds(index_ref[k, r], 1), :]
                row = jnp.where(k < used_ref[r], row, jnp.zeros_like(row))
                acc = acc + coupling_ref[rr, k].astype(jnp.float32) * row
            incoming = jnp.sum(acc.T, axis=0, keepdims=True)
            out_ref[pl.ds(rr, 1), :] = incoming
            absorbed_ref[pl.ds(rr, 1), :] = incoming * emitting_ref[pl.ds(rr, 1), :]

    return kernel


def incoming_of(me, index, used, sources, coupling, emitting, n_row, paired):
    tile_rows, slot_count, tile_size, _ = coupling.shape
    rows_per_step = 32 if tile_rows % 32 == 0 else tile_rows
    n_src = len(sources)
    tiles_per_src = sources[0].shape[0]
    full = lambda shape: pl.BlockSpec(shape, lambda g, m, i, o: (0,) * len(shape))
    return pl.pallas_call(
        incoming_kernel(n_src, rows_per_step, slot_count, n_row, paired),
        grid_spec=pltpu.PrefetchScalarGridSpec(
            num_scalar_prefetch=3,
            grid=(tile_rows // rows_per_step,),
            in_specs=[full(src.shape) for src in sources]
            + [
                pl.BlockSpec(
                    (rows_per_step, slot_count, tile_size, tile_size),
                    lambda g, m, i, o: (g, 0, 0, 0),
                ),
                pl.BlockSpec((rows_per_step, tile_size), lambda g, m, i, o: (g, 0)),
            ],
            out_specs=[
                pl.BlockSpec((rows_per_step, tile_size), lambda g, m, i, o: (g, 0)),
                pl.BlockSpec((rows_per_step, tile_size), lambda g, m, i, o: (g, 0)),
            ],
            scratch_shapes=[pltpu.VMEM((n_src * tiles_per_src, tile_size), jnp.float32)],
        ),
        out_shape=[jax.ShapeDtypeStruct((tile_rows, tile_size), jnp.float32)] * 2,
        compiler_params=pltpu.CompilerParams(dimension_semantics=("arbitrary",)),
    )(me, index, used, *sources, coupling, emitting)


def butterfly_sum(x, axis, size):
    step = 1
    while step < size:
        x = x + lax.ppermute(x, axis, [(i, i ^ step) for i in range(size)])
        step *= 2
    return x


def make_on_device(n_band, n_row):
    def on_device(
        shape_coupling_matrices,
        target_strip_index,
        occupied_entries_per_strip,
        prior_leaving_energy,
        facet_kelvins,
        emitting_ability,
        centre_frequency,
        frequency_span,
        prescribed_power_density,
    ):
        row_me = lax.axis_index("row")
        bands_here, facets_here = prior_leaving_energy.shape
        tile_rows, slot_count = target_strip_index.shape
        tile_size = shape_coupling_matrices.shape[2]
        tiles_dev = facets_here // tile_size

        own = prior_leaving_energy.reshape(tiles_dev, tile_size)
        paired = n_row % 2 == 0
        if paired:
            partner = lax.ppermute(prior_leaving_energy, "row", [(i, i ^ 1) for i in range(n_row)])
            pair = jnp.concatenate([own, partner.reshape(tiles_dev, tile_size)])
            sources = [pair] + [
                lax.ppermute(pair, "row", [(i, (i + 2 * s) % n_row) for i in range(n_row)])
                for s in range(1, n_row // 2)
            ]
        else:
            sources = [own] + [
                lax.ppermute(own, "row", [(i, (i + s) % n_row) for i in range(n_row)])
                for s in range(1, n_row)
            ]
        incoming, absorbed = incoming_of(
            jnp.reshape(row_me, (1,)).astype(jnp.int32),
            target_strip_index.T,
            occupied_entries_per_strip,
            sources,
            shape_coupling_matrices,
            emitting_ability.reshape(tile_rows, tile_size),
            n_row,
            paired,
        )
        incoming = incoming.reshape(bands_here, facets_here)

        partial_terms = emitter_terms(centre_frequency, frequency_span, facet_kelvins)
        quotient = emitting_ability / (1.0 - emitting_ability)
        early_pieces = jnp.concatenate(
            [partial_terms, emitting_ability * partial_terms, quotient * partial_terms]
        )
        if n_band & (n_band - 1) == 0:
            early = butterfly_sum(early_pieces, "band", n_band)
        else:
            early = order_free_sum(shifted(early_pieces, "band", n_band))
        planck_sum, emitted_sum, gradient_sum = early[0], early[1], early[2]
        absorbed_sum = order_free_sum(shifted(absorbed, "band", n_band)).reshape(facets_here)
        energy_portion = partial_terms / planck_sum
        kelvins_third_power = facet_kelvins**3
        ideal_emitter_power = energy_portion * kelvins_third_power * facet_kelvins
        refreshed_leaving_energy = (
            emitting_ability * ideal_emitter_power + (1.0 - emitting_ability) * incoming
        )
        emitted_less_imposed = (
            emitted_sum / planck_sum * kelvins_third_power * facet_kelvins
            - prescribed_power_density
        )
        power_gradient = gradient_sum / planck_sum * 4.0 * kelvins_third_power
        corrected_kelvins = (
            facet_kelvins - (emitted_less_imposed - absorbed_sum) / power_gradient
        )
        return (corrected_kelvins, refreshed_leaving_energy)

    return on_device


def solution(mesh):
    in_specs = (
        P("row", None, None, None),
        P("row", None),
        P("row"),
        P("band", "row"),
        P("row"),
        P("band", "row"),
        P("band"),
        P("band"),
        P("row"),
    )
    out_specs = (P("row"), P("band", "row"))
    on_device = make_on_device(mesh.shape["band"], mesh.shape["row"])
    return jax.shard_map(
        on_device, mesh=mesh, in_specs=in_specs, out_specs=out_specs, check_vma=False
    )
```

```python
import jax
import jax.numpy as jnp
from jax import lax
from jax.experimental import pallas as pl
from jax.experimental.pallas import tpu as pltpu
from jax.sharding import PartitionSpec as P


def emitter_terms(centre_sample, frequency_spacing, facet_kelvins):
    return (
        frequency_spacing[:, None]
        * centre_sample[:, None] ** 3
        / jnp.expm1(centre_sample[:, None] / facet_kelvins[None, :])
    )


def shifted(x, axis, size):
    outs = [x]
    for s in range(1, size):
        outs.append(lax.ppermute(x, axis, [(i, (i + s) % size) for i in range(size)]))
    return outs


def order_free_sum(parts):
    parts = list(parts)
    n = len(parts)
    for sweep in range(n):
        for i in range(sweep % 2, n - 1, 2):
            lo = jnp.minimum(parts[i], parts[i + 1])
            hi = jnp.maximum(parts[i], parts[i + 1])
            parts[i], parts[i + 1] = lo, hi
    total = parts[0]
    for p in parts[1:]:
        total = total + p
    return total


def incoming_kernel(n_src, rows_per_step, slot_count):
    def kernel(index_ref, used_ref, *refs):
        sources = refs[:n_src]
        coupling_ref, emitting_ref, out_ref, absorbed_ref, table_ref = refs[n_src:]
        step = pl.program_id(0)
        tiles_per_src = sources[0].shape[0]

        @pl.when(step == 0)
        def _():
            for s in range(n_src):
                table_ref[pl.ds(s * tiles_per_src, tiles_per_src), :] = sources[s][...].astype(
                    jnp.float32
                )

        for rr in range(rows_per_step):
            r = step * rows_per_step + rr
            acc = jnp.zeros(coupling_ref.shape[2:], jnp.float32)
            for k in range(slot_count):
                row = table_ref[pl.ds(index_ref[k, r], 1), :]
                row = jnp.where(k < used_ref[r], row, jnp.zeros_like(row))
                acc = acc + coupling_ref[rr, k].astype(jnp.float32) * row
            incoming = jnp.sum(acc.T, axis=0, keepdims=True)
            out_ref[pl.ds(rr, 1), :] = incoming
            absorbed_ref[pl.ds(rr, 1), :] = incoming * emitting_ref[pl.ds(rr, 1), :]

    return kernel


def incoming_of(index, used, sources, coupling, emitting):
    tile_rows, slot_count, tile_size, _ = coupling.shape
    rows_per_step = 32 if tile_rows % 32 == 0 else tile_rows
    n_src = len(sources)
    tiles_per_src = sources[0].shape[0]
    full = lambda shape: pl.BlockSpec(shape, lambda g, i, o: (0,) * len(shape))
    return pl.pallas_call(
        incoming_kernel(n_src, rows_per_step, slot_count),
        grid_spec=pltpu.PrefetchScalarGridSpec(
            num_scalar_prefetch=2,
            grid=(tile_rows // rows_per_step,),
            in_specs=[full(src.shape) for src in sources]
            + [
                pl.BlockSpec(
                    (rows_per_step, slot_count, tile_size, tile_size),
                    lambda g, i, o: (g, 0, 0, 0),
                ),
                pl.BlockSpec((rows_per_step, tile_size), lambda g, i, o: (g, 0)),
            ],
            out_specs=[
                pl.BlockSpec((rows_per_step, tile_size), lambda g, i, o: (g, 0)),
                pl.BlockSpec((rows_per_step, tile_size), lambda g, i, o: (g, 0)),
            ],
            scratch_shapes=[pltpu.VMEM((n_src * tiles_per_src, tile_size), jnp.float32)],
        ),
        out_shape=[jax.ShapeDtypeStruct((tile_rows, tile_size), jnp.float32)] * 2,
        compiler_params=pltpu.CompilerParams(dimension_semantics=("arbitrary",)),
    )(index, used, *sources, coupling, emitting)


def butterfly_sum(x, axis, size):
    step = 1
    while step < size:
        x = x + lax.ppermute(x, axis, [(i, i ^ step) for i in range(size)])
        step *= 2
    return x


def make_on_device(n_band, n_row):
    def on_device(
        shape_coupling_matrices,
        target_strip_index,
        occupied_entries_per_strip,
        prior_leaving_energy,
        facet_kelvins,
        emitting_ability,
        centre_frequency,
        frequency_span,
        prescribed_power_density,
    ):
        row_me = lax.axis_index("row")
        bands_here, facets_here = prior_leaving_energy.shape
        tile_rows, slot_count = target_strip_index.shape
        tile_size = shape_coupling_matrices.shape[2]
        tiles_dev = facets_here // tile_size

        own = prior_leaving_energy.reshape(tiles_dev, tile_size)
        flat_cols = target_strip_index.T
        owner = flat_cols // tiles_dev
        local = flat_cols % tiles_dev
        if n_row % 2 == 0:
            partner = lax.ppermute(prior_leaving_energy, "row", [(i, i ^ 1) for i in range(n_row)])
            pair = jnp.concatenate([own, partner.reshape(tiles_dev, tile_size)])
            sources = [pair] + [
                lax.ppermute(pair, "row", [(i, (i + 2 * s) % n_row) for i in range(n_row)])
                for s in range(1, n_row // 2)
            ]
            half = (owner ^ row_me) & 1
            shift = ((row_me - (owner ^ half)) % n_row) // 2
            index = (shift * 2 + half) * tiles_dev + local
        else:
            sources = [own] + [
                lax.ppermute(own, "row", [(i, (i + s) % n_row) for i in range(n_row)])
                for s in range(1, n_row)
            ]
            index = ((row_me - owner) % n_row) * tiles_dev + local
        incoming, absorbed = incoming_of(
            index,
            occupied_entries_per_strip,
            sources,
            shape_coupling_matrices,
            emitting_ability.reshape(tile_rows, tile_size),
        )
        incoming = incoming.reshape(bands_here, facets_here)

        partial_terms = emitter_terms(centre_frequency, frequency_span, facet_kelvins)
        quotient = emitting_ability / (1.0 - emitting_ability)
        early_pieces = jnp.concatenate(
            [partial_terms, emitting_ability * partial_terms, quotient * partial_terms]
        )
        if n_band & (n_band - 1) == 0:
            early = butterfly_sum(early_pieces, "band", n_band)
        else:
            early = order_free_sum(shifted(early_pieces, "band", n_band))
        planck_sum, emitted_sum, gradient_sum = early[0], early[1], early[2]
        absorbed_sum = order_free_sum(shifted(absorbed, "band", n_band)).reshape(facets_here)
        kelvins_third_power = facet_kelvins**3
        emitted_here = emitting_ability * partial_terms * kelvins_third_power * facet_kelvins
        refreshed_leaving_energy = (
            emitted_here / planck_sum + (1.0 - emitting_ability) * incoming
        )
        emitted_less_imposed = (
            emitted_sum / planck_sum * kelvins_third_power * facet_kelvins
            - prescribed_power_density
        )
        power_gradient = gradient_sum / planck_sum * 4.0 * kelvins_third_power
        corrected_kelvins = (
            facet_kelvins - (emitted_less_imposed - absorbed_sum) / power_gradient
        )
        return (corrected_kelvins, refreshed_leaving_energy)

    return on_device


def solution(mesh):
    in_specs = (
        P("row", None, None, None),
        P("row", None),
        P("row"),
        P("band", "row"),
        P("row"),
        P("band", "row"),
        P("band"),
        P("band"),
        P("row"),
    )
    out_specs = (P("row"), P("band", "row"))
    on_device = make_on_device(mesh.shape["band"], mesh.shape["row"])
    return jax.shard_map(
        on_device, mesh=mesh, in_specs=in_specs, out_specs=out_specs, check_vma=False
    )
```

```python
import jax
import jax.numpy as jnp
from jax import lax
from jax.experimental import pallas as pl
from jax.experimental.pallas import tpu as pltpu
from jax.sharding import PartitionSpec as P


def emitter_terms(centre_sample, frequency_spacing, facet_kelvins):
    return (
        frequency_spacing[:, None]
        * centre_sample[:, None] ** 3
        / jnp.expm1(centre_sample[:, None] / facet_kelvins[None, :])
    )


def shifted(x, axis, size):
    outs = [x]
    for s in range(1, size):
        outs.append(lax.ppermute(x, axis, [(i, (i + s) % size) for i in range(size)]))
    return outs


def order_free_sum(parts):
    parts = list(parts)
    n = len(parts)
    for sweep in range(n):
        for i in range(sweep % 2, n - 1, 2):
            lo = jnp.minimum(parts[i], parts[i + 1])
            hi = jnp.maximum(parts[i], parts[i + 1])
            parts[i], parts[i + 1] = lo, hi
    total = parts[0]
    for p in parts[1:]:
        total = total + p
    return total


def incoming_kernel(n_src, rows_per_step, slot_count):
    def kernel(index_ref, used_ref, *refs):
        sources = refs[:n_src]
        coupling_ref, emitting_ref, out_ref, absorbed_ref, table_ref = refs[n_src:]
        step = pl.program_id(0)
        tiles_per_src = sources[0].shape[0]

        @pl.when(step == 0)
        def _():
            for s in range(n_src):
                table_ref[pl.ds(s * tiles_per_src, tiles_per_src), :] = sources[s][...].astype(
                    jnp.float32
                )

        for rr in range(rows_per_step):
            r = step * rows_per_step + rr
            acc = jnp.zeros(coupling_ref.shape[2:], jnp.float32)
            for k in range(slot_count):
                row = table_ref[pl.ds(index_ref[k, r], 1), :]
                row = jnp.where(k < used_ref[r], row, jnp.zeros_like(row))
                acc = acc + coupling_ref[rr, k].astype(jnp.float32) * row
            incoming = jnp.sum(acc.T, axis=0, keepdims=True)
            out_ref[pl.ds(rr, 1), :] = incoming
            absorbed_ref[pl.ds(rr, 1), :] = incoming * emitting_ref[pl.ds(rr, 1), :]

    return kernel


def incoming_of(index, used, sources, coupling, emitting):
    tile_rows, slot_count, tile_size, _ = coupling.shape
    rows_per_step = 32 if tile_rows % 32 == 0 else tile_rows
    n_src = len(sources)
    tiles_per_src = sources[0].shape[0]
    full = lambda shape: pl.BlockSpec(shape, lambda g, i, o: (0,) * len(shape))
    return pl.pallas_call(
        incoming_kernel(n_src, rows_per_step, slot_count),
        grid_spec=pltpu.PrefetchScalarGridSpec(
            num_scalar_prefetch=2,
            grid=(tile_rows // rows_per_step,),
            in_specs=[full(src.shape) for src in sources]
            + [
                pl.BlockSpec(
                    (rows_per_step, slot_count, tile_size, tile_size),
                    lambda g, i, o: (g, 0, 0, 0),
                ),
                pl.BlockSpec((rows_per_step, tile_size), lambda g, i, o: (g, 0)),
            ],
            out_specs=[
                pl.BlockSpec((rows_per_step, tile_size), lambda g, i, o: (g, 0)),
                pl.BlockSpec((rows_per_step, tile_size), lambda g, i, o: (g, 0)),
            ],
            scratch_shapes=[pltpu.VMEM((n_src * tiles_per_src, tile_size), jnp.float32)],
        ),
        out_shape=[jax.ShapeDtypeStruct((tile_rows, tile_size), jnp.float32)] * 2,
        compiler_params=pltpu.CompilerParams(dimension_semantics=("arbitrary",)),
    )(index, used, *sources, coupling, emitting)


def butterfly_sum(x, axis, size):
    step = 1
    while step < size:
        x = x + lax.ppermute(x, axis, [(i, i ^ step) for i in range(size)])
        step *= 2
    return x


def make_on_device(n_band, n_row):
    def on_device(
        shape_coupling_matrices,
        target_strip_index,
        occupied_entries_per_strip,
        prior_leaving_energy,
        facet_kelvins,
        emitting_ability,
        centre_frequency,
        frequency_span,
        prescribed_power_density,
    ):
        row_me = lax.axis_index("row")
        bands_here, facets_here = prior_leaving_energy.shape
        tile_rows, slot_count = target_strip_index.shape
        tile_size = shape_coupling_matrices.shape[2]
        tiles_dev = facets_here // tile_size

        own = prior_leaving_energy.reshape(tiles_dev, tile_size)
        flat_cols = target_strip_index.T
        owner = flat_cols // tiles_dev
        local = flat_cols % tiles_dev
        if n_row % 2 == 0:
            partner = lax.ppermute(prior_leaving_energy, "row", [(i, i ^ 1) for i in range(n_row)])
            pair = jnp.concatenate([own, partner.reshape(tiles_dev, tile_size)])
            sources = [pair] + [
                lax.ppermute(pair, "row", [(i, (i + 2 * s) % n_row) for i in range(n_row)])
                for s in range(1, n_row // 2)
            ]
            half = (owner ^ row_me) & 1
            shift = ((row_me - (owner ^ half)) % n_row) // 2
            index = (shift * 2 + half) * tiles_dev + local
        else:
            sources = [own] + [
                lax.ppermute(own, "row", [(i, (i + s) % n_row) for i in range(n_row)])
                for s in range(1, n_row)
            ]
            index = ((row_me - owner) % n_row) * tiles_dev + local
        incoming, absorbed = incoming_of(
            index,
            occupied_entries_per_strip,
            sources,
            shape_coupling_matrices,
            emitting_ability.reshape(tile_rows, tile_size),
        )
        incoming = incoming.reshape(bands_here, facets_here)

        dense = lambda x: x.reshape(tile_rows, tile_size)
        kelvins = dense(facet_kelvins)
        emitting = dense(emitting_ability)
        partial_terms = dense(emitter_terms(centre_frequency, frequency_span, facet_kelvins))
        quotient = emitting / (1.0 - emitting)
        early_pieces = jnp.stack(
            [partial_terms, emitting * partial_terms, quotient * partial_terms]
        )
        if n_band & (n_band - 1) == 0:
            early = butterfly_sum(early_pieces, "band", n_band)
        else:
            early = order_free_sum(shifted(early_pieces, "band", n_band))
        planck_sum, emitted_sum, gradient_sum = early[0], early[1], early[2]
        absorbed_sum = order_free_sum(shifted(absorbed, "band", n_band))
        energy_portion = partial_terms / planck_sum
        kelvins_third_power = kelvins**3
        ideal_emitter_power = energy_portion * kelvins_third_power * kelvins
        refreshed_leaving_energy = (
            emitting * ideal_emitter_power + (1.0 - emitting) * dense(incoming)
        ).reshape(bands_here, facets_here)
        emitted_less_imposed = (
            emitted_sum / planck_sum * kelvins_third_power * kelvins
            - dense(prescribed_power_density)
        )
        power_gradient = gradient_sum / planck_sum * 4.0 * kelvins_third_power
        corrected_kelvins = (
            kelvins - (emitted_less_imposed - absorbed_sum) / power_gradient
        ).reshape(facets_here)
        return (corrected_kelvins, refreshed_leaving_energy)

    return on_device


def solution(mesh):
    in_specs = (
        P("row", None, None, None),
        P("row", None),
        P("row"),
        P("band", "row"),
        P("row"),
        P("band", "row"),
        P("band"),
        P("band"),
        P("row"),
    )
    out_specs = (P("row"), P("band", "row"))
    on_device = make_on_device(mesh.shape["band"], mesh.shape["row"])
    return jax.shard_map(
        on_device, mesh=mesh, in_specs=in_specs, out_specs=out_specs, check_vma=False
    )
```

```python
import jax
import jax.numpy as jnp
from jax import lax
from jax.experimental import pallas as pl
from jax.experimental.pallas import tpu as pltpu
from jax.sharding import PartitionSpec as P


def emitter_terms(centre_sample, frequency_spacing, facet_kelvins):
    return (
        frequency_spacing[:, None]
        * centre_sample[:, None] ** 3
        / jnp.expm1(centre_sample[:, None] / facet_kelvins[None, :])
    )


def shifted(x, axis, size):
    outs = [x]
    for s in range(1, size):
        outs.append(lax.ppermute(x, axis, [(i, (i + s) % size) for i in range(size)]))
    return outs


def order_free_sum(parts):
    parts = list(parts)
    n = len(parts)
    for sweep in range(n):
        for i in range(sweep % 2, n - 1, 2):
            lo = jnp.minimum(parts[i], parts[i + 1])
            hi = jnp.maximum(parts[i], parts[i + 1])
            parts[i], parts[i + 1] = lo, hi
    total = parts[0]
    for p in parts[1:]:
        total = total + p
    return total


def incoming_kernel(n_src, rows_per_step, slot_count):
    def kernel(index_ref, used_ref, *refs):
        sources = refs[:n_src]
        coupling_ref, emitting_ref, out_ref, absorbed_ref, table_ref = refs[n_src:]
        step = pl.program_id(0)
        tiles_per_src = sources[0].shape[0]

        @pl.when(step == 0)
        def _():
            for s in range(n_src):
                table_ref[pl.ds(s * tiles_per_src, tiles_per_src), :] = sources[s][...].astype(
                    jnp.float32
                )

        for rr in range(rows_per_step):
            r = step * rows_per_step + rr
            acc = jnp.zeros(coupling_ref.shape[2:], jnp.float32)
            for k in range(slot_count):
                row = table_ref[pl.ds(index_ref[k, r], 1), :]
                row = jnp.where(k < used_ref[r], row, jnp.zeros_like(row))
                acc = acc + coupling_ref[rr, k].astype(jnp.float32) * row
            incoming = jnp.sum(acc.T, axis=0, keepdims=True)
            out_ref[pl.ds(rr, 1), :] = incoming
            absorbed_ref[pl.ds(rr, 1), :] = incoming * emitting_ref[pl.ds(rr, 1), :]

    return kernel


def incoming_of(index, used, sources, coupling, emitting):
    tile_rows, slot_count, tile_size, _ = coupling.shape
    rows_per_step = 32 if tile_rows % 32 == 0 else tile_rows
    n_src = len(sources)
    tiles_per_src = sources[0].shape[0]
    full = lambda shape: pl.BlockSpec(shape, lambda g, i, o: (0,) * len(shape))
    return pl.pallas_call(
        incoming_kernel(n_src, rows_per_step, slot_count),
        grid_spec=pltpu.PrefetchScalarGridSpec(
            num_scalar_prefetch=2,
            grid=(tile_rows // rows_per_step,),
            in_specs=[full(src.shape) for src in sources]
            + [
                pl.BlockSpec(
                    (rows_per_step, slot_count, tile_size, tile_size),
                    lambda g, i, o: (g, 0, 0, 0),
                ),
                pl.BlockSpec((rows_per_step, tile_size), lambda g, i, o: (g, 0)),
            ],
            out_specs=[
                pl.BlockSpec((rows_per_step, tile_size), lambda g, i, o: (g, 0)),
                pl.BlockSpec((rows_per_step, tile_size), lambda g, i, o: (g, 0)),
            ],
            scratch_shapes=[pltpu.VMEM((n_src * tiles_per_src, tile_size), jnp.float32)],
        ),
        out_shape=[jax.ShapeDtypeStruct((tile_rows, tile_size), jnp.float32)] * 2,
        compiler_params=pltpu.CompilerParams(dimension_semantics=("arbitrary",)),
    )(index, used, *sources, coupling, emitting)


def butterfly_sum(x, axis, size):
    step = size // 2
    while step >= 1:
        x = x + lax.ppermute(x, axis, [(i, i ^ step) for i in range(size)])
        step //= 2
    return x


def make_on_device(n_band, n_row):
    def on_device(
        shape_coupling_matrices,
        target_strip_index,
        occupied_entries_per_strip,
        prior_leaving_energy,
        facet_kelvins,
        emitting_ability,
        centre_frequency,
        frequency_span,
        prescribed_power_density,
    ):
        row_me = lax.axis_index("row")
        bands_here, facets_here = prior_leaving_energy.shape
        tile_rows, slot_count = target_strip_index.shape
        tile_size = shape_coupling_matrices.shape[2]
        tiles_dev = facets_here // tile_size

        own = prior_leaving_energy.reshape(tiles_dev, tile_size)
        flat_cols = target_strip_index.T
        owner = flat_cols // tiles_dev
        local = flat_cols % tiles_dev
        if n_row % 2 == 0:
            partner = lax.ppermute(prior_leaving_energy, "row", [(i, i ^ 1) for i in range(n_row)])
            pair = jnp.concatenate([own, partner.reshape(tiles_dev, tile_size)])
            sources = [pair] + [
                lax.ppermute(pair, "row", [(i, (i + 2 * s) % n_row) for i in range(n_row)])
                for s in range(1, n_row // 2)
            ]
            half = (owner ^ row_me) & 1
            shift = ((row_me - (owner ^ half)) % n_row) // 2
            index = (shift * 2 + half) * tiles_dev + local
        else:
            sources = [own] + [
                lax.ppermute(own, "row", [(i, (i + s) % n_row) for i in range(n_row)])
                for s in range(1, n_row)
            ]
            index = ((row_me - owner) % n_row) * tiles_dev + local
        incoming, absorbed = incoming_of(
            index,
            occupied_entries_per_strip,
            sources,
            shape_coupling_matrices,
            emitting_ability.reshape(tile_rows, tile_size),
        )
        incoming = incoming.reshape(bands_here, facets_here)

        partial_terms = emitter_terms(centre_frequency, frequency_span, facet_kelvins)
        quotient = emitting_ability / (1.0 - emitting_ability)
        early_pieces = jnp.concatenate(
            [partial_terms, emitting_ability * partial_terms, quotient * partial_terms]
        )
        if n_band & (n_band - 1) == 0:
            early = butterfly_sum(early_pieces, "band", n_band)
        else:
            early = order_free_sum(shifted(early_pieces, "band", n_band))
        planck_sum, emitted_sum, gradient_sum = early[0], early[1], early[2]
        absorbed_sum = order_free_sum(shifted(absorbed, "band", n_band)).reshape(facets_here)
        energy_portion = partial_terms / planck_sum
        kelvins_third_power = facet_kelvins**3
        ideal_emitter_power = energy_portion * kelvins_third_power * facet_kelvins
        refreshed_leaving_energy = (
            emitting_ability * ideal_emitter_power + (1.0 - emitting_ability) * incoming
        )
        emitted_less_imposed = (
            emitted_sum / planck_sum * kelvins_third_power * facet_kelvins
            - prescribed_power_density
        )
        power_gradient = gradient_sum / planck_sum * 4.0 * kelvins_third_power
        corrected_kelvins = (
            facet_kelvins - (emitted_less_imposed - absorbed_sum) / power_gradient
        )
        return (corrected_kelvins, refreshed_leaving_energy)

    return on_device


def solution(mesh):
    in_specs = (
        P("row", None, None, None),
        P("row", None),
        P("row"),
        P("band", "row"),
        P("row"),
        P("band", "row"),
        P("band"),
        P("band"),
        P("row"),
    )
    out_specs = (P("row"), P("band", "row"))
    on_device = make_on_device(mesh.shape["band"], mesh.shape["row"])
    return jax.shard_map(
        on_device, mesh=mesh, in_specs=in_specs, out_specs=out_specs, check_vma=False
    )
```

```python
import jax
import jax.numpy as jnp
from jax import lax
from jax.experimental import pallas as pl
from jax.experimental.pallas import tpu as pltpu
from jax.sharding import PartitionSpec as P


def emitter_terms(centre_sample, frequency_spacing, facet_kelvins):
    return (
        frequency_spacing[:, None]
        * centre_sample[:, None] ** 3
        / jnp.expm1(centre_sample[:, None] / facet_kelvins[None, :])
    )


def shifted(x, axis, size):
    outs = [x]
    for s in range(1, size):
        outs.append(lax.ppermute(x, axis, [(i, (i + s) % size) for i in range(size)]))
    return outs


def order_free_sum(parts):
    parts = list(parts)
    n = len(parts)
    for sweep in range(n):
        for i in range(sweep % 2, n - 1, 2):
            lo = jnp.minimum(parts[i], parts[i + 1])
            hi = jnp.maximum(parts[i], parts[i + 1])
            parts[i], parts[i + 1] = lo, hi
    total = parts[0]
    for p in parts[1:]:
        total = total + p
    return total


def incoming_kernel(n_src, rows_per_step, slot_count):
    def kernel(index_ref, used_ref, *refs):
        sources = refs[:n_src]
        coupling_ref, emitting_ref, out_ref, absorbed_ref, table_ref = refs[n_src:]
        step = pl.program_id(0)
        tiles_per_src = sources[0].shape[0]

        @pl.when(step == 0)
        def _():
            for s in range(n_src):
                table_ref[pl.ds(s * tiles_per_src, tiles_per_src), :] = sources[s][...].astype(
                    jnp.float32
                )

        for rr in range(rows_per_step):
            r = step * rows_per_step + rr
            acc = jnp.zeros(coupling_ref.shape[2:], jnp.float32)
            for k in range(slot_count):
                row = table_ref[pl.ds(index_ref[k, r], 1), :]
                row = jnp.where(k < used_ref[r], row, jnp.zeros_like(row))
                acc = acc + coupling_ref[rr, k].astype(jnp.float32) * row
            incoming = jnp.sum(acc.T, axis=0, keepdims=True)
            out_ref[pl.ds(rr, 1), :] = incoming
            absorbed_ref[pl.ds(rr, 1), :] = incoming * emitting_ref[pl.ds(rr, 1), :]

    return kernel


def incoming_of(index, used, sources, coupling, emitting):
    tile_rows, slot_count, tile_size, _ = coupling.shape
    rows_per_step = 32 if tile_rows % 32 == 0 else tile_rows
    n_src = len(sources)
    tiles_per_src = sources[0].shape[0]
    full = lambda shape: pl.BlockSpec(shape, lambda g, i, o: (0,) * len(shape))
    return pl.pallas_call(
        incoming_kernel(n_src, rows_per_step, slot_count),
        grid_spec=pltpu.PrefetchScalarGridSpec(
            num_scalar_prefetch=2,
            grid=(tile_rows // rows_per_step,),
            in_specs=[full(src.shape) for src in sources]
            + [
                pl.BlockSpec(
                    (rows_per_step, slot_count, tile_size, tile_size),
                    lambda g, i, o: (g, 0, 0, 0),
                ),
                pl.BlockSpec((rows_per_step, tile_size), lambda g, i, o: (g, 0)),
            ],
            out_specs=[
                pl.BlockSpec((rows_per_step, tile_size), lambda g, i, o: (g, 0)),
                pl.BlockSpec((rows_per_step, tile_size), lambda g, i, o: (g, 0)),
            ],
            scratch_shapes=[pltpu.VMEM((n_src * tiles_per_src, tile_size), jnp.float32)],
        ),
        out_shape=[jax.ShapeDtypeStruct((tile_rows, tile_size), jnp.float32)] * 2,
        compiler_params=pltpu.CompilerParams(dimension_semantics=("arbitrary",)),
    )(index, used, *sources, coupling, emitting)


def butterfly_sum(x, axis, size, upto=None):
    step = 1
    while step < (size if upto is None else upto):
        x = x + lax.ppermute(x, axis, [(i, i ^ step) for i in range(size)])
        step *= 2
    return x


def make_on_device(n_band, n_row):
    def on_device(
        shape_coupling_matrices,
        target_strip_index,
        occupied_entries_per_strip,
        prior_leaving_energy,
        facet_kelvins,
        emitting_ability,
        centre_frequency,
        frequency_span,
        prescribed_power_density,
    ):
        row_me = lax.axis_index("row")
        bands_here, facets_here = prior_leaving_energy.shape
        tile_rows, slot_count = target_strip_index.shape
        tile_size = shape_coupling_matrices.shape[2]
        tiles_dev = facets_here // tile_size

        own = prior_leaving_energy.reshape(tiles_dev, tile_size)
        flat_cols = target_strip_index.T
        owner = flat_cols // tiles_dev
        local = flat_cols % tiles_dev
        if n_row % 2 == 0:
            partner = lax.ppermute(prior_leaving_energy, "row", [(i, i ^ 1) for i in range(n_row)])
            pair = jnp.concatenate([own, partner.reshape(tiles_dev, tile_size)])
            sources = [pair] + [
                lax.ppermute(pair, "row", [(i, (i + 2 * s) % n_row) for i in range(n_row)])
                for s in range(1, n_row // 2)
            ]
            half = (owner ^ row_me) & 1
            shift = ((row_me - (owner ^ half)) % n_row) // 2
            index = (shift * 2 + half) * tiles_dev + local
        else:
            sources = [own] + [
                lax.ppermute(own, "row", [(i, (i + s) % n_row) for i in range(n_row)])
                for s in range(1, n_row)
            ]
            index = ((row_me - owner) % n_row) * tiles_dev + local
        incoming, absorbed = incoming_of(
            index,
            occupied_entries_per_strip,
            sources,
            shape_coupling_matrices,
            emitting_ability.reshape(tile_rows, tile_size),
        )
        incoming = incoming.reshape(bands_here, facets_here)

        partial_terms = emitter_terms(centre_frequency, frequency_span, facet_kelvins)
        quotient = emitting_ability / (1.0 - emitting_ability)
        early_pieces = jnp.concatenate(
            [partial_terms, emitting_ability * partial_terms, quotient * partial_terms]
        )
        if n_band & (n_band - 1) == 0:
            early = butterfly_sum(early_pieces, "band", n_band, upto=n_band // 2)
            if n_band > 1:
                early, absorbed = lax.optimization_barrier((early, absorbed))
                last = n_band // 2
                early = early + lax.ppermute(
                    early, "band", [(i, i ^ last) for i in range(n_band)]
                )
        else:
            early = order_free_sum(shifted(early_pieces, "band", n_band))
        planck_sum, emitted_sum, gradient_sum = early[0], early[1], early[2]
        absorbed_sum = order_free_sum(shifted(absorbed, "band", n_band)).reshape(facets_here)
        energy_portion = partial_terms / planck_sum
        kelvins_third_power = facet_kelvins**3
        ideal_emitter_power = energy_portion * kelvins_third_power * facet_kelvins
        refreshed_leaving_energy = (
            emitting_ability * ideal_emitter_power + (1.0 - emitting_ability) * incoming
        )
        emitted_less_imposed = (
            emitted_sum / planck_sum * kelvins_third_power * facet_kelvins
            - prescribed_power_density
        )
        power_gradient = gradient_sum / planck_sum * 4.0 * kelvins_third_power
        corrected_kelvins = (
            facet_kelvins - (emitted_less_imposed - absorbed_sum) / power_gradient
        )
        return (corrected_kelvins, refreshed_leaving_energy)

    return on_device


def solution(mesh):
    in_specs = (
        P("row", None, None, None),
        P("row", None),
        P("row"),
        P("band", "row"),
        P("row"),
        P("band", "row"),
        P("band"),
        P("band"),
        P("row"),
    )
    out_specs = (P("row"), P("band", "row"))
    on_device = make_on_device(mesh.shape["band"], mesh.shape["row"])
    return jax.shard_map(
        on_device, mesh=mesh, in_specs=in_specs, out_specs=out_specs, check_vma=False
    )
```

```python
import jax
import jax.numpy as jnp
from jax import lax
from jax.experimental import pallas as pl
from jax.experimental.pallas import tpu as pltpu
from jax.sharding import PartitionSpec as P


def emitter_terms(centre_sample, frequency_spacing, facet_kelvins):
    return (
        frequency_spacing[:, None]
        * centre_sample[:, None] ** 3
        / jnp.expm1(centre_sample[:, None] / facet_kelvins[None, :])
    )


def shifted(x, axis, size):
    outs = [x]
    for s in range(1, size):
        outs.append(lax.ppermute(x, axis, [(i, (i + s) % size) for i in range(size)]))
    return outs


def order_free_sum(parts):
    parts = list(parts)
    n = len(parts)
    for sweep in range(n):
        for i in range(sweep % 2, n - 1, 2):
            lo = jnp.minimum(parts[i], parts[i + 1])
            hi = jnp.maximum(parts[i], parts[i + 1])
            parts[i], parts[i + 1] = lo, hi
    total = parts[0]
    for p in parts[1:]:
        total = total + p
    return total


def incoming_kernel(n_src, rows_per_step, slot_count):
    def kernel(index_ref, used_ref, *refs):
        sources = refs[:n_src]
        coupling_ref, emitting_ref, out_ref, absorbed_ref, table_ref = refs[n_src:]
        step = pl.program_id(0)
        tiles_per_src = sources[0].shape[0]

        @pl.when(step == 0)
        def _():
            for s in range(n_src):
                table_ref[pl.ds(s * tiles_per_src, tiles_per_src), :] = sources[s][...].astype(
                    jnp.float32
                )

        for rr in range(rows_per_step):
            r = step * rows_per_step + rr
            acc = jnp.zeros(coupling_ref.shape[2:], jnp.float32)
            for k in range(slot_count):
                row = table_ref[pl.ds(index_ref[k, r], 1), :]
                row = jnp.where(k < used_ref[r], row, jnp.zeros_like(row))
                acc = acc + coupling_ref[rr, k].astype(jnp.float32) * row
            incoming = jnp.sum(acc.T, axis=0, keepdims=True)
            out_ref[pl.ds(rr, 1), :] = incoming
            absorbed_ref[pl.ds(rr, 1), :] = incoming * emitting_ref[pl.ds(rr, 1), :]

    return kernel


def incoming_of(index, used, sources, coupling, emitting):
    tile_rows, slot_count, tile_size, _ = coupling.shape
    rows_per_step = 32 if tile_rows % 32 == 0 else tile_rows
    n_src = len(sources)
    tiles_per_src = sources[0].shape[0]
    full = lambda shape: pl.BlockSpec(shape, lambda g, i, o: (0,) * len(shape))
    return pl.pallas_call(
        incoming_kernel(n_src, rows_per_step, slot_count),
        grid_spec=pltpu.PrefetchScalarGridSpec(
            num_scalar_prefetch=2,
            grid=(tile_rows // rows_per_step,),
            in_specs=[full(src.shape) for src in sources]
            + [
                pl.BlockSpec(
                    (rows_per_step, slot_count, tile_size, tile_size),
                    lambda g, i, o: (g, 0, 0, 0),
                ),
                pl.BlockSpec((rows_per_step, tile_size), lambda g, i, o: (g, 0)),
            ],
            out_specs=[
                pl.BlockSpec((rows_per_step, tile_size), lambda g, i, o: (g, 0)),
                pl.BlockSpec((rows_per_step, tile_size), lambda g, i, o: (g, 0)),
            ],
            scratch_shapes=[pltpu.VMEM((n_src * tiles_per_src, tile_size), jnp.float32)],
        ),
        out_shape=[jax.ShapeDtypeStruct((tile_rows, tile_size), jnp.float32)] * 2,
        compiler_params=pltpu.CompilerParams(dimension_semantics=("arbitrary",)),
    )(index, used, *sources, coupling, emitting)


def butterfly_sum(x, axis, size):
    step = 1
    while step < size:
        x = x + lax.ppermute(x, axis, [(i, i ^ step) for i in range(size)])
        step *= 2
    return x


def make_on_device(n_band, n_row):
    def on_device(
        shape_coupling_matrices,
        target_strip_index,
        occupied_entries_per_strip,
        prior_leaving_energy,
        facet_kelvins,
        emitting_ability,
        centre_frequency,
        frequency_span,
        prescribed_power_density,
    ):
        row_me = lax.axis_index("row")
        bands_here, facets_here = prior_leaving_energy.shape
        tile_rows, slot_count = target_strip_index.shape
        tile_size = shape_coupling_matrices.shape[2]
        tiles_dev = facets_here // tile_size

        own = prior_leaving_energy.reshape(tiles_dev, tile_size)
        flat_cols = target_strip_index.T
        owner = flat_cols // tiles_dev
        local = flat_cols % tiles_dev
        if n_row % 2 == 0:
            partner = lax.ppermute(prior_leaving_energy, "row", [(i, i ^ 1) for i in range(n_row)])
            pair = jnp.concatenate([own, partner.reshape(tiles_dev, tile_size)])
            n_pairs = n_row // 2
            order = sorted(range(1, n_pairs), key=lambda s: (min(s, n_pairs - s), s))
            sources = [pair] + [
                lax.ppermute(pair, "row", [(i, (i + 2 * s) % n_row) for i in range(n_row)])
                for s in order
            ]
            place = [0] * n_pairs
            for p, s in enumerate(order):
                place[s] = p + 1
            half = (owner ^ row_me) & 1
            shift = ((row_me - (owner ^ half)) % n_row) // 2
            slot = jnp.take(jnp.array(place, jnp.int32), shift)
            index = (slot * 2 + half) * tiles_dev + local
        else:
            sources = [own] + [
                lax.ppermute(own, "row", [(i, (i + s) % n_row) for i in range(n_row)])
                for s in range(1, n_row)
            ]
            index = ((row_me - owner) % n_row) * tiles_dev + local
        incoming, absorbed = incoming_of(
            index,
            occupied_entries_per_strip,
            sources,
            shape_coupling_matrices,
            emitting_ability.reshape(tile_rows, tile_size),
        )
        incoming = incoming.reshape(bands_here, facets_here)

        partial_terms = emitter_terms(centre_frequency, frequency_span, facet_kelvins)
        quotient = emitting_ability / (1.0 - emitting_ability)
        early_pieces = jnp.concatenate(
            [partial_terms, emitting_ability * partial_terms, quotient * partial_terms]
        )
        if n_band & (n_band - 1) == 0:
            early = butterfly_sum(early_pieces, "band", n_band)
        else:
            early = order_free_sum(shifted(early_pieces, "band", n_band))
        planck_sum, emitted_sum, gradient_sum = early[0], early[1], early[2]
        absorbed_sum = order_free_sum(shifted(absorbed, "band", n_band)).reshape(facets_here)
        energy_portion = partial_terms / planck_sum
        kelvins_third_power = facet_kelvins**3
        ideal_emitter_power = energy_portion * kelvins_third_power * facet_kelvins
        refreshed_leaving_energy = (
            emitting_ability * ideal_emitter_power + (1.0 - emitting_ability) * incoming
        )
        emitted_less_imposed = (
            emitted_sum / planck_sum * kelvins_third_power * facet_kelvins
            - prescribed_power_density
        )
        power_gradient = gradient_sum / planck_sum * 4.0 * kelvins_third_power
        corrected_kelvins = (
            facet_kelvins - (emitted_less_imposed - absorbed_sum) / power_gradient
        )
        return (corrected_kelvins, refreshed_leaving_energy)

    return on_device


def solution(mesh):
    in_specs = (
        P("row", None, None, None),
        P("row", None),
        P("row"),
        P("band", "row"),
        P("row"),
        P("band", "row"),
        P("band"),
        P("band"),
        P("row"),
    )
    out_specs = (P("row"), P("band", "row"))
    on_device = make_on_device(mesh.shape["band"], mesh.shape["row"])
    return jax.shard_map(
        on_device, mesh=mesh, in_specs=in_specs, out_specs=out_specs, check_vma=False
    )
```

```python
import jax
import jax.numpy as jnp
from jax import lax
from jax.experimental import pallas as pl
from jax.experimental.pallas import tpu as pltpu
from jax.sharding import PartitionSpec as P


def emitter_terms(centre_sample, frequency_spacing, facet_kelvins):
    return (
        frequency_spacing[:, None]
        * centre_sample[:, None] ** 3
        / jnp.expm1(centre_sample[:, None] / facet_kelvins[None, :])
    )


def shifted(x, axis, size):
    outs = [x]
    for s in range(1, size):
        outs.append(lax.ppermute(x, axis, [(i, (i + s) % size) for i in range(size)]))
    return outs


def order_free_sum(parts):
    parts = list(parts)
    n = len(parts)
    for sweep in range(n):
        for i in range(sweep % 2, n - 1, 2):
            lo = jnp.minimum(parts[i], parts[i + 1])
            hi = jnp.maximum(parts[i], parts[i + 1])
            parts[i], parts[i + 1] = lo, hi
    total = parts[0]
    for p in parts[1:]:
        total = total + p
    return total


def incoming_kernel(n_src, rows_per_step, slot_count):
    def kernel(index_ref, used_ref, *refs):
        sources = refs[:n_src]
        coupling_ref, emitting_ref, out_ref, absorbed_ref, table_ref = refs[n_src:]
        step = pl.program_id(0)
        tiles_per_src = sources[0].shape[0]

        @pl.when(step == 0)
        def _():
            for s in range(n_src):
                table_ref[pl.ds(s * tiles_per_src, tiles_per_src), :] = sources[s][...].astype(
                    jnp.float32
                )

        for rr in range(rows_per_step):
            r = step * rows_per_step + rr
            acc = jnp.zeros(coupling_ref.shape[2:], jnp.float32)
            for k in range(slot_count):
                row = table_ref[pl.ds(index_ref[k, r], 1), :]
                row = jnp.where(k < used_ref[r], row, jnp.zeros_like(row))
                acc = acc + coupling_ref[rr, k].astype(jnp.float32) * row
            incoming = jnp.sum(acc.T, axis=0, keepdims=True)
            out_ref[pl.ds(rr, 1), :] = incoming
            absorbed_ref[pl.ds(rr, 1), :] = incoming * emitting_ref[pl.ds(rr, 1), :]

    return kernel


def incoming_of(index, used, sources, coupling, emitting):
    tile_rows, slot_count, tile_size, _ = coupling.shape
    rows_per_step = 32 if tile_rows % 32 == 0 else tile_rows
    n_src = len(sources)
    tiles_per_src = sources[0].shape[0]
    full = lambda shape: pl.BlockSpec(shape, lambda g, i, o: (0,) * len(shape))
    return pl.pallas_call(
        incoming_kernel(n_src, rows_per_step, slot_count),
        grid_spec=pltpu.PrefetchScalarGridSpec(
            num_scalar_prefetch=2,
            grid=(tile_rows // rows_per_step,),
            in_specs=[full(src.shape) for src in sources]
            + [
                pl.BlockSpec(
                    (rows_per_step, slot_count, tile_size, tile_size),
                    lambda g, i, o: (g, 0, 0, 0),
                ),
                pl.BlockSpec((rows_per_step, tile_size), lambda g, i, o: (g, 0)),
            ],
            out_specs=[
                pl.BlockSpec((rows_per_step, tile_size), lambda g, i, o: (g, 0)),
                pl.BlockSpec((rows_per_step, tile_size), lambda g, i, o: (g, 0)),
            ],
            scratch_shapes=[pltpu.VMEM((n_src * tiles_per_src, tile_size), jnp.float32)],
        ),
        out_shape=[jax.ShapeDtypeStruct((tile_rows, tile_size), jnp.float32)] * 2,
        compiler_params=pltpu.CompilerParams(dimension_semantics=("arbitrary",)),
    )(index, used, *sources, coupling, emitting)


def butterfly_sum(x, axis, size):
    step = 1
    while step < size:
        x = x + lax.ppermute(x, axis, [(i, i ^ step) for i in range(size)])
        step *= 2
    return x


def make_on_device(n_band, n_row):
    def on_device(
        shape_coupling_matrices,
        target_strip_index,
        occupied_entries_per_strip,
        prior_leaving_energy,
        facet_kelvins,
        emitting_ability,
        centre_frequency,
        frequency_span,
        prescribed_power_density,
    ):
        row_me = lax.axis_index("row")
        bands_here, facets_here = prior_leaving_energy.shape
        tile_rows, slot_count = target_strip_index.shape
        tile_size = shape_coupling_matrices.shape[2]
        tiles_dev = facets_here // tile_size

        own = prior_leaving_energy.reshape(tiles_dev, tile_size)
        flat_cols = target_strip_index.T
        owner = flat_cols // tiles_dev
        local = flat_cols % tiles_dev
        if n_row % 2 == 0:
            partner = lax.ppermute(prior_leaving_energy, "row", [(i, i ^ 1) for i in range(n_row)])
            pair = jnp.concatenate([own, partner.reshape(tiles_dev, tile_size)])
            sources = [pair] + [
                lax.ppermute(pair, "row", [(i, (i + 2 * s) % n_row) for i in range(n_row)])
                for s in range(1, n_row // 2)
            ]
            half = (owner ^ row_me) & 1
            shift = ((row_me - (owner ^ half)) % n_row) // 2
            index = (shift * 2 + half) * tiles_dev + local
        else:
            sources = [own] + [
                lax.ppermute(own, "row", [(i, (i + s) % n_row) for i in range(n_row)])
                for s in range(1, n_row)
            ]
            index = ((row_me - owner) % n_row) * tiles_dev + local
        incoming, absorbed = incoming_of(
            index,
            occupied_entries_per_strip,
            sources,
            shape_coupling_matrices,
            emitting_ability.reshape(tile_rows, tile_size),
        )
        incoming = incoming.reshape(bands_here, facets_here)

        partial_terms = emitter_terms(centre_frequency, frequency_span, facet_kelvins)
        quotient = emitting_ability / (1.0 - emitting_ability)
        early_pieces = jnp.concatenate(
            [partial_terms, emitting_ability * partial_terms, quotient * partial_terms]
        )
        if n_band & (n_band - 1) == 0:
            early = butterfly_sum(early_pieces, "band", n_band)
        else:
            early = order_free_sum(shifted(early_pieces, "band", n_band))
        planck_sum, emitted_sum, gradient_sum = early[0], early[1], early[2]
        if n_band & (n_band - 1) == 0:
            parts = [absorbed] + [
                lax.ppermute(absorbed, "band", [(i, i ^ m) for i in range(n_band)])
                for m in range(1, n_band)
            ]
        else:
            parts = shifted(absorbed, "band", n_band)
        absorbed_sum = order_free_sum(parts).reshape(facets_here)
        energy_portion = partial_terms / planck_sum
        kelvins_third_power = facet_kelvins**3
        ideal_emitter_power = energy_portion * kelvins_third_power * facet_kelvins
        refreshed_leaving_energy = (
            emitting_ability * ideal_emitter_power + (1.0 - emitting_ability) * incoming
        )
        emitted_less_imposed = (
            emitted_sum / planck_sum * kelvins_third_power * facet_kelvins
            - prescribed_power_density
        )
        power_gradient = gradient_sum / planck_sum * 4.0 * kelvins_third_power
        corrected_kelvins = (
            facet_kelvins - (emitted_less_imposed - absorbed_sum) / power_gradient
        )
        return (corrected_kelvins, refreshed_leaving_energy)

    return on_device


def solution(mesh):
    in_specs = (
        P("row", None, None, None),
        P("row", None),
        P("row"),
        P("band", "row"),
        P("row"),
        P("band", "row"),
        P("band"),
        P("band"),
        P("row"),
    )
    out_specs = (P("row"), P("band", "row"))
    on_device = make_on_device(mesh.shape["band"], mesh.shape["row"])
    return jax.shard_map(
        on_device, mesh=mesh, in_specs=in_specs, out_specs=out_specs, check_vma=False
    )
```

```python
import jax
import jax.numpy as jnp
from jax import lax
from jax.experimental import pallas as pl
from jax.experimental.pallas import tpu as pltpu
from jax.sharding import PartitionSpec as P


def emitter_terms(centre_sample, frequency_spacing, facet_kelvins):
    return (
        frequency_spacing[:, None]
        * centre_sample[:, None] ** 3
        / jnp.expm1(centre_sample[:, None] / facet_kelvins[None, :])
    )


def shifted(x, axis, size):
    outs = [x]
    for s in range(1, size):
        outs.append(lax.ppermute(x, axis, [(i, (i + s) % size) for i in range(size)]))
    return outs


def order_free_sum(parts):
    parts = list(parts)
    n = len(parts)
    for sweep in range(n):
        for i in range(sweep % 2, n - 1, 2):
            lo = jnp.minimum(parts[i], parts[i + 1])
            hi = jnp.maximum(parts[i], parts[i + 1])
            parts[i], parts[i + 1] = lo, hi
    total = parts[0]
    for p in parts[1:]:
        total = total + p
    return total


def incoming_kernel(n_src, rows_per_step, slot_count):
    def kernel(index_ref, used_ref, *refs):
        sources = refs[:n_src]
        coupling_ref, emitting_ref, out_ref, absorbed_ref, table_ref = refs[n_src:]
        step = pl.program_id(0)
        tiles_per_src = sources[0].shape[0]

        @pl.when(step == 0)
        def _():
            for s in range(n_src):
                table_ref[pl.ds(s * tiles_per_src, tiles_per_src), :] = sources[s][...].astype(
                    jnp.float32
                )

        for rr in range(rows_per_step):
            r = step * rows_per_step + rr
            acc = jnp.zeros(coupling_ref.shape[2:], jnp.float32)
            for k in range(slot_count):
                row = table_ref[pl.ds(index_ref[k, r], 1), :]
                row = jnp.where(k < used_ref[r], row, jnp.zeros_like(row))
                acc = acc + coupling_ref[rr, k].astype(jnp.float32) * row
            incoming = jnp.sum(acc.T, axis=0, keepdims=True)
            out_ref[pl.ds(rr, 1), :] = incoming
            absorbed_ref[pl.ds(rr, 1), :] = incoming * emitting_ref[pl.ds(rr, 1), :]

    return kernel


def incoming_of(index, used, sources, coupling, emitting):
    tile_rows, slot_count, tile_size, _ = coupling.shape
    rows_per_step = 32 if tile_rows % 32 == 0 else tile_rows
    n_src = len(sources)
    tiles_per_src = sources[0].shape[0]
    full = lambda shape: pl.BlockSpec(shape, lambda g, i, o: (0,) * len(shape))
    return pl.pallas_call(
        incoming_kernel(n_src, rows_per_step, slot_count),
        grid_spec=pltpu.PrefetchScalarGridSpec(
            num_scalar_prefetch=2,
            grid=(tile_rows // rows_per_step,),
            in_specs=[full(src.shape) for src in sources]
            + [
                pl.BlockSpec(
                    (rows_per_step, slot_count, tile_size, tile_size),
                    lambda g, i, o: (g, 0, 0, 0),
                ),
                pl.BlockSpec((rows_per_step, tile_size), lambda g, i, o: (g, 0)),
            ],
            out_specs=[
                pl.BlockSpec((rows_per_step, tile_size), lambda g, i, o: (g, 0)),
                pl.BlockSpec((rows_per_step, tile_size), lambda g, i, o: (g, 0)),
            ],
            scratch_shapes=[pltpu.VMEM((n_src * tiles_per_src, tile_size), jnp.float32)],
        ),
        out_shape=[jax.ShapeDtypeStruct((tile_rows, tile_size), jnp.float32)] * 2,
        compiler_params=pltpu.CompilerParams(dimension_semantics=("arbitrary",)),
    )(index, used, *sources, coupling, emitting)


def butterfly_sum(x, axis, size):
    step = 1
    while step < size:
        x = x + lax.ppermute(x, axis, [(i, i ^ step) for i in range(size)])
        step *= 2
    return x


def make_on_device(n_band, n_row):
    def on_device(
        shape_coupling_matrices,
        target_strip_index,
        occupied_entries_per_strip,
        prior_leaving_energy,
        facet_kelvins,
        emitting_ability,
        centre_frequency,
        frequency_span,
        prescribed_power_density,
    ):
        row_me = lax.axis_index("row")
        bands_here, facets_here = prior_leaving_energy.shape
        tile_rows, slot_count = target_strip_index.shape
        tile_size = shape_coupling_matrices.shape[2]
        tiles_dev = facets_here // tile_size

        own = prior_leaving_energy.reshape(tiles_dev, tile_size)
        flat_cols = target_strip_index.T
        owner = flat_cols // tiles_dev
        local = flat_cols % tiles_dev
        if n_row % 2 == 0:
            partner = lax.ppermute(prior_leaving_energy, "row", [(i, i ^ 1) for i in range(n_row)])
            pair = jnp.concatenate([own, partner.reshape(tiles_dev, tile_size)])
            if n_row & (n_row - 1) == 0:
                sources = [pair] + [
                    lax.ppermute(pair, "row", [(i, i ^ (2 * m)) for i in range(n_row)])
                    for m in range(1, n_row // 2)
                ]
                index = (owner ^ row_me) * tiles_dev + local
            else:
                sources = [pair] + [
                    lax.ppermute(pair, "row", [(i, (i + 2 * s) % n_row) for i in range(n_row)])
                    for s in range(1, n_row // 2)
                ]
                half = (owner ^ row_me) & 1
                shift = ((row_me - (owner ^ half)) % n_row) // 2
                index = (shift * 2 + half) * tiles_dev + local
        else:
            sources = [own] + [
                lax.ppermute(own, "row", [(i, (i + s) % n_row) for i in range(n_row)])
                for s in range(1, n_row)
            ]
            index = ((row_me - owner) % n_row) * tiles_dev + local
        incoming, absorbed = incoming_of(
            index,
            occupied_entries_per_strip,
            sources,
            shape_coupling_matrices,
            emitting_ability.reshape(tile_rows, tile_size),
        )
        incoming = incoming.reshape(bands_here, facets_here)

        partial_terms = emitter_terms(centre_frequency, frequency_span, facet_kelvins)
        quotient = emitting_ability / (1.0 - emitting_ability)
        early_pieces = jnp.concatenate(
            [partial_terms, emitting_ability * partial_terms, quotient * partial_terms]
        )
        if n_band & (n_band - 1) == 0:
            early = butterfly_sum(early_pieces, "band", n_band)
        else:
            early = order_free_sum(shifted(early_pieces, "band", n_band))
        planck_sum, emitted_sum, gradient_sum = early[0], early[1], early[2]
        absorbed_sum = order_free_sum(shifted(absorbed, "band", n_band)).reshape(facets_here)
        energy_portion = partial_terms / planck_sum
        kelvins_third_power = facet_kelvins**3
        ideal_emitter_power = energy_portion * kelvins_third_power * facet_kelvins
        refreshed_leaving_energy = (
            emitting_ability * ideal_emitter_power + (1.0 - emitting_ability) * incoming
        )
        emitted_less_imposed = (
            emitted_sum / planck_sum * kelvins_third_power * facet_kelvins
            - prescribed_power_density
        )
        power_gradient = gradient_sum / planck_sum * 4.0 * kelvins_third_power
        corrected_kelvins = (
            facet_kelvins - (emitted_less_imposed - absorbed_sum) / power_gradient
        )
        return (corrected_kelvins, refreshed_leaving_energy)

    return on_device


def solution(mesh):
    in_specs = (
        P("row", None, None, None),
        P("row", None),
        P("row"),
        P("band", "row"),
        P("row"),
        P("band", "row"),
        P("band"),
        P("band"),
        P("row"),
    )
    out_specs = (P("row"), P("band", "row"))
    on_device = make_on_device(mesh.shape["band"], mesh.shape["row"])
    return jax.shard_map(
        on_device, mesh=mesh, in_specs=in_specs, out_specs=out_specs, check_vma=False
    )
```
